32 devices in a mesh: pipe: 4 (over y, x), expert: 8 (over z, core).
Axes of the slice: x: 2, y: 2, z: 4, core: 2. Of those that a mesh axis runs over, the one named last changes fastest.
Arguments:
- x_fwd: bfloat16 [4, 512, 3584], P('pipe', 'expert'), may hold values from -6 to 6
- routes_fwd: int32 [4, 512, 1], P('pipe', 'expert'), may hold values from 0 to 1; in each aligned block of 64 rows (0 to 63, 64 to 127, ..., all dimensions but the last counted through in order) at most 48 rows name the same one
- gates_fwd: float32 [4, 512, 1], P('pipe', 'expert'), may hold values from 0.25 to 1.5
- x_bwd: bfloat16 [4, 512, 3584], P('pipe', 'expert'), may hold values from -6 to 6
- grad_bwd: bfloat16 [4, 512, 3584], P('pipe', 'expert'), may hold values from -6 to 6
- routes_bwd: int32 [4, 512, 1], P('pipe', 'expert'), may hold values from 0 to 1; in each aligned block of 64 rows (0 to 63, 64 to 127, ..., all dimensions but the last counted through in order) at most 48 rows name the same one
- gates_bwd: float32 [4, 512, 1], P('pipe', 'expert'), may hold values from 0.25 to 1.5
- gate_proj: bfloat16 [4, 3584, 2048], P('pipe', None, 'expert'), may hold values from -0.09375 to 0.09375
- up_proj: bfloat16 [4, 3584, 2048], P('pipe', None, 'expert'), may hold values from -0.09375 to 0.09375
- down_proj: bfloat16 [4, 2048, 3584], P('pipe', 'expert'), may hold values from -0.1875 to 0.1875
Outputs:
- fwd_next: bfloat16 [4, 512, 3584], P('pipe', 'expert')
- bwd_next: bfloat16 [4, 512, 3584], P('pipe', 'expert')
The draws below stay inside these ranges and needn't reach their ends.
Inputs may be any that keep to these rules, and one draw needn't show every extreme that they name: `routes_fwd`: each token names 1 different experts. Among the 64 tokens of one device no expert is named more than 48 times, and in every draw some expert is named exactly 48 times by the tokens of one device. `routes_bwd`: as for routes_fwd.
All inputs are finite; a program needn't handle non-finite values.
Results may differ from the reference program's by a relative error of at most 0.007.
Values may be sent and summed in bfloat16 or wider, within the bound.
A program may use at most 128 MiB of HBM per device.

```python
import math
import jax
import jax.numpy as jnp
import numpy as np
from jax import lax

D = 3584
FF = 1024
HSPLIT = 4
TOPK = 1
TOK_DEV = 64
EXPERTS = 2
CAP = 48
TOKENS = 512
N_PIPE = 4
N_EXPERT = 8


def steps_of(key, shape, cuts, smallest, largest):
    loudness, own = 1.0, jax.random.fold_in(key, 6)
    for axis_at, shards_of in cuts:
        draws = jnp.exp(jax.random.uniform(jax.random.fold_in(own, axis_at), (shards_of,), jnp.float32, smallest / len(cuts), largest / len(cuts)))
        loudness = loudness * jnp.repeat(draws, shape[axis_at] // shards_of).reshape([-1 if axis == axis_at else 1 for axis in range(len(shape))])
    return loudness


def routed_block(stream_key, own, number, rows, number_of, top, most, lean):
    ranking = jax.random.permutation(stream_key, number_of)
    packed, usual = portions_of(number_of, rows * top, most, lean, True), portions_of(number_of, rows * top, most, lean, False)
    places = jnp.arange(number_of)

    def named(lengths, turn):
        used = int((lengths > 0).sum())
        fixed = max(1, used // 4)
        passed = fixed + (places - fixed + turn * (used - fixed)) % max(1, number_of - fixed)
        return jnp.zeros((number_of,), jnp.int32).at[ranking[jnp.where(places < fixed, places, passed)]].set(jnp.asarray(lengths, jnp.int32))

    lengths = jnp.where(number % 4 == 0, named(packed, number // 4), named(usual, number - number // 4 - 1))
    mixed = jax.random.permutation(jax.random.fold_in(own, 3), number_of)
    source_of, taker = mixed[0:number_of // 2 * 2:2], mixed[1:number_of // 2 * 2:2]
    margin = jnp.minimum(lengths[source_of] - 1, most - lengths[taker]) // 2
    margin = jnp.where((source_of == ranking[0]) | (taker == ranking[0]) | (lengths[taker] == 0), 0, jnp.maximum(margin, 0))
    passed = jax.random.randint(jax.random.fold_in(own, 4), (number_of // 2,), 0, 1 << 20) % (margin + 1)
    lengths = lengths.at[source_of].add(-passed).at[taker].add(passed)
    items = jnp.searchsorted(jnp.cumsum(lengths), jnp.arange(rows * top), side="right").astype(jnp.int32)
    listing = items.reshape(top, rows).T
    listing = listing[jax.random.permutation(jax.random.fold_in(own, 1), rows)]
    turn = jax.random.randint(jax.random.fold_in(own, 2), (rows, 1), 0, top)
    return jnp.take_along_axis(listing, (jnp.arange(top)[None, :] + turn) % top, axis=1)


def portions_of(number_of, total, bound, slope, full):
    portions = [(1 << 20) // math.isqrt(grade ** slope) + 1 for grade in range(1, number_of + 1)]
    largest = bound if full else min(bound, max(-(-total // number_of), total * portions[0] // sum(portions)))
    least = 1 if total - largest >= number_of - 1 else 0
    given, spare = [largest] + [least] * (number_of - 1), total - largest - least * (number_of - 1)
    while spare > 0:
        candidates = [i for i in range(1, number_of) if given[i] < largest] or [i for i in range(1, number_of) if given[i] < bound]
        pool, left = sum([portions[i] for i in candidates]), spare
        for i in candidates:
            extra = min(bound - given[i], max(1, left * portions[i] // pool), spare)
            given[i] = given[i] + extra
            spare = spare - extra
    return np.array(given)


def normal_values(stream_key, shape, scale, reach, shards=(), kind=jnp.bfloat16):
    gain = steps_of(stream_key, shape, shards, -0.22, 0.18) if shards else 1.0
    values = jax.random.normal(stream_key, shape, jnp.float32) * scale * gain
    return jnp.minimum(jnp.maximum(values, -reach), reach).astype(kind)


def setup_inputs(seed: int = 0) -> dict:
    key_of = jax.random.split(jax.random.key(seed), 11)
    x_fwd = normal_values(key_of[0], (N_PIPE, TOKENS, D), 1.0, 6.0, ((0, 4), (1, 8)))
    routes_fwd_keys = jax.random.split(jax.random.fold_in(key_of[1], 1), N_PIPE * TOKENS // TOK_DEV)
    routes_fwd_turns = jax.random.permutation(jax.random.fold_in(key_of[1], 3), N_PIPE * TOKENS // TOK_DEV)
    routes_fwd = jax.vmap(lambda own, number: routed_block(jax.random.fold_in(key_of[1], 2), own, number, TOK_DEV, EXPERTS, TOPK, CAP, 1))(routes_fwd_keys, routes_fwd_turns).reshape((N_PIPE, TOKENS, TOPK))
    gates_fwd = jnp.clip(0.25 + 1.25 * jax.random.uniform(key_of[2], (N_PIPE, TOKENS, TOPK), jnp.float32) ** steps_of(key_of[2], (N_PIPE, TOKENS, TOPK), ((0, 4), (1, 8)), -0.2, 0.2), 0.25, 1.5)
    x_bwd = normal_values(key_of[3], (N_PIPE, TOKENS, D), 1.0, 6.0, ((0, 4), (1, 8)))
    grad_bwd = normal_values(key_of[4], (N_PIPE, TOKENS, D), 1.0, 6.0, ((0, 4), (1, 8)))
    routes_bwd_keys = jax.random.split(jax.random.fold_in(key_of[5], 1), N_PIPE * TOKENS // TOK_DEV)
    routes_bwd_turns = jax.random.permutation(jax.random.fold_in(key_of[5], 3), N_PIPE * TOKENS // TOK_DEV)
    routes_bwd = jax.vmap(lambda own, number: routed_block(jax.random.fold_in(key_of[5], 2), own, number, TOK_DEV, EXPERTS, TOPK, CAP, 1))(routes_bwd_keys, routes_bwd_turns).reshape((N_PIPE, TOKENS, TOPK))
    gates_bwd = jnp.clip(0.25 + 1.25 * jax.random.uniform(key_of[6], (N_PIPE, TOKENS, TOPK), jnp.float32) ** steps_of(key_of[6], (N_PIPE, TOKENS, TOPK), ((0, 4), (1, 8)), -0.2, 0.2), 0.25, 1.5)
    gate_proj = normal_values(key_of[7], (N_PIPE, D, EXPERTS * FF), D ** -0.5, 0.09375, ((0, 4), (2, 8)))
    up_proj = normal_values(key_of[8], (N_PIPE, D, EXPERTS * FF), D ** -0.5, 0.09375, ((0, 4), (2, 8)))
    down_proj = normal_values(key_of[9], (N_PIPE, EXPERTS * FF, D), FF ** -0.5, 0.1875, ((0, 4), (1, 8)))
    return {"x_fwd": x_fwd, "routes_fwd": routes_fwd, "gates_fwd": gates_fwd, "x_bwd": x_bwd, "grad_bwd": grad_bwd, "routes_bwd": routes_bwd, "gates_bwd": gates_bwd, "gate_proj": gate_proj, "up_proj": up_proj, "down_proj": down_proj}


def slot_table(routes):
    flat_ids = routes.reshape(-1).astype(jnp.int32)
    hit_table = (flat_ids[:, None] == jnp.arange(EXPERTS, dtype=jnp.int32)[None, :]).astype(jnp.int32)
    earlier = (jnp.cumsum(hit_table, axis=0) - hit_table).astype(jnp.int32)
    places = jnp.sum(earlier * hit_table, axis=1).astype(jnp.int32)
    return places.reshape(routes.shape)


def source_ids(routes):
    return jnp.broadcast_to(jnp.arange(N_EXPERT, dtype=jnp.int32)[:, None, None], routes.shape)


def to_experts(values, routes, places):
    row_block = values.reshape(N_EXPERT, TOK_DEV, 1, D)
    spread = jnp.broadcast_to(row_block, (N_EXPERT, TOK_DEV, TOPK, D))
    buffer = jnp.zeros((EXPERTS, N_EXPERT, CAP, D), values.dtype)
    buffer = buffer.at[routes, source_ids(routes), places].set(spread)
    return buffer.reshape(EXPERTS, N_EXPERT * CAP, D)


def from_experts(base, sums, routes, places, weights):
    sum_table = sums.reshape(EXPERTS, N_EXPERT, CAP, D)
    picked = sum_table[routes, source_ids(routes), places]
    weighted = jnp.sum(weights.reshape(N_EXPERT, TOK_DEV, TOPK, 1) * picked, axis=2)
    return (base.astype(jnp.float32) + weighted.reshape(TOKENS, D)).astype(jnp.bfloat16)


def forward_expert(row_block, gate_cols, up_cols, down_rows):
    pre_gate = jnp.dot(row_block, gate_cols, preferred_element_type=jnp.float32)
    pre_up = jnp.dot(row_block, up_cols, preferred_element_type=jnp.float32)
    hidden = (jax.nn.silu(pre_gate) * pre_up).astype(jnp.bfloat16)
    split_hidden = hidden.astype(jnp.float32).reshape(-1, HSPLIT, FF // HSPLIT)
    split_down = down_rows.astype(jnp.float32).reshape(HSPLIT, FF // HSPLIT, D)
    pieces = jnp.einsum("rsh,shd->srd", split_hidden, split_down).astype(jnp.bfloat16)
    return jnp.sum(pieces.astype(jnp.float32), axis=0)


def backward_expert(rows_x, rows_g, gate_cols, up_cols, down_rows):
    pre_gate = jnp.dot(rows_x, gate_cols, preferred_element_type=jnp.float32)
    pre_up = jnp.dot(rows_x, up_cols, preferred_element_type=jnp.float32)
    act_grad = jnp.dot(rows_g, down_rows.T, preferred_element_type=jnp.float32)
    sigmoid_gate = jax.nn.sigmoid(pre_gate)
    gate_grad = (act_grad * pre_up * sigmoid_gate * (1.0 + pre_gate * (1.0 - sigmoid_gate))).astype(jnp.bfloat16)
    up_grad = (act_grad * pre_gate * sigmoid_gate).astype(jnp.bfloat16)
    split_gate = gate_cols.astype(jnp.float32).reshape(D, HSPLIT, FF // HSPLIT)
    split_up = up_cols.astype(jnp.float32).reshape(D, HSPLIT, FF // HSPLIT)
    pieces = jnp.einsum("rsh,dsh->srd", gate_grad.astype(jnp.float32).reshape(-1, HSPLIT, FF // HSPLIT), split_gate)
    pieces = pieces + jnp.einsum("rsh,dsh->srd", up_grad.astype(jnp.float32).reshape(-1, HSPLIT, FF // HSPLIT), split_up)
    return jnp.sum(pieces.astype(jnp.bfloat16).astype(jnp.float32), axis=0)


def one_section(section_args):
    tokens_a, routes_a, gates_a, tokens_b, grads_b, routes_b, gates_b, gate_section, up_section, down_section = section_args
    gate_all = jnp.moveaxis(gate_section.reshape(D, EXPERTS, FF), 1, 0)
    up_all = jnp.moveaxis(up_section.reshape(D, EXPERTS, FF), 1, 0)
    down_all = down_section.reshape(EXPERTS, FF, D)
    ids_a = routes_a.reshape(N_EXPERT, TOK_DEV, TOPK).astype(jnp.int32)
    ids_b = routes_b.reshape(N_EXPERT, TOK_DEV, TOPK).astype(jnp.int32)
    places_a = jax.vmap(slot_table)(ids_a)
    places_b = jax.vmap(slot_table)(ids_b)
    rows_a = to_experts(tokens_a, ids_a, places_a)
    rows_xb = to_experts(tokens_b, ids_b, places_b)
    rows_gb = to_experts(grads_b, ids_b, places_b)

    def forward_item(item):
        return forward_expert(item[0], item[1], item[2], item[3])

    def backward_item(item):
        return backward_expert(item[0], item[1], item[2], item[3], item[4])

    sums_a = lax.map(forward_item, (rows_a, gate_all, up_all, down_all))
    sums_b = lax.map(backward_item, (rows_xb, rows_gb, gate_all, up_all, down_all))
    out_a = from_experts(tokens_a, sums_a, ids_a, places_a, gates_a)
    out_b = from_experts(grads_b, sums_b, ids_b, places_b, gates_b)
    return out_a, out_b


def reference(x_fwd, routes_fwd, gates_fwd, x_bwd, grad_bwd, routes_bwd, gates_bwd, gate_proj, up_proj, down_proj):
    outs_a, outs_b = lax.map(one_section, (x_fwd, routes_fwd, gates_fwd, x_bwd, grad_bwd, routes_bwd, gates_bwd, gate_proj, up_proj, down_proj))
    fwd_next = jnp.concatenate([jnp.zeros_like(outs_a[:1]), outs_a[:-1]], axis=0)
    bwd_next = jnp.concatenate([outs_b[1:], jnp.zeros_like(outs_b[:1])], axis=0)
    return fwd_next, bwd_next
```

```python
import functools
import jax
import jax.numpy as jnp
from jax import lax
from jax.sharding import PartitionSpec as P
from jax.experimental import pallas as pl
from jax.experimental.pallas import tpu as pltpu

HSPLIT = 4
TOPK = 1
MESH = pl.DeviceIdType.MESH
F32, BF16 = jnp.float32, jnp.bfloat16
COLS = 896


def to_column(row):
    count = row.shape[1]
    first = lax.broadcasted_iota(jnp.int32, (count, count), 0)
    second = lax.broadcasted_iota(jnp.int32, (count, count), 1)
    wide = jnp.broadcast_to(row, (count, count))
    return jnp.sum(jnp.where(first == second, wide, 0.0), axis=1, keepdims=True)


def places_rows(ids_row):
    count = ids_row.shape[1]
    first = lax.broadcasted_iota(jnp.int32, (count, count), 0)
    second = lax.broadcasted_iota(jnp.int32, (count, count), 1)
    ids = to_column(ids_row)
    same = ids == ids_row
    row = jnp.sum(jnp.where(same & (first < second), 1.0, 0.0), axis=0, keepdims=True)
    col = jnp.sum(jnp.where(same & (second < first), 1.0, 0.0), axis=1, keepdims=True)
    return ids_row, row, ids, col


def crossing_kernel(
    capacity,
    xf_ref, rf_ref, gf_ref, xb_ref, gb_ref, rb_ref, gtb_ref, wg_hbm, wu_hbm, wd_hbm,
    of_ref, ob_ref,
    wg, wu, wd, tok, far, mine, theirs, pbuf, csum, peer_in, comb, ret, outb,
    w_sem, s1_sem, s2_sem, fwd_sem, relay_sem, tok_sem,
    pb_send, pb_recv, cs_send, cs_recv, ret_send, ret_recv, out_send, out_recv,
):
    width = xf_ref.shape[-1]
    me = lax.axis_index("expert")
    pipe = lax.axis_index("pipe")
    n_pipe = lax.axis_size("pipe")
    z, core = lax.div(me, 2), lax.rem(me, 2)
    expert = lax.div(z, 2)
    outer = lax.rem(lax.div(z + 1, 2) + 1, 2)
    peer = me + 2 - 4 * lax.rem(z, 2)
    partner = me + 1 - 2 * core
    far_in = 2 * (2 - expert) + core
    far_out = 2 * (3 - 3 * expert) + core
    is_inner, is_outer = outer == 0, outer == 1
    has_next, has_prev = pipe < n_pipe - 1, pipe > 0

    weight_copies = [
        pltpu.make_async_copy(src.at[0], dst, w_sem.at[i])
        for i, (src, dst) in enumerate(((wg_hbm, wg), (wu_hbm, wu), (wd_hbm, wd)))
    ]
    for copy in weight_copies:
        copy.start()

    barrier = pltpu.get_barrier_semaphore()
    for other in (partner, peer, far_in, far_out):
        pl.semaphore_signal(barrier, inc=1, device_id={"expert": other}, device_id_type=MESH)

    @pl.when(has_next)
    def _():
        pl.semaphore_signal(barrier, inc=1, device_id={"pipe": pipe + 1}, device_id_type=MESH)

    @pl.when(has_prev)
    def _():
        pl.semaphore_signal(barrier, inc=1, device_id={"pipe": pipe - 1}, device_id_type=MESH)

    def remote(src, dst, send, recv, axis, index):
        return pltpu.make_async_remote_copy(
            src_ref=src, dst_ref=dst, send_sem=send, recv_sem=recv,
            device_id={axis: index}, device_id_type=MESH,
        )

    def columns(body):
        def step(i, carry):
            body(pl.ds(pl.multiple_of(i * COLS, COLS), COLS))
            return carry

        lax.fori_loop(0, width // COLS, step, 0)

    mine_id = expert.astype(F32)
    other_id = 1.0 - mine_id
    inputs = (xf_ref, xb_ref, gb_ref)

    def pickers(routes):
        ids_row, row, _, _ = places_rows(routes)
        slot = lax.broadcasted_iota(jnp.int32, (capacity, routes.shape[1]), 0).astype(F32)
        hit = slot == row
        return (
            jnp.where(hit & (ids_row == mine_id), 1.0, 0.0).astype(BF16),
            jnp.where(hit & (ids_row == other_id), 1.0, 0.0).astype(BF16),
        )

    def dispatch(a, picks):
        def body(at):
            block = inputs[a][0, :, at]
            tok[a, 0, 0, :, at] = jnp.dot(picks[0], block, preferred_element_type=F32).astype(BF16)
            far[a, :, at] = jnp.dot(picks[1], block, preferred_element_type=F32).astype(BF16)

        columns(body)

    def to_peer(a):
        return remote(tok.at[a, 0, 0], tok.at[a, 1, 0], s1_sem.at[a], tok_sem.at[a, 1, 0], "expert", peer)

    def to_far(a):
        k = 2 + outer
        return remote(far.at[a], tok.at[a, k, 0], s2_sem.at[a], tok_sem.at[a, k, 0], "expert", far_in)

    def to_partner(a, k):
        return remote(
            tok.at[a, k, 0], tok.at[a, k, 1], fwd_sem.at[a, k], tok_sem.at[a, k, 1], "expert", partner
        )

    def relay(a, k):
        return remote(
            tok.at[a, k, 0], tok.at[a, k, 0], relay_sem.at[a, k - 2], tok_sem.at[a, k, 0], "expert", peer
        )

    def half(m, k):
        return remote(theirs.at[m, k], pbuf.at[m, k], pb_send.at[m, k], pb_recv.at[m, k], "expert", partner)

    parts = range(width // COLS)

    def part(h):
        return pl.ds(h * COLS, COLS)

    def to_combiner(m, k, h):
        at = 0 if k == 1 else k
        return remote(
            csum.at[m, k, :, part(h)], peer_in.at[m, at, :, part(h)],
            cs_send.at[m, at, h], cs_recv.at[m, at, h], "expert", peer,
        )

    def to_home(m, k, h):
        home = far_in if k == 2 else far_out
        return remote(
            comb.at[m, k - 2, :, part(h)], ret.at[m, :, part(h)],
            ret_send.at[m, k - 2, h], ret_recv.at[m, h], "expert", home,
        )

    def to_section(m, h):
        dst = of_ref if m == 0 else ob_ref
        other = pipe + 1 if m == 0 else pipe - 1
        return remote(
            outb.at[m, :, part(h)], dst.at[0, :, part(h)],
            out_send.at[m, h], out_recv.at[m, h], "pipe", other,
        )

    def arrive(a, k):
        relay_like = to_peer(a) if k == 1 else relay(a, k)
        relay_like.wait_recv()
        if k >= 2:
            @pl.when(is_inner)
            def _():
                relay(a, k).start()
        to_partner(a, k).start()

    def rows_of(a, k):
        to_partner(a, k).wait_recv()
        return tok[a, k].reshape(2 * capacity, width)

    def keep(m, k, at, value):
        value = value.astype(BF16)
        mine[m, k, :, at] = value[:capacity]
        theirs[m, k, :, at] = value[capacity:]

    contract = (((1,), (1,)), ((), ()))

    def compute_fwd(k):
        rows = rows_of(0, k)
        pre_gate = jnp.dot(rows, wg[...], preferred_element_type=F32)
        pre_up = jnp.dot(rows, wu[...], preferred_element_type=F32)
        hidden = (pre_gate * jax.nn.sigmoid(pre_gate) * pre_up).astype(BF16)
        columns(lambda at: keep(0, k, at, jnp.dot(hidden, wd[:, at], preferred_element_type=F32)))
        half(0, k).start()

    def compute_bwd(k):
        rows_x, rows_g = rows_of(1, k), rows_of(2, k)
        pre_gate = jnp.dot(rows_x, wg[...], preferred_element_type=F32)
        pre_up = jnp.dot(rows_x, wu[...], preferred_element_type=F32)
        act_grad = lax.dot_general(rows_g, wd[...], contract, preferred_element_type=F32)
        sig = jax.nn.sigmoid(pre_gate)
        gate_grad = (act_grad * pre_up * sig * (1.0 + pre_gate * (1.0 - sig))).astype(BF16)
        up_grad = (act_grad * pre_gate * sig).astype(BF16)

        def body(at):
            total = lax.dot_general(gate_grad, wg[at, :], contract, preferred_element_type=F32)
            total = total + lax.dot_general(up_grad, wu[at, :], contract, preferred_element_type=F32)
            keep(1, k, at, total)

        columns(body)
        half(1, k).start()

    def reduce_chip(m, k):
        half(m, k).wait_recv()
        for h in parts:
            at = part(h)
            csum[m, k, :, at] = (mine[m, k, :, at].astype(F32) + pbuf[m, k, :, at].astype(F32)).astype(BF16)
            if k == 1:
                to_combiner(m, k, h).start()
            if k >= 2:
                @pl.when(is_outer)
                def _():
                    to_combiner(m, k, h).start()

    def combine(m, *groups):
        @pl.when(is_inner)
        def _():
            for h in parts:
                at = part(h)
                for k in groups:
                    to_combiner(m, k, h).wait_recv()
                    comb[m, k - 2, :, at] = (
                        csum[m, k, :, at].astype(F32) + peer_in[m, k, :, at].astype(F32)
                    ).astype(BF16)
                    to_home(m, k, h).start()

    def finish(m):
        routes = (rf_ref if m == 0 else rb_ref)[...].astype(F32)
        gates = to_column((gf_ref if m == 0 else gtb_ref)[...])
        base = xf_ref if m == 0 else gb_ref
        _, _, ids, col = places_rows(routes)
        slot = lax.broadcasted_iota(jnp.int32, (routes.shape[1], capacity), 1).astype(F32)
        hit = slot == col
        pick_mine = jnp.where(hit & (ids == mine_id), 1.0, 0.0).astype(BF16)
        pick_other = jnp.where(hit & (ids == other_id), 1.0, 0.0).astype(BF16)
        for h in parts:
            at = part(h)
            to_combiner(m, 1, h).wait_recv()
            to_home(m, 2, h).wait_recv()
            total = jnp.dot(pick_mine, csum[m, 0, :, at], preferred_element_type=F32)
            total = total + jnp.dot(pick_mine, peer_in[m, 0, :, at], preferred_element_type=F32)
            total = total + jnp.dot(pick_other, ret[m, :, at], preferred_element_type=F32)
            outb[m, :, at] = (base[0, :, at].astype(F32) + gates * total).astype(BF16)

            @pl.when(has_next if m == 0 else has_prev)
            def _():
                to_section(m, h).start()

    picks_f = pickers(rf_ref[...].astype(F32))
    picks_b = pickers(rb_ref[...].astype(F32))
    dispatch(0, picks_f)
    ends = lax.div(n_pipe - 1 - pipe + n_pipe - 2, n_pipe - 1) + lax.div(pipe + n_pipe - 2, n_pipe - 1)
    pl.semaphore_wait(barrier, 4 + ends)

    to_peer(0).start()
    to_far(0).start()
    to_partner(0, 0).start()
    dispatch(1, picks_b)
    to_peer(1).start()
    to_far(1).start()
    to_partner(1, 0).start()
    dispatch(2, picks_b)
    to_peer(2).start()
    to_far(2).start()
    to_partner(2, 0).start()

    @pl.when(pipe == 0)
    def _():
        of_ref[...] = jnp.zeros_like(of_ref)

    @pl.when(pipe == n_pipe - 1)
    def _():
        ob_ref[...] = jnp.zeros_like(ob_ref)

    for copy in weight_copies:
        copy.wait()

    compute_fwd(0)
    arrive(0, 1)
    compute_fwd(1)
    arrive(0, 2)
    reduce_chip(0, 0)
    reduce_chip(0, 1)
    compute_fwd(2)
    arrive(0, 3)
    arrive(1, 1)
    arrive(2, 1)
    compute_bwd(0)
    compute_fwd(3)
    reduce_chip(0, 2)
    arrive(1, 2)
    arrive(2, 2)
    compute_bwd(1)
    reduce_chip(0, 3)
    combine(0, 2)
    reduce_chip(1, 1)
    arrive(1, 3)
    compute_bwd(2)
    reduce_chip(1, 2)
    combine(0, 3)
    arrive(2, 3)
    reduce_chip(1, 0)
    compute_bwd(3)
    reduce_chip(1, 3)
    combine(1, 2)
    finish(0)
    combine(1, 3)
    finish(1)

    for a in range(3):
        to_peer(a).wait_send()
        to_far(a).wait_send()
        for k in range(4):
            to_partner(a, k).wait_send()

    for m in range(2):
        for k in range(4):
            half(m, k).wait_send()
        for h in parts:
            to_combiner(m, 1, h).wait_send()

    @pl.when(is_inner)
    def _():
        for k in (2, 3):
            for a in range(3):
                relay(a, k).wait_send()
            for m in range(2):
                for h in parts:
                    to_home(m, k, h).wait_send()

    @pl.when(is_outer)
    def _():
        for k in (2, 3):
            for m in range(2):
                for h in parts:
                    to_combiner(m, k, h).wait_send()

    @pl.when(has_next)
    def _():
        for h in parts:
            to_section(0, h).wait_send()
            to_section(1, h).wait_recv()

    @pl.when(has_prev)
    def _():
        for h in parts:
            to_section(0, h).wait_recv()
            to_section(1, h).wait_send()


def crossing_body(xf, rf, gf, xb, gb, rb, gtb, wg, wu, wd):
    _, rows, width = xf.shape
    capacity = min(rows, rows * TOPK * 3 // 4)
    hid = wg.shape[2]
    parts = width // COLS
    vmem = pl.BlockSpec(memory_space=pltpu.VMEM)
    hbm = pl.BlockSpec(memory_space=pl.ANY)
    block = (capacity, width)
    dma = pltpu.SemaphoreType.DMA
    out = jax.ShapeDtypeStruct(xf.shape, BF16)
    return pl.pallas_call(
        functools.partial(crossing_kernel, capacity),
        out_shape=(out, out),
        in_specs=[vmem] * 7 + [hbm] * 3,
        out_specs=(vmem, vmem),
        scratch_shapes=[
            pltpu.VMEM((width, hid), BF16),
            pltpu.VMEM((width, hid), BF16),
            pltpu.VMEM((hid, width), BF16),
            pltpu.VMEM((3, 4, 2) + block, BF16),
            pltpu.VMEM((3,) + block, BF16),
            pltpu.VMEM((2, 4) + block, BF16),
            pltpu.VMEM((2, 4) + block, BF16),
            pltpu.VMEM((2, 4) + block, BF16),
            pltpu.VMEM((2, 4) + block, BF16),
            pltpu.VMEM((2, 4) + block, BF16),
            pltpu.VMEM((2, 2) + block, BF16),
            pltpu.VMEM((2,) + block, BF16),
            pltpu.VMEM((2, rows, width), BF16),
            dma((3,)), dma((3,)), dma((3,)), dma((3, 4)), dma((3, 2)), dma((3, 4, 2)),
            dma((2, 4)), dma((2, 4)), dma((2, 4, parts)), dma((2, 4, parts)), dma((2, 2, parts)),
            dma((2, parts)), dma((2, parts)), dma((2, parts)),
        ],
        compiler_params=pltpu.CompilerParams(
            collective_id=0, has_side_effects=True, vmem_limit_bytes=60 * 1024 * 1024
        ),
    )(xf, rf.reshape(1, rows), gf.reshape(1, rows), xb, gb, rb.reshape(1, rows), gtb.reshape(1, rows), wg, wu, wd)


def shifted(block, axis, distance):
    devices = range(lax.axis_size(axis))
    route = [(i - distance, i) for i in devices if i - distance in devices]
    return lax.ppermute(block, axis, route)


def slot_table(routes, experts, capacity):
    flat_ids = routes.reshape(-1)
    number = jnp.arange(flat_ids.shape[0], dtype=jnp.int32)
    same = flat_ids[:, None] == flat_ids[None, :]
    before = number[None, :] < number[:, None]
    places = jnp.sum((same & before).astype(jnp.int32), axis=1)
    return (flat_ids * capacity + places).reshape(routes.shape)


def dispatch_rows(tokens, slot_ids, experts, capacity):
    numbered = jnp.arange(experts * capacity, dtype=jnp.int32)
    picker = jnp.any(slot_ids[None, :, :] == numbered[:, None, None], axis=2).astype(jnp.bfloat16)
    filled = jnp.dot(picker, tokens, preferred_element_type=jnp.float32).astype(jnp.bfloat16)
    return jnp.repeat(filled.reshape(experts, capacity, tokens.shape[1]), HSPLIT, axis=0)


def combine_rows(base, returned, slot_ids, weights, experts, capacity):
    width = base.shape[1]
    summed = jnp.sum(returned.astype(jnp.float32).reshape(experts, HSPLIT, capacity, width), axis=1)
    summed = summed.reshape(experts * capacity, width)
    numbered = jnp.arange(experts * capacity, dtype=jnp.int32)
    mixing = jnp.sum(
        weights[:, :, None] * (slot_ids[:, :, None] == numbered[None, None, :]).astype(jnp.float32),
        axis=1,
    )
    total = base.astype(jnp.float32) + jnp.dot(mixing, summed, precision=lax.Precision.HIGHEST)
    return total.astype(jnp.bfloat16)


def forward_rows(received, gate_cols, up_cols, down_rows):
    in_shape = received.shape
    row_block = received.reshape(-1, in_shape[-1])
    pre_gate = jnp.dot(row_block, gate_cols, preferred_element_type=jnp.float32)
    pre_up = jnp.dot(row_block, up_cols, preferred_element_type=jnp.float32)
    hidden = (jax.nn.silu(pre_gate) * pre_up).astype(jnp.bfloat16)
    result = jnp.dot(hidden, down_rows, preferred_element_type=jnp.float32).astype(jnp.bfloat16)
    return result.reshape(in_shape)


def backward_rows(received_x, received_g, gate_cols, up_cols, down_rows):
    in_shape = received_x.shape
    rows_x = received_x.reshape(-1, in_shape[-1])
    rows_g = received_g.reshape(-1, in_shape[-1])
    contract = (((1,), (1,)), ((), ()))
    pre_gate = jnp.dot(rows_x, gate_cols, preferred_element_type=jnp.float32)
    pre_up = jnp.dot(rows_x, up_cols, preferred_element_type=jnp.float32)
    act_grad = lax.dot_general(rows_g, down_rows, contract, preferred_element_type=jnp.float32)
    sigmoid_gate = jax.nn.sigmoid(pre_gate)
    gate_grad = (act_grad * pre_up * sigmoid_gate * (1.0 + pre_gate * (1.0 - sigmoid_gate))).astype(
        jnp.bfloat16
    )
    up_grad = (act_grad * pre_gate * sigmoid_gate).astype(jnp.bfloat16)
    back_rows = lax.dot_general(gate_grad, gate_cols, contract, preferred_element_type=jnp.float32)
    back_rows = back_rows + lax.dot_general(
        up_grad, up_cols, contract, preferred_element_type=jnp.float32
    )
    return back_rows.astype(jnp.bfloat16).reshape(in_shape)


def body(
    x_fwd,
    routes_fwd,
    gates_fwd,
    x_bwd,
    grad_bwd,
    routes_bwd,
    gates_bwd,
    gate_proj,
    up_proj,
    down_proj,
):
    tokens_a = x_fwd[0]
    tokens_b = x_bwd[0]
    grads_b = grad_bwd[0]
    gate_cols = gate_proj[0]
    up_cols = up_proj[0]
    down_rows = down_proj[0]
    experts = lax.axis_size("expert") // HSPLIT
    tok_rows = tokens_a.shape[0]
    capacity = min(tok_rows, tok_rows * TOPK * 3 // (2 * experts))
    slots_a = slot_table(routes_fwd[0], experts, capacity)
    slots_b = slot_table(routes_bwd[0], experts, capacity)
    send_a = dispatch_rows(tokens_a, slots_a, experts, capacity)
    send_x = dispatch_rows(tokens_b, slots_b, experts, capacity)
    send_g = dispatch_rows(grads_b, slots_b, experts, capacity)
    back_a = lax.all_to_all(
        forward_rows(
            lax.all_to_all(send_a, "expert", split_axis=0, concat_axis=0, tiled=True),
            gate_cols,
            up_cols,
            down_rows,
        ),
        "expert",
        split_axis=0,
        concat_axis=0,
        tiled=True,
    )
    back_b = lax.all_to_all(
        backward_rows(
            lax.all_to_all(send_x, "expert", split_axis=0, concat_axis=0, tiled=True),
            lax.all_to_all(send_g, "expert", split_axis=0, concat_axis=0, tiled=True),
            gate_cols,
            up_cols,
            down_rows,
        ),
        "expert",
        split_axis=0,
        concat_axis=0,
        tiled=True,
    )
    out_fwd = combine_rows(tokens_a, back_a, slots_a, gates_fwd[0], experts, capacity)
    out_bwd = combine_rows(grads_b, back_b, slots_b, gates_bwd[0], experts, capacity)
    fwd_next = shifted(out_fwd, "pipe", 1)
    bwd_next = shifted(out_bwd, "pipe", -1)
    return (fwd_next[None], bwd_next[None])


def solution(mesh):
    in_specs = (
        P("pipe", "expert", None),
        P("pipe", "expert", None),
        P("pipe", "expert", None),
        P("pipe", "expert", None),
        P("pipe", "expert", None),
        P("pipe", "expert", None),
        P("pipe", "expert", None),
        P("pipe", None, "expert"),
        P("pipe", None, "expert"),
        P("pipe", "expert", None),
    )
    out_specs = (P("pipe", "expert", None), P("pipe", "expert", None))
    two_experts = mesh.shape["expert"] == 2 * HSPLIT
    chosen = crossing_body if two_experts else body
    return jax.shard_map(chosen, mesh=mesh, in_specs=in_specs, out_specs=out_specs, check_vma=False)
```

```python
import functools
import jax
import jax.numpy as jnp
from jax import lax
from jax.sharding import PartitionSpec as P
from jax.experimental import pallas as pl
from jax.experimental.pallas import tpu as pltpu

HSPLIT = 4
TOPK = 1
MESH = pl.DeviceIdType.MESH
F32, BF16 = jnp.float32, jnp.bfloat16
COLS = 896


def to_column(row):
    count = row.shape[1]
    first = lax.broadcasted_iota(jnp.int32, (count, count), 0)
    second = lax.broadcasted_iota(jnp.int32, (count, count), 1)
    wide = jnp.broadcast_to(row, (count, count))
    return jnp.sum(jnp.where(first == second, wide, 0.0), axis=1, keepdims=True)


def places_rows(ids_row):
    count = ids_row.shape[1]
    first = lax.broadcasted_iota(jnp.int32, (count, count), 0)
    second = lax.broadcasted_iota(jnp.int32, (count, count), 1)
    ids = to_column(ids_row)
    same = ids == ids_row
    row = jnp.sum(jnp.where(same & (first < second), 1.0, 0.0), axis=0, keepdims=True)
    col = jnp.sum(jnp.where(same & (second < first), 1.0, 0.0), axis=1, keepdims=True)
    return ids_row, row, ids, col


def crossing_kernel(
    capacity,
    xf_ref, rf_ref, gf_ref, xb_ref, gb_ref, rb_ref, gtb_ref, wg_hbm, wu_hbm, wd_hbm,
    of_ref, ob_ref,
    wg, wu, wd, ids_out, ids_in, raw, tok, far, mine, theirs, pbuf, csum, peer_in, comb, ret, dense, dense_in, outb,
    w_sem, ids_sem, raw_send, raw_recv, s1_sem, s2_sem, fwd_sem, relay_sem, tok_sem,
    pb_send, pb_recv, cs_send, cs_recv, ret_send, ret_recv, de_send, de_recv, out_send, out_recv,
):
    rows_here, width = xf_ref.shape[1:]
    me = lax.axis_index("expert")
    pipe = lax.axis_index("pipe")
    n_pipe = lax.axis_size("pipe")
    z, core = lax.div(me, 2), lax.rem(me, 2)
    expert = lax.div(z, 2)
    outer = lax.rem(lax.div(z + 1, 2) + 1, 2)
    peer = me + 2 - 4 * lax.rem(z, 2)
    partner = me + 1 - 2 * core
    across = 2 * (2 - expert) + core
    is_inner, is_outer = outer == 0, outer == 1
    has_next, has_prev = pipe < n_pipe - 1, pipe > 0

    weight_copies = [
        pltpu.make_async_copy(src.at[0], dst, w_sem.at[i])
        for i, (src, dst) in enumerate(((wg_hbm, wg), (wu_hbm, wu), (wd_hbm, wd)))
    ]
    for copy in weight_copies:
        copy.start()

    barrier = pltpu.get_barrier_semaphore()
    for other in (partner, peer):
        pl.semaphore_signal(barrier, inc=1, device_id={"expert": other}, device_id_type=MESH)

    @pl.when(is_inner)
    def _():
        pl.semaphore_signal(barrier, inc=1, device_id={"expert": across}, device_id_type=MESH)

    @pl.when(has_next)
    def _():
        pl.semaphore_signal(barrier, inc=1, device_id={"pipe": pipe + 1}, device_id_type=MESH)

    @pl.when(has_prev)
    def _():
        pl.semaphore_signal(barrier, inc=1, device_id={"pipe": pipe - 1}, device_id_type=MESH)

    def remote(src, dst, send, recv, axis, index):
        return pltpu.make_async_remote_copy(
            src_ref=src, dst_ref=dst, send_sem=send, recv_sem=recv,
            device_id={axis: index}, device_id_type=MESH,
        )

    def columns(body):
        def step(i, carry):
            body(pl.ds(pl.multiple_of(i * COLS, COLS), COLS))
            return carry

        lax.fori_loop(0, width // COLS, step, 0)

    mine_id = expert.astype(F32)
    other_id = 1.0 - mine_id
    inputs = (xf_ref, xb_ref, gb_ref)

    def pickers(routes):
        ids_row, row, _, _ = places_rows(routes)
        slot = lax.broadcasted_iota(jnp.int32, (capacity, routes.shape[1]), 0).astype(F32)
        hit = slot == row
        return (
            jnp.where(hit & (ids_row == mine_id), 1.0, 0.0).astype(BF16),
            jnp.where(hit & (ids_row == other_id), 1.0, 0.0).astype(BF16),
        )

    def placers(routes):
        _, _, ids, col = places_rows(routes)
        slot = lax.broadcasted_iota(jnp.int32, (routes.shape[1], capacity), 1).astype(F32)
        hit = slot == col
        return (
            jnp.where(hit & (ids == mine_id), 1.0, 0.0).astype(BF16),
            jnp.where(hit & (ids == other_id), 1.0, 0.0).astype(BF16),
        )

    def near_ids(m):
        return ids_in[m:m + 1, :rows_here]

    def pick(a, k, source, picks):
        def body(at):
            block = source(at)
            tok[a, k, 0, :, at] = jnp.dot(picks[0], block, preferred_element_type=F32).astype(BF16)

            @pl.when(is_inner)
            def _():
                far[a, k, :, at] = jnp.dot(picks[1], block, preferred_element_type=F32).astype(BF16)

        columns(body)

    def dispatch(a, picks):
        pick(a, 0, lambda at: inputs[a][0, :, at], picks)

    def to_near():
        return remote(ids_out, ids_in, ids_sem.at[0], ids_sem.at[1], "expert", peer)

    def to_raw(a):
        return remote(inputs[a].at[0], raw.at[a], raw_send.at[a], raw_recv.at[a], "expert", peer)

    def to_peer(a):
        return remote(tok.at[a, 0, 0], tok.at[a, 1, 0], s1_sem.at[a], tok_sem.at[a, 1, 0], "expert", peer)

    def to_across(a, k):
        return remote(
            far.at[a, k], tok.at[a, k + 2, 0], s2_sem.at[a, k], tok_sem.at[a, k + 2, 0], "expert", across
        )

    def to_partner(a, k):
        return remote(
            tok.at[a, k, 0], tok.at[a, k, 1], fwd_sem.at[a, k], tok_sem.at[a, k, 1], "expert", partner
        )

    def relay(a, k):
        return remote(
            tok.at[a, k, 0], tok.at[a, k, 0], relay_sem.at[a, k - 2], tok_sem.at[a, k, 0], "expert", peer
        )

    def half(m, k):
        return remote(theirs.at[m, k], pbuf.at[m, k], pb_send.at[m, k], pb_recv.at[m, k], "expert", partner)

    parts = range(width // COLS)

    def part(h):
        return pl.ds(h * COLS, COLS)

    def to_combiner(m, k, h):
        return remote(
            csum.at[m, k, :, part(h)], peer_in.at[m, k - 1, :, part(h)],
            cs_send.at[m, k - 1, h], cs_recv.at[m, k - 1, h], "expert", peer,
        )

    def to_home(m, k, h):
        return remote(
            comb.at[m, k - 2, :, part(h)], ret.at[m, k - 2, :, part(h)],
            ret_send.at[m, k - 2, h], ret_recv.at[m, k - 2, h], "expert", across,
        )

    def to_outer(m, h):
        return remote(
            dense.at[m, :, part(h)], dense_in.at[m, :, part(h)],
            de_send.at[m, h], de_recv.at[m, h], "expert", peer,
        )

    def to_section(m, h):
        dst = of_ref if m == 0 else ob_ref
        other = pipe + 1 if m == 0 else pipe - 1
        return remote(
            outb.at[m, :, part(h)], dst.at[0, :, part(h)],
            out_send.at[m, h], out_recv.at[m, h], "pipe", other,
        )

    def near(a):
        @pl.when(is_inner)
        def _():
            if a == 0:
                to_near().wait_recv()
            to_raw(a).wait_recv()
            pick(a, 1, lambda at: raw[a, :, at], pickers(near_ids(min(a, 1))))
            to_across(a, 1).start()
            to_partner(a, 1).start()

    def given(a):
        @pl.when(is_outer)
        def _():
            to_peer(a).wait_recv()
            to_partner(a, 1).start()

    def arrive(a, k):
        relay(a, k).wait_recv()

        @pl.when(is_inner)
        def _():
            relay(a, k).start()

        to_partner(a, k).start()

    def rows_of(a, k):
        to_partner(a, k).wait_recv()
        return tok[a, k].reshape(2 * capacity, width)

    def keep(m, k, at, value):
        value = value.astype(BF16)
        mine[m, k, :, at] = value[:capacity]
        theirs[m, k, :, at] = value[capacity:]

    contract = (((1,), (1,)), ((), ()))

    def compute_fwd(k):
        rows = rows_of(0, k)
        pre_gate = jnp.dot(rows, wg[...], preferred_element_type=F32)
        pre_up = jnp.dot(rows, wu[...], preferred_element_type=F32)
        hidden = (pre_gate * jax.nn.sigmoid(pre_gate) * pre_up).astype(BF16)
        columns(lambda at: keep(0, k, at, jnp.dot(hidden, wd[:, at], preferred_element_type=F32)))
        half(0, k).start()

    def compute_bwd(k):
        rows_x, rows_g = rows_of(1, k), rows_of(2, k)
        pre_gate = jnp.dot(rows_x, wg[...], preferred_element_type=F32)
        pre_up = jnp.dot(rows_x, wu[...], preferred_element_type=F32)
        act_grad = lax.dot_general(rows_g, wd[...], contract, preferred_element_type=F32)
        sig = jax.nn.sigmoid(pre_gate)
        gate_grad = (act_grad * pre_up * sig * (1.0 + pre_gate * (1.0 - sig))).astype(BF16)
        up_grad = (act_grad * pre_gate * sig).astype(BF16)

        def body(at):
            total = lax.dot_general(gate_grad, wg[at, :], contract, preferred_element_type=F32)
            total = total + lax.dot_general(up_grad, wu[at, :], contract, preferred_element_type=F32)
            keep(1, k, at, total)

        columns(body)
        half(1, k).start()

    def reduce_chip(m, k):
        half(m, k).wait_recv()
        for h in parts:
            at = part(h)
            csum[m, k, :, at] = (mine[m, k, :, at].astype(F32) + pbuf[m, k, :, at].astype(F32)).astype(BF16)
            if k >= 1:
                @pl.when(is_outer)
                def _():
                    to_combiner(m, k, h).start()

    def combine(m, k):
        @pl.when(is_inner)
        def _():
            for h in parts:
                at = part(h)
                to_combiner(m, k, h).wait_recv()
                comb[m, k - 2, :, at] = (
                    csum[m, k, :, at].astype(F32) + peer_in[m, k - 1, :, at].astype(F32)
                ).astype(BF16)
                to_home(m, k, h).start()

    def serve(m):
        @pl.when(is_inner)
        def _():
            pick_mine, pick_other = placers(near_ids(m))
            for h in parts:
                at = part(h)
                to_home(m, 3, h).wait_recv()
                total = jnp.dot(pick_mine, csum[m, 1, :, at], preferred_element_type=F32)
                total = total + jnp.dot(pick_other, ret[m, 1, :, at], preferred_element_type=F32)
                dense[m, :, at] = total.astype(BF16)
                to_outer(m, h).start()

    def finish(m):
        pick_mine, pick_other = placers((rf_ref if m == 0 else rb_ref)[...].astype(F32))
        gates = to_column((gf_ref if m == 0 else gtb_ref)[...])
        base = xf_ref if m == 0 else gb_ref

        def close(h, total):
            at = part(h)
            outb[m, :, at] = (base[0, :, at].astype(F32) + gates * total).astype(BF16)

            @pl.when(has_next if m == 0 else has_prev)
            def _():
                to_section(m, h).start()

        @pl.when(is_inner)
        def _():
            for h in parts:
                at = part(h)
                to_combiner(m, 1, h).wait_recv()
                to_home(m, 2, h).wait_recv()
                total = jnp.dot(pick_mine, csum[m, 0, :, at], preferred_element_type=F32)
                total = total + jnp.dot(pick_mine, peer_in[m, 0, :, at], preferred_element_type=F32)
                close(h, total + jnp.dot(pick_other, ret[m, 0, :, at], preferred_element_type=F32))

        @pl.when(is_outer)
        def _():
            for h in parts:
                at = part(h)
                total = jnp.dot(pick_mine, csum[m, 0, :, at], preferred_element_type=F32)
                to_outer(m, h).wait_recv()
                close(h, total + dense_in[m, :, at].astype(F32))

    ids_out[...] = jnp.zeros_like(ids_out)
    ids_out[0:1, :rows_here] = rf_ref[...].astype(F32)
    ids_out[1:2, :rows_here] = rb_ref[...].astype(F32)
    picks_f = pickers(rf_ref[...].astype(F32))
    picks_b = pickers(rb_ref[...].astype(F32))
    dispatch(0, picks_f)
    ends = lax.div(n_pipe - 1 - pipe + n_pipe - 2, n_pipe - 1) + lax.div(pipe + n_pipe - 2, n_pipe - 1)
    pl.semaphore_wait(barrier, 3 - outer + ends)

    @pl.when(is_outer)
    def _():
        to_near().start()
        for a in range(3):
            to_raw(a).start()

    @pl.when(is_inner)
    def _():
        to_peer(0).start()
        to_across(0, 0).start()

    to_partner(0, 0).start()
    dispatch(1, picks_b)

    @pl.when(is_inner)
    def _():
        to_peer(1).start()
        to_across(1, 0).start()

    to_partner(1, 0).start()
    dispatch(2, picks_b)

    @pl.when(is_inner)
    def _():
        to_across(2, 0).start()

    to_partner(2, 0).start()

    @pl.when(pipe == 0)
    def _():
        of_ref[...] = jnp.zeros_like(of_ref)

    @pl.when(pipe == n_pipe - 1)
    def _():
        ob_ref[...] = jnp.zeros_like(ob_ref)

    for copy in weight_copies:
        copy.wait()

    compute_fwd(0)
    compute_bwd(0)
    arrive(0, 2)
    near(0)
    given(0)
    compute_fwd(1)
    arrive(1, 2)
    near(1)
    given(1)
    compute_fwd(2)
    arrive(2, 2)
    near(2)
    reduce_chip(0, 1)
    reduce_chip(0, 2)
    compute_bwd(2)
    arrive(0, 3)
    reduce_chip(1, 2)
    compute_fwd(3)
    arrive(1, 3)
    reduce_chip(0, 3)
    reduce_chip(0, 0)
    arrive(2, 3)

    @pl.when(is_inner)
    def _():
        to_peer(2).start()

    compute_bwd(3)
    reduce_chip(1, 3)
    reduce_chip(1, 0)
    combine(0, 2)
    combine(1, 2)
    combine(0, 3)
    given(2)
    compute_bwd(1)
    reduce_chip(1, 1)
    serve(0)
    finish(0)
    combine(1, 3)
    serve(1)
    finish(1)

    for a in range(3):
        for k in range(4):
            to_partner(a, k).wait_send()

    for m in range(2):
        for k in range(4):
            half(m, k).wait_send()

    @pl.when(is_inner)
    def _():
        for a in range(3):
            to_peer(a).wait_send()
            for k in range(2):
                to_across(a, k).wait_send()
                relay(a, k + 2).wait_send()
        for m in range(2):
            for h in parts:
                to_outer(m, h).wait_send()
                for k in (2, 3):
                    to_home(m, k, h).wait_send()

    @pl.when(is_outer)
    def _():
        to_near().wait_send()
        for a in range(3):
            to_raw(a).wait_send()
        for m in range(2):
            for k in (1, 2, 3):
                for h in parts:
                    to_combiner(m, k, h).wait_send()

    @pl.when(has_next)
    def _():
        for h in parts:
            to_section(0, h).wait_send()
            to_section(1, h).wait_recv()

    @pl.when(has_prev)
    def _():
        for h in parts:
            to_section(0, h).wait_recv()
            to_section(1, h).wait_send()


def crossing_body(xf, rf, gf, xb, gb, rb, gtb, wg, wu, wd):
    _, rows, width = xf.shape
    capacity = min(rows, rows * TOPK * 3 // 4)
    hid = wg.shape[2]
    parts = width // COLS
    vmem = pl.BlockSpec(memory_space=pltpu.VMEM)
    hbm = pl.BlockSpec(memory_space=pl.ANY)
    block = (capacity, width)
    dma = pltpu.SemaphoreType.DMA
    out = jax.ShapeDtypeStruct(xf.shape, BF16)
    return pl.pallas_call(
        functools.partial(crossing_kernel, capacity),
        out_shape=(out, out),
        in_specs=[vmem] * 7 + [hbm] * 3,
        out_specs=(vmem, vmem),
        scratch_shapes=[
            pltpu.VMEM((width, hid), BF16),
            pltpu.VMEM((width, hid), BF16),
            pltpu.VMEM((hid, width), BF16),
            pltpu.VMEM((8, max(rows, 128)), F32),
            pltpu.VMEM((8, max(rows, 128)), F32),
            pltpu.VMEM((3, rows, width), BF16),
            pltpu.VMEM((3, 4, 2) + block, BF16),
            pltpu.VMEM((3, 2) + block, BF16),
            pltpu.VMEM((2, 4) + block, BF16),
            pltpu.VMEM((2, 4) + block, BF16),
            pltpu.VMEM((2, 4) + block, BF16),
            pltpu.VMEM((2, 4) + block, BF16),
            pltpu.VMEM((2, 3) + block, BF16),
            pltpu.VMEM((2, 2) + block, BF16),
            pltpu.VMEM((2, 2) + block, BF16),
            pltpu.VMEM((2, rows, width), BF16),
            pltpu.VMEM((2, rows, width), BF16),
            pltpu.VMEM((2, rows, width), BF16),
            dma((3,)), dma((2,)), dma((3,)), dma((3,)), dma((3,)), dma((3, 2)), dma((3, 4)), dma((3, 2)), dma((3, 4, 2)),
            dma((2, 4)), dma((2, 4)), dma((2, 3, parts)), dma((2, 3, parts)), dma((2, 2, parts)), dma((2, 2, parts)),
            dma((2, parts)), dma((2, parts)), dma((2, parts)), dma((2, parts)),
        ],
        compiler_params=pltpu.CompilerParams(
            collective_id=0, has_side_effects=True, vmem_limit_bytes=60 * 1024 * 1024
        ),
    )(xf, rf.reshape(1, rows), gf.reshape(1, rows), xb, gb, rb.reshape(1, rows), gtb.reshape(1, rows), wg, wu, wd)


def shifted(block, axis, distance):
    devices = range(lax.axis_size(axis))
    route = [(i - distance, i) for i in devices if i - distance in devices]
    return lax.ppermute(block, axis, route)


def slot_table(routes, experts, capacity):
    flat_ids = routes.reshape(-1)
    number = jnp.arange(flat_ids.shape[0], dtype=jnp.int32)
    same = flat_ids[:, None] == flat_ids[None, :]
    before = number[None, :] < number[:, None]
    places = jnp.sum((same & before).astype(jnp.int32), axis=1)
    return (flat_ids * capacity + places).reshape(routes.shape)


def dispatch_rows(tokens, slot_ids, experts, capacity):
    numbered = jnp.arange(experts * capacity, dtype=jnp.int32)
    picker = jnp.any(slot_ids[None, :, :] == numbered[:, None, None], axis=2).astype(jnp.bfloat16)
    filled = jnp.dot(picker, tokens, preferred_element_type=jnp.float32).astype(jnp.bfloat16)
    return jnp.repeat(filled.reshape(experts, capacity, tokens.shape[1]), HSPLIT, axis=0)


def combine_rows(base, returned, slot_ids, weights, experts, capacity):
    width = base.shape[1]
    summed = jnp.sum(returned.astype(jnp.float32).reshape(experts, HSPLIT, capacity, width), axis=1)
    summed = summed.reshape(experts * capacity, width)
    numbered = jnp.arange(experts * capacity, dtype=jnp.int32)
    mixing = jnp.sum(
        weights[:, :, None] * (slot_ids[:, :, None] == numbered[None, None, :]).astype(jnp.float32),
        axis=1,
    )
    total = base.astype(jnp.float32) + jnp.dot(mixing, summed, precision=lax.Precision.HIGHEST)
    return total.astype(jnp.bfloat16)


def forward_rows(received, gate_cols, up_cols, down_rows):
    in_shape = received.shape
    row_block = received.reshape(-1, in_shape[-1])
    pre_gate = jnp.dot(row_block, gate_cols, preferred_element_type=jnp.float32)
    pre_up = jnp.dot(row_block, up_cols, preferred_element_type=jnp.float32)
    hidden = (jax.nn.silu(pre_gate) * pre_up).astype(jnp.bfloat16)
    result = jnp.dot(hidden, down_rows, preferred_element_type=jnp.float32).astype(jnp.bfloat16)
    return result.reshape(in_shape)


def backward_rows(received_x, received_g, gate_cols, up_cols, down_rows):
    in_shape = received_x.shape
    rows_x = received_x.reshape(-1, in_shape[-1])
    rows_g = received_g.reshape(-1, in_shape[-1])
    contract = (((1,), (1,)), ((), ()))
    pre_gate = jnp.dot(rows_x, gate_cols, preferred_element_type=jnp.float32)
    pre_up = jnp.dot(rows_x, up_cols, preferred_element_type=jnp.float32)
    act_grad = lax.dot_general(rows_g, down_rows, contract, preferred_element_type=jnp.float32)
    sigmoid_gate = jax.nn.sigmoid(pre_gate)
    gate_grad = (act_grad * pre_up * sigmoid_gate * (1.0 + pre_gate * (1.0 - sigmoid_gate))).astype(
        jnp.bfloat16
    )
    up_grad = (act_grad * pre_gate * sigmoid_gate).astype(jnp.bfloat16)
    back_rows = lax.dot_general(gate_grad, gate_cols, contract, preferred_element_type=jnp.float32)
    back_rows = back_rows + lax.dot_general(
        up_grad, up_cols, contract, preferred_element_type=jnp.float32
    )
    return back_rows.astype(jnp.bfloat16).reshape(in_shape)


def body(
    x_fwd,
    routes_fwd,
    gates_fwd,
    x_bwd,
    grad_bwd,
    routes_bwd,
    gates_bwd,
    gate_proj,
    up_proj,
    down_proj,
):
    tokens_a = x_fwd[0]
    tokens_b = x_bwd[0]
    grads_b = grad_bwd[0]
    gate_cols = gate_proj[0]
    up_cols = up_proj[0]
    down_rows = down_proj[0]
    experts = lax.axis_size("expert") // HSPLIT
    tok_rows = tokens_a.shape[0]
    capacity = min(tok_rows, tok_rows * TOPK * 3 // (2 * experts))
    slots_a = slot_table(routes_fwd[0], experts, capacity)
    slots_b = slot_table(routes_bwd[0], experts, capacity)
    send_a = dispatch_rows(tokens_a, slots_a, experts, capacity)
    send_x = dispatch_rows(tokens_b, slots_b, experts, capacity)
    send_g = dispatch_rows(grads_b, slots_b, experts, capacity)
    back_a = lax.all_to_all(
        forward_rows(
            lax.all_to_all(send_a, "expert", split_axis=0, concat_axis=0, tiled=True),
            gate_cols,
            up_cols,
            down_rows,
        ),
        "expert",
        split_axis=0,
        concat_axis=0,
        tiled=True,
    )
    back_b = lax.all_to_all(
        backward_rows(
            lax.all_to_all(send_x, "expert", split_axis=0, concat_axis=0, tiled=True),
            lax.all_to_all(send_g, "expert", split_axis=0, concat_axis=0, tiled=True),
            gate_cols,
            up_cols,
            down_rows,
        ),
        "expert",
        split_axis=0,
        concat_axis=0,
        tiled=True,
    )
    out_fwd = combine_rows(tokens_a, back_a, slots_a, gates_fwd[0], experts, capacity)
    out_bwd = combine_rows(grads_b, back_b, slots_b, gates_bwd[0], experts, capacity)
    fwd_next = shifted(out_fwd, "pipe", 1)
    bwd_next = shifted(out_bwd, "pipe", -1)
    return (fwd_next[None], bwd_next[None])


def solution(mesh):
    in_specs = (
        P("pipe", "expert", None),
        P("pipe", "expert", None),
        P("pipe", "expert", None),
        P("pipe", "expert", None),
        P("pipe", "expert", None),
        P("pipe", "expert", None),
        P("pipe", "expert", None),
        P("pipe", None, "expert"),
        P("pipe", None, "expert"),
        P("pipe", "expert", None),
    )
    out_specs = (P("pipe", "expert", None), P("pipe", "expert", None))
    two_experts = mesh.shape["expert"] == 2 * HSPLIT
    chosen = crossing_body if two_experts else body
    return jax.shard_map(chosen, mesh=mesh, in_specs=in_specs, out_specs=out_specs, check_vma=False)
```

```python
import functools
import jax
import jax.numpy as jnp
from jax import lax
from jax.sharding import PartitionSpec as P
from jax.experimental import pallas as pl
from jax.experimental.pallas import tpu as pltpu

HSPLIT = 4
TOPK = 1
MESH = pl.DeviceIdType.MESH
F32, BF16 = jnp.float32, jnp.bfloat16
COLS = 896


def to_column(row):
    count = row.shape[1]
    first = lax.broadcasted_iota(jnp.int32, (count, count), 0)
    second = lax.broadcasted_iota(jnp.int32, (count, count), 1)
    wide = jnp.broadcast_to(row, (count, count))
    return jnp.sum(jnp.where(first == second, wide, 0.0), axis=1, keepdims=True)


def places_rows(ids_row):
    count = ids_row.shape[1]
    first = lax.broadcasted_iota(jnp.int32, (count, count), 0)
    second = lax.broadcasted_iota(jnp.int32, (count, count), 1)
    ids = to_column(ids_row)
    same = ids == ids_row
    row = jnp.sum(jnp.where(same & (first < second), 1.0, 0.0), axis=0, keepdims=True)
    col = jnp.sum(jnp.where(same & (second < first), 1.0, 0.0), axis=1, keepdims=True)
    return ids_row, row, ids, col


def crossing_kernel(
    capacity,
    xf_ref, rf_ref, gf_ref, xb_ref, gb_ref, rb_ref, gtb_ref, wg_hbm, wu_hbm, wd_hbm,
    of_ref, ob_ref,
    wg, wu, wd, ids_out, ids_in, raw, tok, far, mine, theirs, pbuf, csum, peer_in, comb, ret, dense, dense_in, outb,
    w_sem, ids_sem, raw_send, raw_recv, s1_sem, s2_sem, fwd_sem, relay_sem, tok_sem,
    pb_send, pb_recv, cs_send, cs_recv, ret_send, ret_recv, de_send, de_recv, out_send, out_recv,
):
    rows_here, width = xf_ref.shape[1:]
    me = lax.axis_index("expert")
    pipe = lax.axis_index("pipe")
    n_pipe = lax.axis_size("pipe")
    z, core = lax.div(me, 2), lax.rem(me, 2)
    expert = lax.div(z, 2)
    outer = lax.rem(lax.div(z + 1, 2) + 1, 2)
    peer = me + 2 - 4 * lax.rem(z, 2)
    partner = me + 1 - 2 * core
    across = 2 * (2 - expert) + core
    is_inner, is_outer = outer == 0, outer == 1
    has_next, has_prev = pipe < n_pipe - 1, pipe > 0

    weight_copies = [
        pltpu.make_async_copy(src.at[0], dst, w_sem.at[i])
        for i, (src, dst) in enumerate(((wg_hbm, wg), (wu_hbm, wu), (wd_hbm, wd)))
    ]
    for copy in weight_copies:
        copy.start()

    barrier = pltpu.get_barrier_semaphore()
    for other in (partner, peer):
        pl.semaphore_signal(barrier, inc=1, device_id={"expert": other}, device_id_type=MESH)

    @pl.when(is_inner)
    def _():
        pl.semaphore_signal(barrier, inc=1, device_id={"expert": across}, device_id_type=MESH)

    @pl.when(has_next)
    def _():
        pl.semaphore_signal(barrier, inc=1, device_id={"pipe": pipe + 1}, device_id_type=MESH)

    @pl.when(has_prev)
    def _():
        pl.semaphore_signal(barrier, inc=1, device_id={"pipe": pipe - 1}, device_id_type=MESH)

    def remote(src, dst, send, recv, axis, index):
        return pltpu.make_async_remote_copy(
            src_ref=src, dst_ref=dst, send_sem=send, recv_sem=recv,
            device_id={axis: index}, device_id_type=MESH,
        )

    def columns(body):
        def step(i, carry):
            body(pl.ds(pl.multiple_of(i * COLS, COLS), COLS))
            return carry

        lax.fori_loop(0, width // COLS, step, 0)

    mine_id = expert.astype(F32)
    other_id = 1.0 - mine_id
    inputs = (xf_ref, xb_ref, gb_ref)

    def pickers(routes):
        ids_row, row, _, _ = places_rows(routes)
        slot = lax.broadcasted_iota(jnp.int32, (capacity, routes.shape[1]), 0).astype(F32)
        hit = slot == row
        return (
            jnp.where(hit & (ids_row == mine_id), 1.0, 0.0).astype(BF16),
            jnp.where(hit & (ids_row == other_id), 1.0, 0.0).astype(BF16),
        )

    def placers(routes):
        _, _, ids, col = places_rows(routes)
        slot = lax.broadcasted_iota(jnp.int32, (routes.shape[1], capacity), 1).astype(F32)
        hit = slot == col
        return (
            jnp.where(hit & (ids == mine_id), 1.0, 0.0).astype(BF16),
            jnp.where(hit & (ids == other_id), 1.0, 0.0).astype(BF16),
        )

    def near_ids(m):
        return ids_in[m:m + 1, :rows_here]

    def pick(a, k, source, picks):
        def body(at):
            block = source(at)
            tok[a, k, 0, :, at] = jnp.dot(picks[0], block, preferred_element_type=F32).astype(BF16)

            @pl.when(is_inner)
            def _():
                far[a, k, :, at] = jnp.dot(picks[1], block, preferred_element_type=F32).astype(BF16)

        columns(body)

    def dispatch(a, picks):
        pick(a, 0, lambda at: inputs[a][0, :, at], picks)

    def to_near():
        return remote(ids_out, ids_in, ids_sem.at[0], ids_sem.at[1], "expert", peer)

    def to_raw(a):
        return remote(inputs[a].at[0], raw.at[a], raw_send.at[a], raw_recv.at[a], "expert", peer)

    def to_peer(a):
        return remote(tok.at[a, 0, 0], tok.at[a, 1, 0], s1_sem.at[a], tok_sem.at[a, 1, 0], "expert", peer)

    def to_across(a, k):
        return remote(
            far.at[a, k], tok.at[a, k + 2, 0], s2_sem.at[a, k], tok_sem.at[a, k + 2, 0], "expert", across
        )

    def to_partner(a, k):
        return remote(
            tok.at[a, k, 0], tok.at[a, k, 1], fwd_sem.at[a, k], tok_sem.at[a, k, 1], "expert", partner
        )

    def relay(a, k):
        return remote(
            tok.at[a, k, 0], tok.at[a, k, 0], relay_sem.at[a, k - 2], tok_sem.at[a, k, 0], "expert", peer
        )

    def half(m, k):
        return remote(theirs.at[m, k], pbuf.at[m, k], pb_send.at[m, k], pb_recv.at[m, k], "expert", partner)

    parts = range(width // COLS)

    def part(h):
        return pl.ds(h * COLS, COLS)

    def to_combiner(m, k, h):
        return remote(
            csum.at[m, k, :, part(h)], peer_in.at[m, k - 1, :, part(h)],
            cs_send.at[m, k - 1, h], cs_recv.at[m, k - 1, h], "expert", peer,
        )

    def to_home(m, k, h):
        return remote(
            comb.at[m, k - 2, :, part(h)], ret.at[m, k - 2, :, part(h)],
            ret_send.at[m, k - 2, h], ret_recv.at[m, k - 2, h], "expert", across,
        )

    def to_outer(m, h):
        return remote(
            dense.at[m, :, part(h)], dense_in.at[m, :, part(h)],
            de_send.at[m, h], de_recv.at[m, h], "expert", peer,
        )

    def to_section(m, h):
        dst = of_ref if m == 0 else ob_ref
        other = pipe + 1 if m == 0 else pipe - 1
        return remote(
            outb.at[m, :, part(h)], dst.at[0, :, part(h)],
            out_send.at[m, h], out_recv.at[m, h], "pipe", other,
        )

    def near(a):
        @pl.when(is_inner)
        def _():
            if a == 0:
                to_near().wait_recv()
            to_raw(a).wait_recv()
            pick(a, 1, lambda at: raw[a, :, at], pickers(near_ids(min(a, 1))))
            to_across(a, 1).start()
            to_partner(a, 1).start()

    def given(a):
        @pl.when(is_outer)
        def _():
            to_peer(a).wait_recv()
            to_partner(a, 1).start()

    def arrive(a, k):
        relay(a, k).wait_recv()

        @pl.when(is_inner)
        def _():
            relay(a, k).start()

        to_partner(a, k).start()

    def rows_of(a, k):
        to_partner(a, k).wait_recv()
        return tok[a, k].reshape(2 * capacity, width)

    def keep(m, k, at, value):
        value = value.astype(BF16)
        mine[m, k, :, at] = value[:capacity]
        theirs[m, k, :, at] = value[capacity:]

    contract = (((1,), (1,)), ((), ()))

    def compute_fwd(k):
        rows = rows_of(0, k)
        pre_gate = jnp.dot(rows, wg[...], preferred_element_type=F32)
        pre_up = jnp.dot(rows, wu[...], preferred_element_type=F32)
        hidden = (pre_gate * jax.nn.sigmoid(pre_gate) * pre_up).astype(BF16)
        columns(lambda at: keep(0, k, at, jnp.dot(hidden, wd[:, at], preferred_element_type=F32)))
        half(0, k).start()

    def compute_bwd(k):
        rows_x, rows_g = rows_of(1, k), rows_of(2, k)
        pre_gate = jnp.dot(rows_x, wg[...], preferred_element_type=F32)
        pre_up = jnp.dot(rows_x, wu[...], preferred_element_type=F32)
        act_grad = lax.dot_general(rows_g, wd[...], contract, preferred_element_type=F32)
        sig = jax.nn.sigmoid(pre_gate)
        gate_grad = (act_grad * pre_up * sig * (1.0 + pre_gate * (1.0 - sig))).astype(BF16)
        up_grad = (act_grad * pre_gate * sig).astype(BF16)

        def body(at):
            total = lax.dot_general(gate_grad, wg[at, :], contract, preferred_element_type=F32)
            total = total + lax.dot_general(up_grad, wu[at, :], contract, preferred_element_type=F32)
            keep(1, k, at, total)

        columns(body)
        half(1, k).start()

    def reduce_chip(m, k):
        half(m, k).wait_recv()
        for h in parts:
            at = part(h)
            csum[m, k, :, at] = (mine[m, k, :, at].astype(F32) + pbuf[m, k, :, at].astype(F32)).astype(BF16)
            if k >= 1:
                @pl.when(is_outer)
                def _():
                    to_combiner(m, k, h).start()

    def combine(m, k):
        @pl.when(is_inner)
        def _():
            for h in parts:
                at = part(h)
                to_combiner(m, k, h).wait_recv()
                comb[m, k - 2, :, at] = (
                    csum[m, k, :, at].astype(F32) + peer_in[m, k - 1, :, at].astype(F32)
                ).astype(BF16)
                to_home(m, k, h).start()

    def serve(m):
        @pl.when(is_inner)
        def _():
            pick_mine, pick_other = placers(near_ids(m))
            for h in parts:
                at = part(h)
                to_home(m, 3, h).wait_recv()
                total = jnp.dot(pick_mine, csum[m, 1, :, at], preferred_element_type=F32)
                total = total + jnp.dot(pick_other, ret[m, 1, :, at], preferred_element_type=F32)
                dense[m, :, at] = total.astype(BF16)
                to_outer(m, h).start()

    def finish(m):
        pick_mine, pick_other = placers((rf_ref if m == 0 else rb_ref)[...].astype(F32))
        gates = to_column((gf_ref if m == 0 else gtb_ref)[...])
        base = xf_ref if m == 0 else gb_ref

        def close(h, total):
            at = part(h)
            outb[m, :, at] = (base[0, :, at].astype(F32) + gates * total).astype(BF16)

            @pl.when(has_next if m == 0 else has_prev)
            def _():
                to_section(m, h).start()

        @pl.when(is_inner)
        def _():
            for h in parts:
                at = part(h)
                to_combiner(m, 1, h).wait_recv()
                to_home(m, 2, h).wait_recv()
                total = jnp.dot(pick_mine, csum[m, 0, :, at], preferred_element_type=F32)
                total = total + jnp.dot(pick_mine, peer_in[m, 0, :, at], preferred_element_type=F32)
                close(h, total + jnp.dot(pick_other, ret[m, 0, :, at], preferred_element_type=F32))

        @pl.when(is_outer)
        def _():
            for h in parts:
                at = part(h)
                total = jnp.dot(pick_mine, csum[m, 0, :, at], preferred_element_type=F32)
                to_outer(m, h).wait_recv()
                close(h, total + dense_in[m, :, at].astype(F32))

    ids_out[...] = jnp.zeros_like(ids_out)
    ids_out[0:1, :rows_here] = rf_ref[...].astype(F32)
    ids_out[1:2, :rows_here] = rb_ref[...].astype(F32)
    picks_f = pickers(rf_ref[...].astype(F32))
    picks_b = pickers(rb_ref[...].astype(F32))
    dispatch(0, picks_f)
    ends = lax.div(n_pipe - 1 - pipe + n_pipe - 2, n_pipe - 1) + lax.div(pipe + n_pipe - 2, n_pipe - 1)
    pl.semaphore_wait(barrier, 3 - outer + ends)

    @pl.when(is_outer)
    def _():
        to_near().start()
        for a in range(3):
            to_raw(a).start()

    @pl.when(is_inner)
    def _():
        to_peer(0).start()
        to_across(0, 0).start()

    to_partner(0, 0).start()
    dispatch(1, picks_b)

    @pl.when(is_inner)
    def _():
        to_peer(1).start()
        to_across(1, 0).start()

    to_partner(1, 0).start()
    dispatch(2, picks_b)

    @pl.when(is_inner)
    def _():
        to_across(2, 0).start()

    to_partner(2, 0).start()

    @pl.when(pipe == 0)
    def _():
        of_ref[...] = jnp.zeros_like(of_ref)

    @pl.when(pipe == n_pipe - 1)
    def _():
        ob_ref[...] = jnp.zeros_like(ob_ref)

    for copy in weight_copies:
        copy.wait()

    compute_fwd(0)
    near(0)
    given(0)
    compute_fwd(1)
    arrive(0, 2)
    compute_bwd(0)
    reduce_chip(0, 1)
    arrive(1, 2)
    compute_fwd(2)
    reduce_chip(0, 2)
    near(1)
    given(1)
    arrive(2, 2)
    near(2)
    compute_bwd(2)
    reduce_chip(1, 2)
    arrive(0, 3)
    compute_fwd(3)
    reduce_chip(0, 3)
    arrive(1, 3)
    arrive(2, 3)

    @pl.when(is_inner)
    def _():
        to_peer(2).start()

    compute_bwd(3)
    reduce_chip(1, 3)
    reduce_chip(0, 0)
    reduce_chip(1, 0)
    combine(0, 2)
    combine(1, 2)
    combine(0, 3)
    given(2)
    compute_bwd(1)
    reduce_chip(1, 1)
    serve(0)
    finish(0)
    combine(1, 3)
    serve(1)
    finish(1)

    for a in range(3):
        for k in range(4):
            to_partner(a, k).wait_send()

    for m in range(2):
        for k in range(4):
            half(m, k).wait_send()

    @pl.when(is_inner)
    def _():
        for a in range(3):
            to_peer(a).wait_send()
            for k in range(2):
                to_across(a, k).wait_send()
                relay(a, k + 2).wait_send()
        for m in range(2):
            for h in parts:
                to_outer(m, h).wait_send()
                for k in (2, 3):
                    to_home(m, k, h).wait_send()

    @pl.when(is_outer)
    def _():
        to_near().wait_send()
        for a in range(3):
            to_raw(a).wait_send()
        for m in range(2):
            for k in (1, 2, 3):
                for h in parts:
                    to_combiner(m, k, h).wait_send()

    @pl.when(has_next)
    def _():
        for h in parts:
            to_section(0, h).wait_send()
            to_section(1, h).wait_recv()

    @pl.when(has_prev)
    def _():
        for h in parts:
            to_section(0, h).wait_recv()
            to_section(1, h).wait_send()


def hand_on_kernel(a_ref, b_ref, c_ref, d_ref):
    c_ref[...] = a_ref[...]
    d_ref[...] = b_ref[...]


def handed_on(a, b):
    vmem = pl.BlockSpec(memory_space=pltpu.VMEM)
    return pl.pallas_call(
        hand_on_kernel,
        out_shape=(jax.ShapeDtypeStruct(a.shape, a.dtype), jax.ShapeDtypeStruct(b.shape, b.dtype)),
        in_specs=[vmem, vmem],
        out_specs=(vmem, vmem),
    )(a, b)


def crossing_body(xf, rf, gf, xb, gb, rb, gtb, wg, wu, wd):
    _, rows, width = xf.shape
    capacity = min(rows, rows * TOPK * 3 // 4)
    hid = wg.shape[2]
    parts = width // COLS
    vmem = pl.BlockSpec(memory_space=pltpu.VMEM)
    hbm = pl.BlockSpec(memory_space=pl.ANY)
    block = (capacity, width)
    dma = pltpu.SemaphoreType.DMA
    out = jax.ShapeDtypeStruct(xf.shape, BF16)
    arrived = pl.pallas_call(
        functools.partial(crossing_kernel, capacity),
        out_shape=(out, out),
        in_specs=[vmem] * 7 + [hbm] * 3,
        out_specs=(vmem, vmem),
        scratch_shapes=[
            pltpu.VMEM((width, hid), BF16),
            pltpu.VMEM((width, hid), BF16),
            pltpu.VMEM((hid, width), BF16),
            pltpu.VMEM((8, max(rows, 128)), F32),
            pltpu.VMEM((8, max(rows, 128)), F32),
            pltpu.VMEM((3, rows, width), BF16),
            pltpu.VMEM((3, 4, 2) + block, BF16),
            pltpu.VMEM((3, 2) + block, BF16),
            pltpu.VMEM((2, 4) + block, BF16),
            pltpu.VMEM((2, 4) + block, BF16),
            pltpu.VMEM((2, 4) + block, BF16),
            pltpu.VMEM((2, 4) + block, BF16),
            pltpu.VMEM((2, 3) + block, BF16),
            pltpu.VMEM((2, 2) + block, BF16),
            pltpu.VMEM((2, 2) + block, BF16),
            pltpu.VMEM((2, rows, width), BF16),
            pltpu.VMEM((2, rows, width), BF16),
            pltpu.VMEM((2, rows, width), BF16),
            dma((3,)), dma((2,)), dma((3,)), dma((3,)), dma((3,)), dma((3, 2)), dma((3, 4)), dma((3, 2)), dma((3, 4, 2)),
            dma((2, 4)), dma((2, 4)), dma((2, 3, parts)), dma((2, 3, parts)), dma((2, 2, parts)), dma((2, 2, parts)),
            dma((2, parts)), dma((2, parts)), dma((2, parts)), dma((2, parts)),
        ],
        compiler_params=pltpu.CompilerParams(
            collective_id=0, has_side_effects=True, vmem_limit_bytes=60 * 1024 * 1024
        ),
    )(xf, rf.reshape(1, rows), gf.reshape(1, rows), xb, gb, rb.reshape(1, rows), gtb.reshape(1, rows), wg, wu, wd)
    return handed_on(*arrived)


def shifted(block, axis, distance):
    devices = range(lax.axis_size(axis))
    route = [(i - distance, i) for i in devices if i - distance in devices]
    return lax.ppermute(block, axis, route)


def slot_table(routes, experts, capacity):
    flat_ids = routes.reshape(-1)
    number = jnp.arange(flat_ids.shape[0], dtype=jnp.int32)
    same = flat_ids[:, None] == flat_ids[None, :]
    before = number[None, :] < number[:, None]
    places = jnp.sum((same & before).astype(jnp.int32), axis=1)
    return (flat_ids * capacity + places).reshape(routes.shape)


def dispatch_rows(tokens, slot_ids, experts, capacity):
    numbered = jnp.arange(experts * capacity, dtype=jnp.int32)
    picker = jnp.any(slot_ids[None, :, :] == numbered[:, None, None], axis=2).astype(jnp.bfloat16)
    filled = jnp.dot(picker, tokens, preferred_element_type=jnp.float32).astype(jnp.bfloat16)
    return jnp.repeat(filled.reshape(experts, capacity, tokens.shape[1]), HSPLIT, axis=0)


def combine_rows(base, returned, slot_ids, weights, experts, capacity):
    width = base.shape[1]
    summed = jnp.sum(returned.astype(jnp.float32).reshape(experts, HSPLIT, capacity, width), axis=1)
    summed = summed.reshape(experts * capacity, width)
    numbered = jnp.arange(experts * capacity, dtype=jnp.int32)
    mixing = jnp.sum(
        weights[:, :, None] * (slot_ids[:, :, None] == numbered[None, None, :]).astype(jnp.float32),
        axis=1,
    )
    total = base.astype(jnp.float32) + jnp.dot(mixing, summed, precision=lax.Precision.HIGHEST)
    return total.astype(jnp.bfloat16)


def forward_rows(received, gate_cols, up_cols, down_rows):
    in_shape = received.shape
    row_block = received.reshape(-1, in_shape[-1])
    pre_gate = jnp.dot(row_block, gate_cols, preferred_element_type=jnp.float32)
    pre_up = jnp.dot(row_block, up_cols, preferred_element_type=jnp.float32)
    hidden = (jax.nn.silu(pre_gate) * pre_up).astype(jnp.bfloat16)
    result = jnp.dot(hidden, down_rows, preferred_element_type=jnp.float32).astype(jnp.bfloat16)
    return result.reshape(in_shape)


def backward_rows(received_x, received_g, gate_cols, up_cols, down_rows):
    in_shape = received_x.shape
    rows_x = received_x.reshape(-1, in_shape[-1])
    rows_g = received_g.reshape(-1, in_shape[-1])
    contract = (((1,), (1,)), ((), ()))
    pre_gate = jnp.dot(rows_x, gate_cols, preferred_element_type=jnp.float32)
    pre_up = jnp.dot(rows_x, up_cols, preferred_element_type=jnp.float32)
    act_grad = lax.dot_general(rows_g, down_rows, contract, preferred_element_type=jnp.float32)
    sigmoid_gate = jax.nn.sigmoid(pre_gate)
    gate_grad = (act_grad * pre_up * sigmoid_gate * (1.0 + pre_gate * (1.0 - sigmoid_gate))).astype(
        jnp.bfloat16
    )
    up_grad = (act_grad * pre_gate * sigmoid_gate).astype(jnp.bfloat16)
    back_rows = lax.dot_general(gate_grad, gate_cols, contract, preferred_element_type=jnp.float32)
    back_rows = back_rows + lax.dot_general(
        up_grad, up_cols, contract, preferred_element_type=jnp.float32
    )
    return back_rows.astype(jnp.bfloat16).reshape(in_shape)


def body(
    x_fwd,
    routes_fwd,
    gates_fwd,
    x_bwd,
    grad_bwd,
    routes_bwd,
    gates_bwd,
    gate_proj,
    up_proj,
    down_proj,
):
    tokens_a = x_fwd[0]
    tokens_b = x_bwd[0]
    grads_b = grad_bwd[0]
    gate_cols = gate_proj[0]
    up_cols = up_proj[0]
    down_rows = down_proj[0]
    experts = lax.axis_size("expert") // HSPLIT
    tok_rows = tokens_a.shape[0]
    capacity = min(tok_rows, tok_rows * TOPK * 3 // (2 * experts))
    slots_a = slot_table(routes_fwd[0], experts, capacity)
    slots_b = slot_table(routes_bwd[0], experts, capacity)
    send_a = dispatch_rows(tokens_a, slots_a, experts, capacity)
    send_x = dispatch_rows(tokens_b, slots_b, experts, capacity)
    send_g = dispatch_rows(grads_b, slots_b, experts, capacity)
    back_a = lax.all_to_all(
        forward_rows(
            lax.all_to_all(send_a, "expert", split_axis=0, concat_axis=0, tiled=True),
            gate_cols,
            up_cols,
            down_rows,
        ),
        "expert",
        split_axis=0,
        concat_axis=0,
        tiled=True,
    )
    back_b = lax.all_to_all(
        backward_rows(
            lax.all_to_all(send_x, "expert", split_axis=0, concat_axis=0, tiled=True),
            lax.all_to_all(send_g, "expert", split_axis=0, concat_axis=0, tiled=True),
            gate_cols,
            up_cols,
            down_rows,
        ),
        "expert",
        split_axis=0,
        concat_axis=0,
        tiled=True,
    )
    out_fwd = combine_rows(tokens_a, back_a, slots_a, gates_fwd[0], experts, capacity)
    out_bwd = combine_rows(grads_b, back_b, slots_b, gates_bwd[0], experts, capacity)
    fwd_next = shifted(out_fwd, "pipe", 1)
    bwd_next = shifted(out_bwd, "pipe", -1)
    return (fwd_next[None], bwd_next[None])


def solution(mesh):
    in_specs = (
        P("pipe", "expert", None),
        P("pipe", "expert", None),
        P("pipe", "expert", None),
        P("pipe", "expert", None),
        P("pipe", "expert", None),
        P("pipe", "expert", None),
        P("pipe", "expert", None),
        P("pipe", None, "expert"),
        P("pipe", None, "expert"),
        P("pipe", "expert", None),
    )
    out_specs = (P("pipe", "expert", None), P("pipe", "expert", None))
    two_experts = mesh.shape["expert"] == 2 * HSPLIT
    chosen = crossing_body if two_experts else body
    return jax.shard_map(chosen, mesh=mesh, in_specs=in_specs, out_specs=out_specs, check_vma=False)
```

```python
import functools
import jax
import jax.numpy as jnp
from jax import lax
from jax.sharding import PartitionSpec as P
from jax.experimental import pallas as pl
from jax.experimental.pallas import tpu as pltpu

HSPLIT = 4
TOPK = 1
MESH = pl.DeviceIdType.MESH
F32, BF16 = jnp.float32, jnp.bfloat16
COLS = 896


def to_column(row):
    count = row.shape[1]
    first = lax.broadcasted_iota(jnp.int32, (count, count), 0)
    second = lax.broadcasted_iota(jnp.int32, (count, count), 1)
    wide = jnp.broadcast_to(row, (count, count))
    return jnp.sum(jnp.where(first == second, wide, 0.0), axis=1, keepdims=True)


def places_rows(ids_row):
    count = ids_row.shape[1]
    first = lax.broadcasted_iota(jnp.int32, (count, count), 0)
    second = lax.broadcasted_iota(jnp.int32, (count, count), 1)
    ids = to_column(ids_row)
    same = ids == ids_row
    row = jnp.sum(jnp.where(same & (first < second), 1.0, 0.0), axis=0, keepdims=True)
    col = jnp.sum(jnp.where(same & (second < first), 1.0, 0.0), axis=1, keepdims=True)
    return ids_row, row, ids, col


def crossing_kernel(
    capacity,
    xf_ref, rf_ref, gf_ref, xb_ref, gb_ref, rb_ref, gtb_ref, wg_hbm, wu_hbm, wd_hbm,
    of_ref, ob_ref,
    wg, wu, wd, ids_out, ids_in, raw, tok, far, mine, theirs, pbuf, csum, peer_own, peer_in, comb, ret, dense, dense_in, outb,
    w_sem, ids_sem, raw_send, raw_recv, s1_sem, s2_sem, fwd_sem, relay_sem, tok_sem,
    pb_send, pb_recv, own_send, own_recv, cs_send, cs_recv, ret_send, ret_recv, de_send, de_recv, out_send, out_recv,
):
    rows_here, width = xf_ref.shape[1:]
    me = lax.axis_index("expert")
    pipe = lax.axis_index("pipe")
    n_pipe = lax.axis_size("pipe")
    z, core = lax.div(me, 2), lax.rem(me, 2)
    expert = lax.div(z, 2)
    outer = lax.rem(lax.div(z + 1, 2) + 1, 2)
    peer = me + 2 - 4 * lax.rem(z, 2)
    partner = me + 1 - 2 * core
    across = 2 * (2 - expert) + core
    is_inner, is_outer = outer == 0, outer == 1
    has_next, has_prev = pipe < n_pipe - 1, pipe > 0

    weight_copies = [
        pltpu.make_async_copy(src.at[0], dst, w_sem.at[i])
        for i, (src, dst) in enumerate(((wg_hbm, wg), (wu_hbm, wu), (wd_hbm, wd)))
    ]
    for copy in weight_copies:
        copy.start()

    barrier = pltpu.get_barrier_semaphore()
    for other in (partner, peer):
        pl.semaphore_signal(barrier, inc=1, device_id={"expert": other}, device_id_type=MESH)

    def greet(other_pipe, other):
        pl.semaphore_signal(
            barrier, inc=1, device_id={"pipe": other_pipe, "expert": other}, device_id_type=MESH
        )

    @pl.when(is_inner)
    def _():
        greet(pipe, across)

    @pl.when(has_next)
    def _():
        greet(pipe + 1, (1 - outer) * me + outer * peer)

    @pl.when(has_prev)
    def _():
        greet(pipe - 1, me)

    def remote(src, dst, send, recv, axis, index):
        return pltpu.make_async_remote_copy(
            src_ref=src, dst_ref=dst, send_sem=send, recv_sem=recv,
            device_id={axis: index}, device_id_type=MESH,
        )

    def columns(body):
        def step(i, carry):
            body(pl.ds(pl.multiple_of(i * COLS, COLS), COLS))
            return carry

        lax.fori_loop(0, width // COLS, step, 0)

    mine_id = expert.astype(F32)
    other_id = 1.0 - mine_id
    inputs = (xf_ref, xb_ref, gb_ref)

    def pickers(routes):
        ids_row, row, _, _ = places_rows(routes)
        slot = lax.broadcasted_iota(jnp.int32, (capacity, routes.shape[1]), 0).astype(F32)
        hit = slot == row
        return (
            jnp.where(hit & (ids_row == mine_id), 1.0, 0.0).astype(BF16),
            jnp.where(hit & (ids_row == other_id), 1.0, 0.0).astype(BF16),
        )

    def placers(routes):
        _, _, ids, col = places_rows(routes)
        slot = lax.broadcasted_iota(jnp.int32, (routes.shape[1], capacity), 1).astype(F32)
        hit = slot == col
        return (
            jnp.where(hit & (ids == mine_id), 1.0, 0.0).astype(BF16),
            jnp.where(hit & (ids == other_id), 1.0, 0.0).astype(BF16),
        )

    def near_ids(m):
        return ids_in[m:m + 1, :rows_here]

    def near_gates(m):
        return ids_in[m + 2:m + 3, :rows_here]

    def pick(a, k, source, picks):
        def body(at):
            block = source(at)
            tok[a, k, 0, :, at] = jnp.dot(picks[0], block, preferred_element_type=F32).astype(BF16)

            @pl.when(is_inner)
            def _():
                far[a, k, :, at] = jnp.dot(picks[1], block, preferred_element_type=F32).astype(BF16)

        columns(body)

    def dispatch(a, picks):
        pick(a, 0, lambda at: inputs[a][0, :, at], picks)

    def to_near():
        return remote(ids_out, ids_in, ids_sem.at[0], ids_sem.at[1], "expert", peer)

    def to_raw(a):
        return remote(inputs[a].at[0], raw.at[a], raw_send.at[a], raw_recv.at[a], "expert", peer)

    def to_peer(a):
        return remote(tok.at[a, 0, 0], tok.at[a, 1, 0], s1_sem.at[a], tok_sem.at[a, 1, 0], "expert", peer)

    def to_across(a, k):
        return remote(
            far.at[a, k], tok.at[a, k + 2, 0], s2_sem.at[a, k], tok_sem.at[a, k + 2, 0], "expert", across
        )

    def to_partner(a, k):
        return remote(
            tok.at[a, k, 0], tok.at[a, k, 1], fwd_sem.at[a, k], tok_sem.at[a, k, 1], "expert", partner
        )

    def relay(a, k):
        return remote(
            tok.at[a, k, 0], tok.at[a, k, 0], relay_sem.at[a, k - 2], tok_sem.at[a, k, 0], "expert", peer
        )

    def half(m, k):
        return remote(theirs.at[m, k], pbuf.at[m, k], pb_send.at[m, k], pb_recv.at[m, k], "expert", partner)

    parts = range(width // COLS)

    def part(h):
        return pl.ds(h * COLS, COLS)

    def to_combiner(m, k, h):
        return remote(
            csum.at[m, k, :, part(h)], peer_in.at[m, k - 1, :, part(h)],
            cs_send.at[m, k - 1, h], cs_recv.at[m, k - 1, h], "expert", peer,
        )

    def to_finisher(h):
        return remote(
            csum.at[1, 0, :, part(h)], peer_own.at[:, part(h)], own_send.at[h], own_recv.at[h], "expert", peer
        )

    def to_home(m, k, h):
        return remote(
            comb.at[m, k - 2, :, part(h)], ret.at[m, k - 2, :, part(h)],
            ret_send.at[m, k - 2, h], ret_recv.at[m, k - 2, h], "expert", across,
        )

    def to_outer(h):
        return remote(
            dense.at[0, :, part(h)], dense_in.at[:, part(h)], de_send.at[0, h], de_recv.at[h], "expert", peer
        )

    def to_outer_section(h):
        return pltpu.make_async_remote_copy(
            src_ref=dense.at[1, :, part(h)], dst_ref=ob_ref.at[0, :, part(h)],
            send_sem=de_send.at[1, h], recv_sem=out_recv.at[1, h],
            device_id={"pipe": pipe - 1, "expert": peer}, device_id_type=MESH,
        )

    def to_section(m, h):
        dst = of_ref if m == 0 else ob_ref
        other = pipe + 1 if m == 0 else pipe - 1
        return remote(
            outb.at[m, :, part(h)], dst.at[0, :, part(h)],
            out_send.at[m, h], out_recv.at[m, h], "pipe", other,
        )

    def near(a):
        if a == 0:
            to_near().wait_recv()
        to_raw(a).wait_recv()
        pick(a, 1, lambda at: raw[a, :, at], pickers(near_ids(min(a, 1))))
        to_across(a, 1).start()
        to_partner(a, 1).start()

    def pass_on(a, k):
        relay(a, k).wait_recv()
        relay(a, k).start()
        to_partner(a, k).start()

    def take(a, k):
        (to_peer(a) if k == 1 else relay(a, k)).wait_recv()
        to_partner(a, k).start()

    def rows_of(a, k):
        to_partner(a, k).wait_recv()
        return tok[a, k].reshape(2 * capacity, width)

    def keep(m, k, at, value):
        value = value.astype(BF16)
        mine[m, k, :, at] = value[:capacity]
        theirs[m, k, :, at] = value[capacity:]

    contract = (((1,), (1,)), ((), ()))

    def compute_fwd(k):
        rows = rows_of(0, k)
        pre_gate = jnp.dot(rows, wg[...], preferred_element_type=F32)
        pre_up = jnp.dot(rows, wu[...], preferred_element_type=F32)
        hidden = (pre_gate * jax.nn.sigmoid(pre_gate) * pre_up).astype(BF16)
        columns(lambda at: keep(0, k, at, jnp.dot(hidden, wd[:, at], preferred_element_type=F32)))
        half(0, k).start()

    def compute_bwd(k):
        rows_x, rows_g = rows_of(1, k), rows_of(2, k)
        pre_gate = jnp.dot(rows_x, wg[...], preferred_element_type=F32)
        pre_up = jnp.dot(rows_x, wu[...], preferred_element_type=F32)
        act_grad = lax.dot_general(rows_g, wd[...], contract, preferred_element_type=F32)
        sig = jax.nn.sigmoid(pre_gate)
        gate_grad = (act_grad * pre_up * sig * (1.0 + pre_gate * (1.0 - sig))).astype(BF16)
        up_grad = (act_grad * pre_gate * sig).astype(BF16)

        def body(at):
            total = lax.dot_general(gate_grad, wg[at, :], contract, preferred_element_type=F32)
            total = total + lax.dot_general(up_grad, wu[at, :], contract, preferred_element_type=F32)
            keep(1, k, at, total)

        columns(body)
        half(1, k).start()

    def chip_sum(m, k, at):
        csum[m, k, :, at] = (mine[m, k, :, at].astype(F32) + pbuf[m, k, :, at].astype(F32)).astype(BF16)

    def hold(m, k):
        half(m, k).wait_recv()
        for h in parts:
            chip_sum(m, k, part(h))

    def give(m, k):
        half(m, k).wait_recv()
        for h in parts:
            chip_sum(m, k, part(h))
            if k >= 1:
                to_combiner(m, k, h).start()
            elif m == 1:
                to_finisher(h).start()

    def combine(m, k):
        for h in parts:
            at = part(h)
            to_combiner(m, k, h).wait_recv()
            comb[m, k - 2, :, at] = (
                csum[m, k, :, at].astype(F32) + peer_in[m, k - 1, :, at].astype(F32)
            ).astype(BF16)
            to_home(m, k, h).start()

    def serve(m):
        pick_mine, pick_other = placers(near_ids(m))
        gates = to_column(near_gates(m))
        for h in parts:
            at = part(h)
            to_home(m, 3, h).wait_recv()
            total = jnp.dot(pick_mine, csum[m, 1, :, at], preferred_element_type=F32)
            total = total + jnp.dot(pick_other, ret[m, 1, :, at], preferred_element_type=F32)
            if m == 0:
                dense[m, :, at] = total.astype(BF16)
                to_outer(h).start()
            else:
                to_finisher(h).wait_recv()
                total = total + jnp.dot(pick_mine, peer_own[:, at], preferred_element_type=F32)
                dense[m, :, at] = (raw[2, :, at].astype(F32) + gates * total).astype(BF16)

                @pl.when(has_prev)
                def _():
                    to_outer_section(h).start()

    def tables(m):
        return (
            *placers((rf_ref if m == 0 else rb_ref)[...].astype(F32)),
            to_column((gf_ref if m == 0 else gtb_ref)[...]),
        )

    def close(m, h, gates, total):
        at = part(h)
        base = xf_ref if m == 0 else gb_ref
        outb[m, :, at] = (base[0, :, at].astype(F32) + gates * total).astype(BF16)

        @pl.when(has_next if m == 0 else has_prev)
        def _():
            to_section(m, h).start()

    def finish(m):
        pick_mine, pick_other, gates = tables(m)
        for h in parts:
            at = part(h)
            to_combiner(m, 1, h).wait_recv()
            to_home(m, 2, h).wait_recv()
            total = jnp.dot(pick_mine, csum[m, 0, :, at], preferred_element_type=F32)
            total = total + jnp.dot(pick_mine, peer_in[m, 0, :, at], preferred_element_type=F32)
            close(m, h, gates, total + jnp.dot(pick_other, ret[m, 0, :, at], preferred_element_type=F32))

    def finish_outer():
        pick_mine, _, gates = tables(0)
        for h in parts:
            at = part(h)
            total = jnp.dot(pick_mine, csum[0, 0, :, at], preferred_element_type=F32)
            to_outer(h).wait_recv()
            close(0, h, gates, total + dense_in[:, at].astype(F32))

    ids_out[...] = jnp.zeros_like(ids_out)
    ids_out[0:1, :rows_here] = rf_ref[...].astype(F32)
    ids_out[1:2, :rows_here] = rb_ref[...].astype(F32)
    ids_out[2:3, :rows_here] = gf_ref[...]
    ids_out[3:4, :rows_here] = gtb_ref[...]
    picks_f = pickers(rf_ref[...].astype(F32))
    picks_b = pickers(rb_ref[...].astype(F32))
    dispatch(0, picks_f)
    nexts = lax.div(n_pipe - 1 - pipe + n_pipe - 2, n_pipe - 1)
    prevs = lax.div(pipe + n_pipe - 2, n_pipe - 1)
    pl.semaphore_wait(barrier, 3 - outer + nexts + 2 * (1 - outer) * prevs)

    @pl.when(is_outer)
    def _():
        to_near().start()
        for a in range(3):
            to_raw(a).start()

    @pl.when(is_inner)
    def _():
        to_peer(0).start()
        to_across(0, 0).start()

    to_partner(0, 0).start()
    dispatch(1, picks_b)

    @pl.when(is_inner)
    def _():
        to_peer(1).start()

    to_partner(1, 0).start()
    dispatch(2, picks_b)

    to_partner(2, 0).start()

    @pl.when(pipe == 0)
    def _():
        of_ref[...] = jnp.zeros_like(of_ref)

    @pl.when(pipe == n_pipe - 1)
    def _():
        ob_ref[...] = jnp.zeros_like(ob_ref)

    for copy in weight_copies:
        copy.wait()

    @pl.when(is_inner)
    def _():
        to_across(1, 0).start()
        near(0)
        pass_on(0, 2)

    @pl.when(is_outer)
    def _():
        take(0, 2)

    compute_fwd(0)

    @pl.when(is_outer)
    def _():
        take(0, 1)

    compute_fwd(2)

    @pl.when(is_inner)
    def _():
        to_across(2, 0).start()

    @pl.when(is_outer)
    def _():
        give(0, 2)

    compute_fwd(1)

    @pl.when(is_inner)
    def _():
        pass_on(1, 2)
        near(1)

    @pl.when(is_outer)
    def _():
        give(0, 0)

    compute_bwd(0)

    @pl.when(is_inner)
    def _():
        pass_on(0, 3)
        hold(0, 2)

    @pl.when(is_outer)
    def _():
        take(1, 2)
        take(0, 3)
        give(0, 1)
        take(1, 1)

    compute_fwd(3)

    @pl.when(is_inner)
    def _():
        pass_on(2, 2)
        hold(0, 3)

    @pl.when(is_outer)
    def _():
        give(0, 3)
        take(2, 2)

    compute_bwd(2)

    @pl.when(is_inner)
    def _():
        pass_on(1, 3)
        hold(0, 1)
        near(2)
        combine(0, 2)
        hold(1, 2)
        pass_on(2, 3)

    @pl.when(is_outer)
    def _():
        take(1, 3)
        give(1, 2)
        give(1, 0)
        take(2, 3)

    compute_bwd(3)

    @pl.when(is_inner)
    def _():
        combine(0, 3)
        hold(1, 0)
        hold(1, 3)
        to_peer(2).start()

    @pl.when(is_outer)
    def _():
        take(2, 1)
        give(1, 3)

    compute_bwd(1)

    @pl.when(is_inner)
    def _():
        hold(0, 0)
        combine(1, 2)
        finish(0)
        serve(0)
        hold(1, 1)
        combine(1, 3)
        serve(1)
        finish(1)

    @pl.when(is_outer)
    def _():
        finish_outer()
        give(1, 1)

    for a in range(3):
        for k in range(4):
            to_partner(a, k).wait_send()

    for m in range(2):
        for k in range(4):
            half(m, k).wait_send()

    @pl.when(is_inner)
    def _():
        for a in range(3):
            to_peer(a).wait_send()
            for k in range(2):
                to_across(a, k).wait_send()
                relay(a, k + 2).wait_send()
        for h in parts:
            to_outer(h).wait_send()
            for m in range(2):
                for k in (2, 3):
                    to_home(m, k, h).wait_send()

    @pl.when(is_outer)
    def _():
        to_near().wait_send()
        for a in range(3):
            to_raw(a).wait_send()
        for h in parts:
            to_finisher(h).wait_send()
            for m in range(2):
                for k in (1, 2, 3):
                    to_combiner(m, k, h).wait_send()

    @pl.when(has_next)
    def _():
        for h in parts:
            to_section(0, h).wait_send()
            to_section(1, h).wait_recv()

    @pl.when(has_prev)
    def _():
        for h in parts:
            to_section(0, h).wait_recv()

    @pl.when(has_prev & is_inner)
    def _():
        for h in parts:
            to_section(1, h).wait_send()
            to_outer_section(h).wait_send()


def hand_on_kernel(a_ref, b_ref, c_ref, d_ref):
    c_ref[...] = a_ref[...]
    d_ref[...] = b_ref[...]


def handed_on(a, b):
    vmem = pl.BlockSpec(memory_space=pltpu.VMEM)
    return pl.pallas_call(
        hand_on_kernel,
        out_shape=(jax.ShapeDtypeStruct(a.shape, a.dtype), jax.ShapeDtypeStruct(b.shape, b.dtype)),
        in_specs=[vmem, vmem],
        out_specs=(vmem, vmem),
    )(a, b)


def crossing_body(xf, rf, gf, xb, gb, rb, gtb, wg, wu, wd):
    _, rows, width = xf.shape
    capacity = min(rows, rows * TOPK * 3 // 4)
    hid = wg.shape[2]
    parts = width // COLS
    vmem = pl.BlockSpec(memory_space=pltpu.VMEM)
    hbm = pl.BlockSpec(memory_space=pl.ANY)
    block = (capacity, width)
    dma = pltpu.SemaphoreType.DMA
    out = jax.ShapeDtypeStruct(xf.shape, BF16)
    arrived = pl.pallas_call(
        functools.partial(crossing_kernel, capacity),
        out_shape=(out, out),
        in_specs=[vmem] * 7 + [hbm] * 3,
        out_specs=(vmem, vmem),
        scratch_shapes=[
            pltpu.VMEM((width, hid), BF16),
            pltpu.VMEM((width, hid), BF16),
            pltpu.VMEM((hid, width), BF16),
            pltpu.VMEM((8, max(rows, 128)), F32),
            pltpu.VMEM((8, max(rows, 128)), F32),
            pltpu.VMEM((3, rows, width), BF16),
            pltpu.VMEM((3, 4, 2) + block, BF16),
            pltpu.VMEM((3, 2) + block, BF16),
            pltpu.VMEM((2, 4) + block, BF16),
            pltpu.VMEM((2, 4) + block, BF16),
            pltpu.VMEM((2, 4) + block, BF16),
            pltpu.VMEM((2, 4) + block, BF16),
            pltpu.VMEM(block, BF16),
            pltpu.VMEM((2, 3) + block, BF16),
            pltpu.VMEM((2, 2) + block, BF16),
            pltpu.VMEM((2, 2) + block, BF16),
            pltpu.VMEM((2, rows, width), BF16),
            pltpu.VMEM((rows, width), BF16),
            pltpu.VMEM((2, rows, width), BF16),
            dma((3,)), dma((2,)), dma((3,)), dma((3,)), dma((3,)), dma((3, 2)), dma((3, 4)), dma((3, 2)), dma((3, 4, 2)),
            dma((2, 4)), dma((2, 4)), dma((parts,)), dma((parts,)), dma((2, 3, parts)), dma((2, 3, parts)), dma((2, 2, parts)), dma((2, 2, parts)),
            dma((2, parts)), dma((parts,)), dma((2, parts)), dma((2, parts)),
        ],
        compiler_params=pltpu.CompilerParams(
            collective_id=0, has_side_effects=True, vmem_limit_bytes=60 * 1024 * 1024
        ),
    )(xf, rf.reshape(1, rows), gf.reshape(1, rows), xb, gb, rb.reshape(1, rows), gtb.reshape(1, rows), wg, wu, wd)
    return handed_on(*arrived)


def shifted(block, axis, distance):
    devices = range(lax.axis_size(axis))
    route = [(i - distance, i) for i in devices if i - distance in devices]
    return lax.ppermute(block, axis, route)


def slot_table(routes, experts, capacity):
    flat_ids = routes.reshape(-1)
    number = jnp.arange(flat_ids.shape[0], dtype=jnp.int32)
    same = flat_ids[:, None] == flat_ids[None, :]
    before = number[None, :] < number[:, None]
    places = jnp.sum((same & before).astype(jnp.int32), axis=1)
    return (flat_ids * capacity + places).reshape(routes.shape)


def dispatch_rows(tokens, slot_ids, experts, capacity):
    numbered = jnp.arange(experts * capacity, dtype=jnp.int32)
    picker = jnp.any(slot_ids[None, :, :] == numbered[:, None, None], axis=2).astype(jnp.bfloat16)
    filled = jnp.dot(picker, tokens, preferred_element_type=jnp.float32).astype(jnp.bfloat16)
    return jnp.repeat(filled.reshape(experts, capacity, tokens.shape[1]), HSPLIT, axis=0)


def combine_rows(base, returned, slot_ids, weights, experts, capacity):
    width = base.shape[1]
    summed = jnp.sum(returned.astype(jnp.float32).reshape(experts, HSPLIT, capacity, width), axis=1)
    summed = summed.reshape(experts * capacity, width)
    numbered = jnp.arange(experts * capacity, dtype=jnp.int32)
    mixing = jnp.sum(
        weights[:, :, None] * (slot_ids[:, :, None] == numbered[None, None, :]).astype(jnp.float32),
        axis=1,
    )
    total = base.astype(jnp.float32) + jnp.dot(mixing, summed, precision=lax.Precision.HIGHEST)
    return total.astype(jnp.bfloat16)


def forward_rows(received, gate_cols, up_cols, down_rows):
    in_shape = received.shape
    row_block = received.reshape(-1, in_shape[-1])
    pre_gate = jnp.dot(row_block, gate_cols, preferred_element_type=jnp.float32)
    pre_up = jnp.dot(row_block, up_cols, preferred_element_type=jnp.float32)
    hidden = (jax.nn.silu(pre_gate) * pre_up).astype(jnp.bfloat16)
    result = jnp.dot(hidden, down_rows, preferred_element_type=jnp.float32).astype(jnp.bfloat16)
    return result.reshape(in_shape)


def backward_rows(received_x, received_g, gate_cols, up_cols, down_rows):
    in_shape = received_x.shape
    rows_x = received_x.reshape(-1, in_shape[-1])
    rows_g = received_g.reshape(-1, in_shape[-1])
    contract = (((1,), (1,)), ((), ()))
    pre_gate = jnp.dot(rows_x, gate_cols, preferred_element_type=jnp.float32)
    pre_up = jnp.dot(rows_x, up_cols, preferred_element_type=jnp.float32)
    act_grad = lax.dot_general(rows_g, down_rows, contract, preferred_element_type=jnp.float32)
    sigmoid_gate = jax.nn.sigmoid(pre_gate)
    gate_grad = (act_grad * pre_up * sigmoid_gate * (1.0 + pre_gate * (1.0 - sigmoid_gate))).astype(
        jnp.bfloat16
    )
    up_grad = (act_grad * pre_gate * sigmoid_gate).astype(jnp.bfloat16)
    back_rows = lax.dot_general(gate_grad, gate_cols, contract, preferred_element_type=jnp.float32)
    back_rows = back_rows + lax.dot_general(
        up_grad, up_cols, contract, preferred_element_type=jnp.float32
    )
    return back_rows.astype(jnp.bfloat16).reshape(in_shape)


def body(
    x_fwd,
    routes_fwd,
    gates_fwd,
    x_bwd,
    grad_bwd,
    routes_bwd,
    gates_bwd,
    gate_proj,
    up_proj,
    down_proj,
):
    tokens_a = x_fwd[0]
    tokens_b = x_bwd[0]
    grads_b = grad_bwd[0]
    gate_cols = gate_proj[0]
    up_cols = up_proj[0]
    down_rows = down_proj[0]
    experts = lax.axis_size("expert") // HSPLIT
    tok_rows = tokens_a.shape[0]
    capacity = min(tok_rows, tok_rows * TOPK * 3 // (2 * experts))
    slots_a = slot_table(routes_fwd[0], experts, capacity)
    slots_b = slot_table(routes_bwd[0], experts, capacity)
    send_a = dispatch_rows(tokens_a, slots_a, experts, capacity)
    send_x = dispatch_rows(tokens_b, slots_b, experts, capacity)
    send_g = dispatch_rows(grads_b, slots_b, experts, capacity)
    back_a = lax.all_to_all(
        forward_rows(
            lax.all_to_all(send_a, "expert", split_axis=0, concat_axis=0, tiled=True),
            gate_cols,
            up_cols,
            down_rows,
        ),
        "expert",
        split_axis=0,
        concat_axis=0,
        tiled=True,
    )
    back_b = lax.all_to_all(
        backward_rows(
            lax.all_to_all(send_x, "expert", split_axis=0, concat_axis=0, tiled=True),
            lax.all_to_all(send_g, "expert", split_axis=0, concat_axis=0, tiled=True),
            gate_cols,
            up_cols,
            down_rows,
        ),
        "expert",
        split_axis=0,
        concat_axis=0,
        tiled=True,
    )
    out_fwd = combine_rows(tokens_a, back_a, slots_a, gates_fwd[0], experts, capacity)
    out_bwd = combine_rows(grads_b, back_b, slots_b, gates_bwd[0], experts, capacity)
    fwd_next = shifted(out_fwd, "pipe", 1)
    bwd_next = shifted(out_bwd, "pipe", -1)
    return (fwd_next[None], bwd_next[None])


def solution(mesh):
    in_specs = (
        P("pipe", "expert", None),
        P("pipe", "expert", None),
        P("pipe", "expert", None),
        P("pipe", "expert", None),
        P("pipe", "expert", None),
        P("pipe", "expert", None),
        P("pipe", "expert", None),
        P("pipe", None, "expert"),
        P("pipe", None, "expert"),
        P("pipe", "expert", None),
    )
    out_specs = (P("pipe", "expert", None), P("pipe", "expert", None))
    two_experts = mesh.shape["expert"] == 2 * HSPLIT
    chosen = crossing_body if two_experts else body
    return jax.shard_map(chosen, mesh=mesh, in_specs=in_specs, out_specs=out_specs, check_vma=False)
```

```python
import functools
import jax
import jax.numpy as jnp
from jax import lax
from jax.sharding import PartitionSpec as P
from jax.experimental import pallas as pl
from jax.experimental.pallas import tpu as pltpu

HSPLIT = 4
TOPK = 1
MESH = pl.DeviceIdType.MESH
F32, BF16 = jnp.float32, jnp.bfloat16
COLS = 896


def to_column(row):
    count = row.shape[1]
    first = lax.broadcasted_iota(jnp.int32, (count, count), 0)
    second = lax.broadcasted_iota(jnp.int32, (count, count), 1)
    wide = jnp.broadcast_to(row, (count, count))
    return jnp.sum(jnp.where(first == second, wide, 0.0), axis=1, keepdims=True)


def places_rows(ids_row):
    count = ids_row.shape[1]
    first = lax.broadcasted_iota(jnp.int32, (count, count), 0)
    second = lax.broadcasted_iota(jnp.int32, (count, count), 1)
    ids = to_column(ids_row)
    same = ids == ids_row
    row = jnp.sum(jnp.where(same & (first < second), 1.0, 0.0), axis=0, keepdims=True)
    col = jnp.sum(jnp.where(same & (second < first), 1.0, 0.0), axis=1, keepdims=True)
    return ids_row, row, ids, col


def crossing_kernel(
    capacity,
    xf_ref, rf_ref, gf_ref, xb_ref, gb_ref, rb_ref, gtb_ref, wg_hbm, wu_hbm, wd_hbm,
    of_ref, ob_ref,
    wg, wu, wd, ids_out, ids_in, raw, tok, far, mine, theirs, pbuf, csum, peer_own, peer_in, comb, ret, dense, dense_in, outb,
    w_sem, ids_sem, raw_send, raw_recv, s1_sem, s2_sem, fwd_sem, relay_sem, tok_sem,
    pb_send, pb_recv, own_send, own_recv, cs_send, cs_recv, ret_send, ret_recv, de_send, de_recv, out_send, out_recv,
):
    rows_here, width = xf_ref.shape[1:]
    me = lax.axis_index("expert")
    pipe = lax.axis_index("pipe")
    n_pipe = lax.axis_size("pipe")
    z, core = lax.div(me, 2), lax.rem(me, 2)
    expert = lax.div(z, 2)
    outer = lax.rem(lax.div(z + 1, 2) + 1, 2)
    peer = me + 2 - 4 * lax.rem(z, 2)
    partner = me + 1 - 2 * core
    across = 2 * (2 - expert) + core
    is_inner, is_outer = outer == 0, outer == 1
    has_next, has_prev = pipe < n_pipe - 1, pipe > 0

    weight_copies = [
        pltpu.make_async_copy(src.at[0], dst, w_sem.at[i])
        for i, (src, dst) in enumerate(((wg_hbm, wg), (wu_hbm, wu), (wd_hbm, wd)))
    ]
    for copy in weight_copies:
        copy.start()

    barrier = pltpu.get_barrier_semaphore()
    for other in (partner, peer):
        pl.semaphore_signal(barrier, inc=1, device_id={"expert": other}, device_id_type=MESH)

    def greet(other_pipe, other):
        pl.semaphore_signal(
            barrier, inc=1, device_id={"pipe": other_pipe, "expert": other}, device_id_type=MESH
        )

    @pl.when(is_inner)
    def _():
        greet(pipe, across)

    @pl.when(has_next)
    def _():
        greet(pipe + 1, (1 - outer) * me + outer * peer)

    @pl.when(has_prev)
    def _():
        greet(pipe - 1, me)

    def remote(src, dst, send, recv, axis, index):
        return pltpu.make_async_remote_copy(
            src_ref=src, dst_ref=dst, send_sem=send, recv_sem=recv,
            device_id={axis: index}, device_id_type=MESH,
        )

    def columns(body):
        def step(i, carry):
            body(pl.ds(pl.multiple_of(i * COLS, COLS), COLS))
            return carry

        lax.fori_loop(0, width // COLS, step, 0)

    mine_id = expert.astype(F32)
    other_id = 1.0 - mine_id
    inputs = (xf_ref, xb_ref, gb_ref)

    def pickers(routes):
        ids_row, row, _, _ = places_rows(routes)
        slot = lax.broadcasted_iota(jnp.int32, (capacity, routes.shape[1]), 0).astype(F32)
        hit = slot == row
        return (
            jnp.where(hit & (ids_row == mine_id), 1.0, 0.0).astype(BF16),
            jnp.where(hit & (ids_row == other_id), 1.0, 0.0).astype(BF16),
        )

    def placers(routes):
        _, _, ids, col = places_rows(routes)
        slot = lax.broadcasted_iota(jnp.int32, (routes.shape[1], capacity), 1).astype(F32)
        hit = slot == col
        return (
            jnp.where(hit & (ids == mine_id), 1.0, 0.0).astype(BF16),
            jnp.where(hit & (ids == other_id), 1.0, 0.0).astype(BF16),
        )

    def near_ids(m):
        return ids_in[m:m + 1, :rows_here]

    def near_gates(m):
        return ids_in[m + 2:m + 3, :rows_here]

    def pick(a, k, source, picks):
        def body(at):
            block = source(at)
            tok[a, k, 0, :, at] = jnp.dot(picks[0], block, preferred_element_type=F32).astype(BF16)

            @pl.when(is_inner)
            def _():
                far[a, k, :, at] = jnp.dot(picks[1], block, preferred_element_type=F32).astype(BF16)

        columns(body)

    def dispatch(a, picks):
        pick(a, 0, lambda at: inputs[a][0, :, at], picks)

    def to_near():
        return remote(ids_out, ids_in, ids_sem.at[0], ids_sem.at[1], "expert", peer)

    def to_raw(a):
        return remote(inputs[a].at[0], raw.at[a], raw_send.at[a], raw_recv.at[a], "expert", peer)

    def to_peer(a):
        return remote(tok.at[a, 0, 0], tok.at[a, 1, 0], s1_sem.at[a], tok_sem.at[a, 1, 0], "expert", peer)

    def to_across(a, k):
        return remote(
            far.at[a, k], tok.at[a, k + 2, 0], s2_sem.at[a, k], tok_sem.at[a, k + 2, 0], "expert", across
        )

    def to_partner(a, k):
        return remote(
            tok.at[a, k, 0], tok.at[a, k, 1], fwd_sem.at[a, k], tok_sem.at[a, k, 1], "expert", partner
        )

    def relay(a, k):
        return remote(
            tok.at[a, k, 0], tok.at[a, k, 0], relay_sem.at[a, k - 2], tok_sem.at[a, k, 0], "expert", peer
        )

    def half(m, k):
        return remote(theirs.at[m, k], pbuf.at[m, k], pb_send.at[m, k], pb_recv.at[m, k], "expert", partner)

    parts = range(width // COLS)

    def part(h):
        return pl.ds(h * COLS, COLS)

    def to_combiner(m, k, h):
        return remote(
            csum.at[m, k, :, part(h)], peer_in.at[m, k - 1, :, part(h)],
            cs_send.at[m, k - 1, h], cs_recv.at[m, k - 1, h], "expert", peer,
        )

    def to_finisher(h):
        return remote(
            csum.at[1, 0, :, part(h)], peer_own.at[:, part(h)], own_send.at[h], own_recv.at[h], "expert", peer
        )

    def to_home(m, k, h):
        return remote(
            comb.at[m, k - 2, :, part(h)], ret.at[m, k - 2, :, part(h)],
            ret_send.at[m, k - 2, h], ret_recv.at[m, k - 2, h], "expert", across,
        )

    def to_outer(h):
        return remote(
            dense.at[0, :, part(h)], dense_in.at[:, part(h)], de_send.at[0, h], de_recv.at[h], "expert", peer
        )

    def to_outer_section(h):
        return pltpu.make_async_remote_copy(
            src_ref=dense.at[1, :, part(h)], dst_ref=ob_ref.at[0, :, part(h)],
            send_sem=de_send.at[1, h], recv_sem=out_recv.at[1, h],
            device_id={"pipe": pipe - 1, "expert": peer}, device_id_type=MESH,
        )

    def to_section(m, h):
        dst = of_ref if m == 0 else ob_ref
        other = pipe + 1 if m == 0 else pipe - 1
        return remote(
            outb.at[m, :, part(h)], dst.at[0, :, part(h)],
            out_send.at[m, h], out_recv.at[m, h], "pipe", other,
        )

    def near(a):
        if a == 0:
            to_near().wait_recv()
        to_raw(a).wait_recv()
        pick(a, 1, lambda at: raw[a, :, at], pickers(near_ids(min(a, 1))))
        to_across(a, 1).start()
        to_partner(a, 1).start()

    def pass_on(a, k):
        relay(a, k).wait_recv()
        relay(a, k).start()
        to_partner(a, k).start()

    def take(a, k):
        (to_peer(a) if k == 1 else relay(a, k)).wait_recv()
        to_partner(a, k).start()

    def rows_of(a, k):
        to_partner(a, k).wait_recv()
        return tok[a, k].reshape(2 * capacity, width)

    def keep(m, k, at, value):
        value = value.astype(BF16)
        mine[m, k, :, at] = value[:capacity]
        theirs[m, k, :, at] = value[capacity:]

    contract = (((1,), (1,)), ((), ()))

    def compute_fwd(k):
        rows = rows_of(0, k)
        pre_gate = jnp.dot(rows, wg[...], preferred_element_type=F32)
        pre_up = jnp.dot(rows, wu[...], preferred_element_type=F32)
        hidden = (pre_gate * jax.nn.sigmoid(pre_gate) * pre_up).astype(BF16)
        columns(lambda at: keep(0, k, at, jnp.dot(hidden, wd[:, at], preferred_element_type=F32)))
        half(0, k).start()

    def compute_bwd(k):
        rows_x, rows_g = rows_of(1, k), rows_of(2, k)
        pre_gate = jnp.dot(rows_x, wg[...], preferred_element_type=F32)
        pre_up = jnp.dot(rows_x, wu[...], preferred_element_type=F32)
        act_grad = lax.dot_general(rows_g, wd[...], contract, preferred_element_type=F32)
        sig = jax.nn.sigmoid(pre_gate)
        gate_grad = (act_grad * pre_up * sig * (1.0 + pre_gate * (1.0 - sig))).astype(BF16)
        up_grad = (act_grad * pre_gate * sig).astype(BF16)

        def body(at):
            total = lax.dot_general(gate_grad, wg[at, :], contract, preferred_element_type=F32)
            total = total + lax.dot_general(up_grad, wu[at, :], contract, preferred_element_type=F32)
            keep(1, k, at, total)

        columns(body)
        half(1, k).start()

    def chip_sum(m, k, at):
        csum[m, k, :, at] = (mine[m, k, :, at].astype(F32) + pbuf[m, k, :, at].astype(F32)).astype(BF16)

    def hold(m, k):
        half(m, k).wait_recv()
        for h in parts:
            chip_sum(m, k, part(h))

    def give(m, k):
        half(m, k).wait_recv()
        for h in parts:
            chip_sum(m, k, part(h))
            if k >= 1:
                to_combiner(m, k, h).start()
            elif m == 1:
                to_finisher(h).start()

    def combine(m, k):
        for h in parts:
            at = part(h)
            to_combiner(m, k, h).wait_recv()
            comb[m, k - 2, :, at] = (
                csum[m, k, :, at].astype(F32) + peer_in[m, k - 1, :, at].astype(F32)
            ).astype(BF16)
            to_home(m, k, h).start()

    def serve(m):
        pick_mine, pick_other = placers(near_ids(m))
        gates = to_column(near_gates(m))
        for h in parts:
            at = part(h)
            to_home(m, 3, h).wait_recv()
            total = jnp.dot(pick_mine, csum[m, 1, :, at], preferred_element_type=F32)
            total = total + jnp.dot(pick_other, ret[m, 1, :, at], preferred_element_type=F32)
            if m == 0:
                dense[m, :, at] = total.astype(BF16)
                to_outer(h).start()
            else:
                to_finisher(h).wait_recv()
                total = total + jnp.dot(pick_mine, peer_own[:, at], preferred_element_type=F32)
                dense[m, :, at] = (raw[2, :, at].astype(F32) + gates * total).astype(BF16)

                @pl.when(has_prev)
                def _():
                    to_outer_section(h).start()

    def tables(m):
        return (
            *placers((rf_ref if m == 0 else rb_ref)[...].astype(F32)),
            to_column((gf_ref if m == 0 else gtb_ref)[...]),
        )

    def close(m, h, gates, total):
        at = part(h)
        base = xf_ref if m == 0 else gb_ref
        outb[m, :, at] = (base[0, :, at].astype(F32) + gates * total).astype(BF16)

        @pl.when(has_next if m == 0 else has_prev)
        def _():
            to_section(m, h).start()

    def finish(m):
        pick_mine, pick_other, gates = tables(m)
        for h in parts:
            at = part(h)
            to_combiner(m, 1, h).wait_recv()
            to_home(m, 2, h).wait_recv()
            total = jnp.dot(pick_mine, csum[m, 0, :, at], preferred_element_type=F32)
            total = total + jnp.dot(pick_mine, peer_in[m, 0, :, at], preferred_element_type=F32)
            close(m, h, gates, total + jnp.dot(pick_other, ret[m, 0, :, at], preferred_element_type=F32))

    def finish_outer():
        pick_mine, _, gates = tables(0)
        for h in parts:
            at = part(h)
            total = jnp.dot(pick_mine, csum[0, 0, :, at], preferred_element_type=F32)
            to_outer(h).wait_recv()
            close(0, h, gates, total + dense_in[:, at].astype(F32))

    ids_out[...] = jnp.zeros_like(ids_out)
    ids_out[0:1, :rows_here] = rf_ref[...].astype(F32)
    ids_out[1:2, :rows_here] = rb_ref[...].astype(F32)
    ids_out[2:3, :rows_here] = gf_ref[...]
    ids_out[3:4, :rows_here] = gtb_ref[...]
    picks_f = pickers(rf_ref[...].astype(F32))
    picks_b = pickers(rb_ref[...].astype(F32))
    dispatch(0, picks_f)
    nexts = lax.div(n_pipe - 1 - pipe + n_pipe - 2, n_pipe - 1)
    prevs = lax.div(pipe + n_pipe - 2, n_pipe - 1)
    pl.semaphore_wait(barrier, 3 - outer + nexts + 2 * (1 - outer) * prevs)

    @pl.when(is_outer)
    def _():
        to_near().start()
        for a in range(3):
            to_raw(a).start()

    @pl.when(is_inner)
    def _():
        to_peer(0).start()
        to_across(0, 0).start()

    to_partner(0, 0).start()
    dispatch(1, picks_b)

    @pl.when(is_inner)
    def _():
        to_peer(1).start()

    to_partner(1, 0).start()
    dispatch(2, picks_b)

    to_partner(2, 0).start()

    @pl.when(pipe == 0)
    def _():
        of_ref[...] = jnp.zeros_like(of_ref)

    @pl.when(pipe == n_pipe - 1)
    def _():
        ob_ref[...] = jnp.zeros_like(ob_ref)

    for copy in weight_copies:
        copy.wait()

    @pl.when(is_inner)
    def _():
        to_across(1, 0).start()
        near(0)
        pass_on(0, 2)

    @pl.when(is_outer)
    def _():
        take(0, 2)

    compute_fwd(0)

    @pl.when(is_outer)
    def _():
        take(0, 1)

    compute_fwd(2)

    @pl.when(is_inner)
    def _():
        to_across(2, 0).start()

    @pl.when(is_outer)
    def _():
        give(0, 2)

    compute_fwd(1)

    @pl.when(is_inner)
    def _():
        pass_on(1, 2)
        near(1)

    @pl.when(is_outer)
    def _():
        give(0, 0)

    compute_bwd(0)

    @pl.when(is_inner)
    def _():
        pass_on(0, 3)
        hold(0, 2)

    @pl.when(is_outer)
    def _():
        take(1, 2)
        take(0, 3)
        give(0, 1)
        take(1, 1)

    compute_fwd(3)

    @pl.when(is_inner)
    def _():
        pass_on(2, 2)
        hold(0, 3)

    @pl.when(is_outer)
    def _():
        give(0, 3)
        take(2, 2)

    compute_bwd(2)

    @pl.when(is_inner)
    def _():
        pass_on(1, 3)
        hold(0, 1)
        near(2)
        combine(0, 2)
        hold(1, 2)
        pass_on(2, 3)

    @pl.when(is_outer)
    def _():
        take(1, 3)
        give(1, 2)
        give(1, 0)
        take(2, 3)

    compute_bwd(3)

    @pl.when(is_inner)
    def _():
        combine(0, 3)
        hold(1, 0)
        hold(1, 3)
        to_peer(2).start()

    @pl.when(is_outer)
    def _():
        take(2, 1)
        give(1, 3)

    compute_bwd(1)

    @pl.when(is_inner)
    def _():
        hold(0, 0)
        combine(1, 2)
        finish(0)
        serve(0)
        hold(1, 1)
        combine(1, 3)
        serve(1)
        finish(1)

    @pl.when(is_outer)
    def _():
        finish_outer()
        give(1, 1)

    for a in range(3):
        for k in range(4):
            to_partner(a, k).wait_send()

    for m in range(2):
        for k in range(4):
            half(m, k).wait_send()

    @pl.when(is_inner)
    def _():
        for a in range(3):
            to_peer(a).wait_send()
            for k in range(2):
                to_across(a, k).wait_send()
                relay(a, k + 2).wait_send()
        for h in parts:
            to_outer(h).wait_send()
            for m in range(2):
                for k in (2, 3):
                    to_home(m, k, h).wait_send()

    @pl.when(is_outer)
    def _():
        to_near().wait_send()
        for a in range(3):
            to_raw(a).wait_send()
        for h in parts:
            to_finisher(h).wait_send()
            for m in range(2):
                for k in (1, 2, 3):
                    to_combiner(m, k, h).wait_send()

    @pl.when(has_next)
    def _():
        for h in parts:
            to_section(0, h).wait_send()
            to_section(1, h).wait_recv()

    @pl.when(has_prev)
    def _():
        for h in parts:
            to_section(0, h).wait_recv()

    @pl.when(has_prev & is_inner)
    def _():
        for h in parts:
            to_section(1, h).wait_send()
            to_outer_section(h).wait_send()


def hand_on_kernel(a_ref, b_ref, c_ref, d_ref, sem):
    copies = [
        pltpu.make_async_copy(src, dst, sem.at[i])
        for i, (src, dst) in enumerate(((a_ref, c_ref), (b_ref, d_ref)))
    ]
    for copy in copies:
        copy.start()
    for copy in copies:
        copy.wait()


def handed_on(a, b):
    vmem = pl.BlockSpec(memory_space=pltpu.VMEM)
    hbm = pl.BlockSpec(memory_space=pl.ANY)
    return pl.pallas_call(
        hand_on_kernel,
        out_shape=(jax.ShapeDtypeStruct(a.shape, a.dtype), jax.ShapeDtypeStruct(b.shape, b.dtype)),
        in_specs=[vmem, vmem],
        out_specs=(hbm, hbm),
        scratch_shapes=[pltpu.SemaphoreType.DMA((2,))],
    )(*(pltpu.with_memory_space_constraint(x, pltpu.VMEM) for x in (a, b)))


def crossing_body(xf, rf, gf, xb, gb, rb, gtb, wg, wu, wd):
    _, rows, width = xf.shape
    capacity = min(rows, rows * TOPK * 3 // 4)
    hid = wg.shape[2]
    parts = width // COLS
    vmem = pl.BlockSpec(memory_space=pltpu.VMEM)
    hbm = pl.BlockSpec(memory_space=pl.ANY)
    block = (capacity, width)
    dma = pltpu.SemaphoreType.DMA
    out = pltpu.VMEM(xf.shape, BF16)
    arrived = pl.pallas_call(
        functools.partial(crossing_kernel, capacity),
        out_shape=(out, out),
        in_specs=[vmem] * 7 + [hbm] * 3,
        out_specs=(vmem, vmem),
        scratch_shapes=[
            pltpu.VMEM((width, hid), BF16),
            pltpu.VMEM((width, hid), BF16),
            pltpu.VMEM((hid, width), BF16),
            pltpu.VMEM((8, max(rows, 128)), F32),
            pltpu.VMEM((8, max(rows, 128)), F32),
            pltpu.VMEM((3, rows, width), BF16),
            pltpu.VMEM((3, 4, 2) + block, BF16),
            pltpu.VMEM((3, 2) + block, BF16),
            pltpu.VMEM((2, 4) + block, BF16),
            pltpu.VMEM((2, 4) + block, BF16),
            pltpu.VMEM((2, 4) + block, BF16),
            pltpu.VMEM((2, 4) + block, BF16),
            pltpu.VMEM(block, BF16),
            pltpu.VMEM((2, 3) + block, BF16),
            pltpu.VMEM((2, 2) + block, BF16),
            pltpu.VMEM((2, 2) + block, BF16),
            pltpu.VMEM((2, rows, width), BF16),
            pltpu.VMEM((rows, width), BF16),
            pltpu.VMEM((2, rows, width), BF16),
            dma((3,)), dma((2,)), dma((3,)), dma((3,)), dma((3,)), dma((3, 2)), dma((3, 4)), dma((3, 2)), dma((3, 4, 2)),
            dma((2, 4)), dma((2, 4)), dma((parts,)), dma((parts,)), dma((2, 3, parts)), dma((2, 3, parts)), dma((2, 2, parts)), dma((2, 2, parts)),
            dma((2, parts)), dma((parts,)), dma((2, parts)), dma((2, parts)),
        ],
        compiler_params=pltpu.CompilerParams(
            collective_id=0, has_side_effects=True, vmem_limit_bytes=56 * 1024 * 1024
        ),
    )(xf, rf.reshape(1, rows), gf.reshape(1, rows), xb, gb, rb.reshape(1, rows), gtb.reshape(1, rows), wg, wu, wd)
    return handed_on(*arrived)


def shifted(block, axis, distance):
    devices = range(lax.axis_size(axis))
    route = [(i - distance, i) for i in devices if i - distance in devices]
    return lax.ppermute(block, axis, route)


def slot_table(routes, experts, capacity):
    flat_ids = routes.reshape(-1)
    number = jnp.arange(flat_ids.shape[0], dtype=jnp.int32)
    same = flat_ids[:, None] == flat_ids[None, :]
    before = number[None, :] < number[:, None]
    places = jnp.sum((same & before).astype(jnp.int32), axis=1)
    return (flat_ids * capacity + places).reshape(routes.shape)


def dispatch_rows(tokens, slot_ids, experts, capacity):
    numbered = jnp.arange(experts * capacity, dtype=jnp.int32)
    picker = jnp.any(slot_ids[None, :, :] == numbered[:, None, None], axis=2).astype(jnp.bfloat16)
    filled = jnp.dot(picker, tokens, preferred_element_type=jnp.float32).astype(jnp.bfloat16)
    return jnp.repeat(filled.reshape(experts, capacity, tokens.shape[1]), HSPLIT, axis=0)


def combine_rows(base, returned, slot_ids, weights, experts, capacity):
    width = base.shape[1]
    summed = jnp.sum(returned.astype(jnp.float32).reshape(experts, HSPLIT, capacity, width), axis=1)
    summed = summed.reshape(experts * capacity, width)
    numbered = jnp.arange(experts * capacity, dtype=jnp.int32)
    mixing = jnp.sum(
        weights[:, :, None] * (slot_ids[:, :, None] == numbered[None, None, :]).astype(jnp.float32),
        axis=1,
    )
    total = base.astype(jnp.float32) + jnp.dot(mixing, summed, precision=lax.Precision.HIGHEST)
    return total.astype(jnp.bfloat16)


def forward_rows(received, gate_cols, up_cols, down_rows):
    in_shape = received.shape
    row_block = received.reshape(-1, in_shape[-1])
    pre_gate = jnp.dot(row_block, gate_cols, preferred_element_type=jnp.float32)
    pre_up = jnp.dot(row_block, up_cols, preferred_element_type=jnp.float32)
    hidden = (jax.nn.silu(pre_gate) * pre_up).astype(jnp.bfloat16)
    result = jnp.dot(hidden, down_rows, preferred_element_type=jnp.float32).astype(jnp.bfloat16)
    return result.reshape(in_shape)


def backward_rows(received_x, received_g, gate_cols, up_cols, down_rows):
    in_shape = received_x.shape
    rows_x = received_x.reshape(-1, in_shape[-1])
    rows_g = received_g.reshape(-1, in_shape[-1])
    contract = (((1,), (1,)), ((), ()))
    pre_gate = jnp.dot(rows_x, gate_cols, preferred_element_type=jnp.float32)
    pre_up = jnp.dot(rows_x, up_cols, preferred_element_type=jnp.float32)
    act_grad = lax.dot_general(rows_g, down_rows, contract, preferred_element_type=jnp.float32)
    sigmoid_gate = jax.nn.sigmoid(pre_gate)
    gate_grad = (act_grad * pre_up * sigmoid_gate * (1.0 + pre_gate * (1.0 - sigmoid_gate))).astype(
        jnp.bfloat16
    )
    up_grad = (act_grad * pre_gate * sigmoid_gate).astype(jnp.bfloat16)
    back_rows = lax.dot_general(gate_grad, gate_cols, contract, preferred_element_type=jnp.float32)
    back_rows = back_rows + lax.dot_general(
        up_grad, up_cols, contract, preferred_element_type=jnp.float32
    )
    return back_rows.astype(jnp.bfloat16).reshape(in_shape)


def body(
    x_fwd,
    routes_fwd,
    gates_fwd,
    x_bwd,
    grad_bwd,
    routes_bwd,
    gates_bwd,
    gate_proj,
    up_proj,
    down_proj,
):
    tokens_a = x_fwd[0]
    tokens_b = x_bwd[0]
    grads_b = grad_bwd[0]
    gate_cols = gate_proj[0]
    up_cols = up_proj[0]
    down_rows = down_proj[0]
    experts = lax.axis_size("expert") // HSPLIT
    tok_rows = tokens_a.shape[0]
    capacity = min(tok_rows, tok_rows * TOPK * 3 // (2 * experts))
    slots_a = slot_table(routes_fwd[0], experts, capacity)
    slots_b = slot_table(routes_bwd[0], experts, capacity)
    send_a = dispatch_rows(tokens_a, slots_a, experts, capacity)
    send_x = dispatch_rows(tokens_b, slots_b, experts, capacity)
    send_g = dispatch_rows(grads_b, slots_b, experts, capacity)
    back_a = lax.all_to_all(
        forward_rows(
            lax.all_to_all(send_a, "expert", split_axis=0, concat_axis=0, tiled=True),
            gate_cols,
            up_cols,
            down_rows,
        ),
        "expert",
        split_axis=0,
        concat_axis=0,
        tiled=True,
    )
    back_b = lax.all_to_all(
        backward_rows(
            lax.all_to_all(send_x, "expert", split_axis=0, concat_axis=0, tiled=True),
            lax.all_to_all(send_g, "expert", split_axis=0, concat_axis=0, tiled=True),
            gate_cols,
            up_cols,
            down_rows,
        ),
        "expert",
        split_axis=0,
        concat_axis=0,
        tiled=True,
    )
    out_fwd = combine_rows(tokens_a, back_a, slots_a, gates_fwd[0], experts, capacity)
    out_bwd = combine_rows(grads_b, back_b, slots_b, gates_bwd[0], experts, capacity)
    fwd_next = shifted(out_fwd, "pipe", 1)
    bwd_next = shifted(out_bwd, "pipe", -1)
    return (fwd_next[None], bwd_next[None])


def solution(mesh):
    in_specs = (
        P("pipe", "expert", None),
        P("pipe", "expert", None),
        P("pipe", "expert", None),
        P("pipe", "expert", None),
        P("pipe", "expert", None),
        P("pipe", "expert", None),
        P("pipe", "expert", None),
        P("pipe", None, "expert"),
        P("pipe", None, "expert"),
        P("pipe", "expert", None),
    )
    out_specs = (P("pipe", "expert", None), P("pipe", "expert", None))
    two_experts = mesh.shape["expert"] == 2 * HSPLIT
    chosen = crossing_body if two_experts else body
    return jax.shard_map(chosen, mesh=mesh, in_specs=in_specs, out_specs=out_specs, check_vma=False)
```

```python
import functools
import jax
import jax.numpy as jnp
from jax import lax
from jax.sharding import PartitionSpec as P
from jax.experimental import pallas as pl
from jax.experimental.pallas import tpu as pltpu

HSPLIT = 4
TOPK = 1
MESH = pl.DeviceIdType.MESH
F32, BF16 = jnp.float32, jnp.bfloat16
COLS = 896


def to_column(row):
    count = row.shape[1]
    first = lax.broadcasted_iota(jnp.int32, (count, count), 0)
    second = lax.broadcasted_iota(jnp.int32, (count, count), 1)
    wide = jnp.broadcast_to(row, (count, count))
    return jnp.sum(jnp.where(first == second, wide, 0.0), axis=1, keepdims=True)


def places_rows(ids_row):
    count = ids_row.shape[1]
    first = lax.broadcasted_iota(jnp.int32, (count, count), 0)
    second = lax.broadcasted_iota(jnp.int32, (count, count), 1)
    ids = to_column(ids_row)
    same = ids == ids_row
    row = jnp.sum(jnp.where(same & (first < second), 1.0, 0.0), axis=0, keepdims=True)
    col = jnp.sum(jnp.where(same & (second < first), 1.0, 0.0), axis=1, keepdims=True)
    return ids_row, row, ids, col


def crossing_kernel(
    capacity,
    xf_ref, rf_ref, gf_ref, xb_ref, gb_ref, rb_ref, gtb_ref, wg_hbm, wu_hbm, wd_hbm,
    of_ref, ob_ref,
    wg, wu, wd, ids_out, ids_in, raw, tok, far, mine, theirs, pbuf, csum, peer_own, peer_in, comb, ret, dense, dense_in, outb,
    w_sem, ids_sem, raw_send, raw_recv, s1_sem, s2_sem, fwd_sem, relay_sem, tok_sem,
    pb_send, pb_recv, own_send, own_recv, cs_send, cs_recv, ret_send, ret_recv, de_send, de_recv, out_send, out_recv,
):
    rows_here, width = xf_ref.shape[1:]
    me = lax.axis_index("expert")
    pipe = lax.axis_index("pipe")
    n_pipe = lax.axis_size("pipe")
    z, core = lax.div(me, 2), lax.rem(me, 2)
    expert = lax.div(z, 2)
    outer = lax.rem(lax.div(z + 1, 2) + 1, 2)
    peer = me + 2 - 4 * lax.rem(z, 2)
    partner = me + 1 - 2 * core
    across = 2 * (2 - expert) + core
    is_inner, is_outer = outer == 0, outer == 1
    has_next, has_prev = pipe < n_pipe - 1, pipe > 0

    weight_copies = [
        pltpu.make_async_copy(src.at[0], dst, w_sem.at[i])
        for i, (src, dst) in enumerate(((wg_hbm, wg), (wu_hbm, wu), (wd_hbm, wd)))
    ]
    for copy in weight_copies:
        copy.start()

    barrier = pltpu.get_barrier_semaphore()
    for other in (partner, peer):
        pl.semaphore_signal(barrier, inc=1, device_id={"expert": other}, device_id_type=MESH)

    def greet(other_pipe, other):
        pl.semaphore_signal(
            barrier, inc=1, device_id={"pipe": other_pipe, "expert": other}, device_id_type=MESH
        )

    @pl.when(is_inner)
    def _():
        greet(pipe, across)

    @pl.when(has_next)
    def _():
        greet(pipe + 1, me)

    @pl.when(has_prev)
    def _():
        greet(pipe - 1, (1 - outer) * me + outer * peer)

    def remote(src, dst, send, recv, axis, index):
        return pltpu.make_async_remote_copy(
            src_ref=src, dst_ref=dst, send_sem=send, recv_sem=recv,
            device_id={axis: index}, device_id_type=MESH,
        )

    def columns(body):
        def step(i, carry):
            body(pl.ds(pl.multiple_of(i * COLS, COLS), COLS))
            return carry

        lax.fori_loop(0, width // COLS, step, 0)

    mine_id = expert.astype(F32)
    other_id = 1.0 - mine_id
    inputs = (xf_ref, xb_ref, gb_ref)

    def pickers(routes):
        ids_row, row, _, _ = places_rows(routes)
        slot = lax.broadcasted_iota(jnp.int32, (capacity, routes.shape[1]), 0).astype(F32)
        hit = slot == row
        return (
            jnp.where(hit & (ids_row == mine_id), 1.0, 0.0).astype(BF16),
            jnp.where(hit & (ids_row == other_id), 1.0, 0.0).astype(BF16),
        )

    def placers(routes):
        _, _, ids, col = places_rows(routes)
        slot = lax.broadcasted_iota(jnp.int32, (routes.shape[1], capacity), 1).astype(F32)
        hit = slot == col
        return (
            jnp.where(hit & (ids == mine_id), 1.0, 0.0).astype(BF16),
            jnp.where(hit & (ids == other_id), 1.0, 0.0).astype(BF16),
        )

    def near_ids(m):
        return ids_in[m:m + 1, :rows_here]

    def near_gates(m):
        return ids_in[m + 2:m + 3, :rows_here]

    def pick(a, k, source, picks):
        def body(at):
            block = source(at)
            tok[a, k, 0, :, at] = jnp.dot(picks[0], block, preferred_element_type=F32).astype(BF16)

            @pl.when(is_inner)
            def _():
                far[a, k, :, at] = jnp.dot(picks[1], block, preferred_element_type=F32).astype(BF16)

        columns(body)

    def dispatch(a, picks):
        pick(a, 0, lambda at: inputs[a][0, :, at], picks)

    def to_near():
        return remote(ids_out, ids_in, ids_sem.at[0], ids_sem.at[1], "expert", peer)

    def to_raw(a):
        return remote(inputs[a].at[0], raw.at[a], raw_send.at[a], raw_recv.at[a], "expert", peer)

    def to_peer(a):
        return remote(tok.at[a, 0, 0], tok.at[a, 1, 0], s1_sem.at[a], tok_sem.at[a, 1, 0], "expert", peer)

    def to_across(a, k):
        return remote(
            far.at[a, k], tok.at[a, k + 2, 0], s2_sem.at[a, k], tok_sem.at[a, k + 2, 0], "expert", across
        )

    def to_partner(a, k):
        return remote(
            tok.at[a, k, 0], tok.at[a, k, 1], fwd_sem.at[a, k], tok_sem.at[a, k, 1], "expert", partner
        )

    def relay(a, k):
        return remote(
            tok.at[a, k, 0], tok.at[a, k, 0], relay_sem.at[a, k - 2], tok_sem.at[a, k, 0], "expert", peer
        )

    def half(m, k):
        return remote(theirs.at[m, k], pbuf.at[m, k], pb_send.at[m, k], pb_recv.at[m, k], "expert", partner)

    parts = range(width // COLS)

    def part(h):
        return pl.ds(h * COLS, COLS)

    def to_combiner(m, k, h):
        return remote(
            csum.at[m, k, :, part(h)], peer_in.at[m, k - 1, :, part(h)],
            cs_send.at[m, k - 1, h], cs_recv.at[m, k - 1, h], "expert", peer,
        )

    def to_finisher(h):
        return remote(
            csum.at[0, 0, :, part(h)], peer_own.at[:, part(h)], own_send.at[h], own_recv.at[h], "expert", peer
        )

    def to_home(m, k, h):
        return remote(
            comb.at[m, k - 2, :, part(h)], ret.at[m, k - 2, :, part(h)],
            ret_send.at[m, k - 2, h], ret_recv.at[m, k - 2, h], "expert", across,
        )

    def to_outer(h):
        return remote(
            dense.at[1, :, part(h)], dense_in.at[:, part(h)], de_send.at[1, h], de_recv.at[h], "expert", peer
        )

    def to_outer_section(h):
        return pltpu.make_async_remote_copy(
            src_ref=dense.at[0, :, part(h)], dst_ref=of_ref.at[0, :, part(h)],
            send_sem=de_send.at[0, h], recv_sem=out_recv.at[0, h],
            device_id={"pipe": pipe + 1, "expert": peer}, device_id_type=MESH,
        )

    def to_section(m, h):
        dst = of_ref if m == 0 else ob_ref
        other = pipe + 1 if m == 0 else pipe - 1
        return remote(
            outb.at[m, :, part(h)], dst.at[0, :, part(h)],
            out_send.at[m, h], out_recv.at[m, h], "pipe", other,
        )

    def near(a):
        if a == 0:
            to_near().wait_recv()
        to_raw(a).wait_recv()
        pick(a, 1, lambda at: raw[a, :, at], pickers(near_ids(min(a, 1))))
        to_across(a, 1).start()
        to_partner(a, 1).start()

    def pass_on(a, k):
        relay(a, k).wait_recv()
        relay(a, k).start()
        to_partner(a, k).start()

    def take(a, k):
        (to_peer(a) if k == 1 else relay(a, k)).wait_recv()
        to_partner(a, k).start()

    def rows_of(a, k):
        to_partner(a, k).wait_recv()
        return tok[a, k].reshape(2 * capacity, width)

    def keep(m, k, at, value):
        value = value.astype(BF16)
        mine[m, k, :, at] = value[:capacity]
        theirs[m, k, :, at] = value[capacity:]

    contract = (((1,), (1,)), ((), ()))

    def compute_fwd(k):
        rows = rows_of(0, k)
        pre_gate = jnp.dot(rows, wg[...], preferred_element_type=F32)
        pre_up = jnp.dot(rows, wu[...], preferred_element_type=F32)
        hidden = (pre_gate * jax.nn.sigmoid(pre_gate) * pre_up).astype(BF16)
        columns(lambda at: keep(0, k, at, jnp.dot(hidden, wd[:, at], preferred_element_type=F32)))
        half(0, k).start()

    def compute_bwd(k):
        rows_x, rows_g = rows_of(1, k), rows_of(2, k)
        pre_gate = jnp.dot(rows_x, wg[...], preferred_element_type=F32)
        pre_up = jnp.dot(rows_x, wu[...], preferred_element_type=F32)
        act_grad = lax.dot_general(rows_g, wd[...], contract, preferred_element_type=F32)
        sig = jax.nn.sigmoid(pre_gate)
        gate_grad = (act_grad * pre_up * sig * (1.0 + pre_gate * (1.0 - sig))).astype(BF16)
        up_grad = (act_grad * pre_gate * sig).astype(BF16)

        def body(at):
            total = lax.dot_general(gate_grad, wg[at, :], contract, preferred_element_type=F32)
            total = total + lax.dot_general(up_grad, wu[at, :], contract, preferred_element_type=F32)
            keep(1, k, at, total)

        columns(body)
        half(1, k).start()

    def chip_sum(m, k, at):
        csum[m, k, :, at] = (mine[m, k, :, at].astype(F32) + pbuf[m, k, :, at].astype(F32)).astype(BF16)

    def hold(m, k):
        half(m, k).wait_recv()
        for h in parts:
            chip_sum(m, k, part(h))

    def give(m, k):
        half(m, k).wait_recv()
        for h in parts:
            chip_sum(m, k, part(h))
            if k >= 1:
                to_combiner(m, k, h).start()
            elif m == 0:
                to_finisher(h).start()

    def combine(m, k):
        for h in parts:
            at = part(h)
            to_combiner(m, k, h).wait_recv()
            comb[m, k - 2, :, at] = (
                csum[m, k, :, at].astype(F32) + peer_in[m, k - 1, :, at].astype(F32)
            ).astype(BF16)
            to_home(m, k, h).start()

    def serve(m):
        pick_mine, pick_other = placers(near_ids(m))
        gates = to_column(near_gates(m))
        for h in parts:
            at = part(h)
            to_home(m, 3, h).wait_recv()
            total = jnp.dot(pick_mine, csum[m, 1, :, at], preferred_element_type=F32)
            total = total + jnp.dot(pick_other, ret[m, 1, :, at], preferred_element_type=F32)
            if m == 1:
                dense[m, :, at] = total.astype(BF16)
                to_outer(h).start()
            else:
                to_finisher(h).wait_recv()
                total = total + jnp.dot(pick_mine, peer_own[:, at], preferred_element_type=F32)
                dense[m, :, at] = (raw[0, :, at].astype(F32) + gates * total).astype(BF16)

                @pl.when(has_next)
                def _():
                    to_outer_section(h).start()

    def tables(m):
        return (
            *placers((rf_ref if m == 0 else rb_ref)[...].astype(F32)),
            to_column((gf_ref if m == 0 else gtb_ref)[...]),
        )

    def close(m, h, gates, total):
        at = part(h)
        base = xf_ref if m == 0 else gb_ref
        outb[m, :, at] = (base[0, :, at].astype(F32) + gates * total).astype(BF16)

        @pl.when(has_next if m == 0 else has_prev)
        def _():
            to_section(m, h).start()

    def finish(m):
        pick_mine, pick_other, gates = tables(m)
        for h in parts:
            at = part(h)
            to_combiner(m, 1, h).wait_recv()
            to_home(m, 2, h).wait_recv()
            total = jnp.dot(pick_mine, csum[m, 0, :, at], preferred_element_type=F32)
            total = total + jnp.dot(pick_mine, peer_in[m, 0, :, at], preferred_element_type=F32)
            close(m, h, gates, total + jnp.dot(pick_other, ret[m, 0, :, at], preferred_element_type=F32))

    def finish_outer():
        pick_mine, _, gates = tables(1)
        for h in parts:
            at = part(h)
            total = jnp.dot(pick_mine, csum[1, 0, :, at], preferred_element_type=F32)
            to_outer(h).wait_recv()
            close(1, h, gates, total + dense_in[:, at].astype(F32))

    ids_out[...] = jnp.zeros_like(ids_out)
    ids_out[0:1, :rows_here] = rf_ref[...].astype(F32)
    ids_out[1:2, :rows_here] = rb_ref[...].astype(F32)
    ids_out[2:3, :rows_here] = gf_ref[...]
    ids_out[3:4, :rows_here] = gtb_ref[...]
    picks_f = pickers(rf_ref[...].astype(F32))
    picks_b = pickers(rb_ref[...].astype(F32))
    dispatch(0, picks_f)
    nexts = lax.div(n_pipe - 1 - pipe + n_pipe - 2, n_pipe - 1)
    prevs = lax.div(pipe + n_pipe - 2, n_pipe - 1)
    pl.semaphore_wait(barrier, 3 - outer + prevs + 2 * (1 - outer) * nexts)

    @pl.when(is_outer)
    def _():
        to_near().start()
        for a in range(3):
            to_raw(a).start()

    @pl.when(is_inner)
    def _():
        to_peer(0).start()
        to_across(0, 0).start()

    to_partner(0, 0).start()
    dispatch(1, picks_b)

    @pl.when(is_inner)
    def _():
        to_peer(1).start()

    to_partner(1, 0).start()
    dispatch(2, picks_b)

    to_partner(2, 0).start()

    @pl.when(pipe == 0)
    def _():
        of_ref[...] = jnp.zeros_like(of_ref)

    @pl.when(pipe == n_pipe - 1)
    def _():
        ob_ref[...] = jnp.zeros_like(ob_ref)

    for copy in weight_copies:
        copy.wait()

    @pl.when(is_inner)
    def _():
        to_across(1, 0).start()

    compute_bwd(0)

    @pl.when(is_inner)
    def _():
        pass_on(0, 2)
        near(0)
        to_across(2, 0).start()

    @pl.when(is_outer)
    def _():
        take(0, 2)
        take(0, 1)

    compute_fwd(0)

    @pl.when(is_inner)
    def _():
        pass_on(1, 2)

    compute_fwd(2)
    compute_fwd(1)

    @pl.when(is_inner)
    def _():
        pass_on(0, 3)
        hold(0, 1)
        near(2)
        near(1)

    @pl.when(is_outer)
    def _():
        take(1, 1)
        give(0, 0)
        take(1, 2)
        give(0, 2)
        take(0, 3)

    compute_fwd(3)

    @pl.when(is_inner)
    def _():
        pass_on(2, 2)
        hold(1, 0)
        hold(0, 0)

    @pl.when(is_outer)
    def _():
        give(0, 3)
        take(2, 2)
        give(0, 1)
        take(2, 3)

    compute_bwd(2)

    @pl.when(is_inner)
    def _():
        hold(0, 2)
        pass_on(2, 3)
        hold(0, 3)
        hold(1, 2)
        pass_on(1, 3)
        combine(0, 3)
        combine(0, 2)
        to_peer(2).start()

    @pl.when(is_outer)
    def _():
        give(1, 2)
        take(1, 3)
        give(1, 0)

    compute_bwd(3)

    @pl.when(is_inner)
    def _():
        serve(0)
        hold(1, 3)

    @pl.when(is_outer)
    def _():
        give(1, 3)
        take(2, 1)

    compute_bwd(1)

    @pl.when(is_inner)
    def _():
        combine(1, 2)
        finish(0)
        hold(1, 1)
        combine(1, 3)
        serve(1)
        finish(1)

    @pl.when(is_outer)
    def _():
        give(1, 1)
        finish_outer()

    for a in range(3):
        for k in range(4):
            to_partner(a, k).wait_send()

    for m in range(2):
        for k in range(4):
            half(m, k).wait_send()

    @pl.when(is_inner)
    def _():
        for a in range(3):
            to_peer(a).wait_send()
            for k in range(2):
                to_across(a, k).wait_send()
                relay(a, k + 2).wait_send()
        for h in parts:
            to_outer(h).wait_send()
            for m in range(2):
                for k in (2, 3):
                    to_home(m, k, h).wait_send()

    @pl.when(is_outer)
    def _():
        to_near().wait_send()
        for a in range(3):
            to_raw(a).wait_send()
        for h in parts:
            to_finisher(h).wait_send()
            for m in range(2):
                for k in (1, 2, 3):
                    to_combiner(m, k, h).wait_send()

    @pl.when(has_next)
    def _():
        for h in parts:
            to_section(1, h).wait_recv()

    @pl.when(has_prev)
    def _():
        for h in parts:
            to_section(0, h).wait_recv()
            to_section(1, h).wait_send()

    @pl.when(has_next & is_inner)
    def _():
        for h in parts:
            to_section(0, h).wait_send()
            to_outer_section(h).wait_send()


def hand_on_kernel(a_ref, b_ref, c_ref, d_ref, sem):
    copies = [
        pltpu.make_async_copy(src, dst, sem.at[i])
        for i, (src, dst) in enumerate(((a_ref, c_ref), (b_ref, d_ref)))
    ]
    for copy in copies:
        copy.start()
    for copy in copies:
        copy.wait()


def handed_on(a, b):
    vmem = pl.BlockSpec(memory_space=pltpu.VMEM)
    hbm = pl.BlockSpec(memory_space=pl.ANY)
    return pl.pallas_call(
        hand_on_kernel,
        out_shape=(jax.ShapeDtypeStruct(a.shape, a.dtype), jax.ShapeDtypeStruct(b.shape, b.dtype)),
        in_specs=[vmem, vmem],
        out_specs=(hbm, hbm),
        scratch_shapes=[pltpu.SemaphoreType.DMA((2,))],
    )(*(pltpu.with_memory_space_constraint(x, pltpu.VMEM) for x in (a, b)))


def crossing_body(xf, rf, gf, xb, gb, rb, gtb, wg, wu, wd):
    _, rows, width = xf.shape
    capacity = min(rows, rows * TOPK * 3 // 4)
    hid = wg.shape[2]
    parts = width // COLS
    vmem = pl.BlockSpec(memory_space=pltpu.VMEM)
    hbm = pl.BlockSpec(memory_space=pl.ANY)
    block = (capacity, width)
    dma = pltpu.SemaphoreType.DMA
    out = pltpu.VMEM(xf.shape, BF16)
    arrived = pl.pallas_call(
        functools.partial(crossing_kernel, capacity),
        out_shape=(out, out),
        in_specs=[vmem] * 7 + [hbm] * 3,
        out_specs=(vmem, vmem),
        scratch_shapes=[
            pltpu.VMEM((width, hid), BF16),
            pltpu.VMEM((width, hid), BF16),
            pltpu.VMEM((hid, width), BF16),
            pltpu.VMEM((8, max(rows, 128)), F32),
            pltpu.VMEM((8, max(rows, 128)), F32),
            pltpu.VMEM((3, rows, width), BF16),
            pltpu.VMEM((3, 4, 2) + block, BF16),
            pltpu.VMEM((3, 2) + block, BF16),
            pltpu.VMEM((2, 4) + block, BF16),
            pltpu.VMEM((2, 4) + block, BF16),
            pltpu.VMEM((2, 4) + block, BF16),
            pltpu.VMEM((2, 4) + block, BF16),
            pltpu.VMEM(block, BF16),
            pltpu.VMEM((2, 3) + block, BF16),
            pltpu.VMEM((2, 2) + block, BF16),
            pltpu.VMEM((2, 2) + block, BF16),
            pltpu.VMEM((2, rows, width), BF16),
            pltpu.VMEM((rows, width), BF16),
            pltpu.VMEM((2, rows, width), BF16),
            dma((3,)), dma((2,)), dma((3,)), dma((3,)), dma((3,)), dma((3, 2)), dma((3, 4)), dma((3, 2)), dma((3, 4, 2)),
            dma((2, 4)), dma((2, 4)), dma((parts,)), dma((parts,)), dma((2, 3, parts)), dma((2, 3, parts)), dma((2, 2, parts)), dma((2, 2, parts)),
            dma((2, parts)), dma((parts,)), dma((2, parts)), dma((2, parts)),
        ],
        compiler_params=pltpu.CompilerParams(
            collective_id=0, has_side_effects=True, vmem_limit_bytes=56 * 1024 * 1024
        ),
    )(xf, rf.reshape(1, rows), gf.reshape(1, rows), xb, gb, rb.reshape(1, rows), gtb.reshape(1, rows), wg, wu, wd)
    return handed_on(*arrived)


def shifted(block, axis, distance):
    devices = range(lax.axis_size(axis))
    route = [(i - distance, i) for i in devices if i - distance in devices]
    return lax.ppermute(block, axis, route)


def slot_table(routes, experts, capacity):
    flat_ids = routes.reshape(-1)
    number = jnp.arange(flat_ids.shape[0], dtype=jnp.int32)
    same = flat_ids[:, None] == flat_ids[None, :]
    before = number[None, :] < number[:, None]
    places = jnp.sum((same & before).astype(jnp.int32), axis=1)
    return (flat_ids * capacity + places).reshape(routes.shape)


def dispatch_rows(tokens, slot_ids, experts, capacity):
    numbered = jnp.arange(experts * capacity, dtype=jnp.int32)
    picker = jnp.any(slot_ids[None, :, :] == numbered[:, None, None], axis=2).astype(jnp.bfloat16)
    filled = jnp.dot(picker, tokens, preferred_element_type=jnp.float32).astype(jnp.bfloat16)
    return jnp.repeat(filled.reshape(experts, capacity, tokens.shape[1]), HSPLIT, axis=0)


def combine_rows(base, returned, slot_ids, weights, experts, capacity):
    width = base.shape[1]
    summed = jnp.sum(returned.astype(jnp.float32).reshape(experts, HSPLIT, capacity, width), axis=1)
    summed = summed.reshape(experts * capacity, width)
    numbered = jnp.arange(experts * capacity, dtype=jnp.int32)
    mixing = jnp.sum(
        weights[:, :, None] * (slot_ids[:, :, None] == numbered[None, None, :]).astype(jnp.float32),
        axis=1,
    )
    total = base.astype(jnp.float32) + jnp.dot(mixing, summed, precision=lax.Precision.HIGHEST)
    return total.astype(jnp.bfloat16)


def forward_rows(received, gate_cols, up_cols, down_rows):
    in_shape = received.shape
    row_block = received.reshape(-1, in_shape[-1])
    pre_gate = jnp.dot(row_block, gate_cols, preferred_element_type=jnp.float32)
    pre_up = jnp.dot(row_block, up_cols, preferred_element_type=jnp.float32)
    hidden = (jax.nn.silu(pre_gate) * pre_up).astype(jnp.bfloat16)
    result = jnp.dot(hidden, down_rows, preferred_element_type=jnp.float32).astype(jnp.bfloat16)
    return result.reshape(in_shape)


def backward_rows(received_x, received_g, gate_cols, up_cols, down_rows):
    in_shape = received_x.shape
    rows_x = received_x.reshape(-1, in_shape[-1])
    rows_g = received_g.reshape(-1, in_shape[-1])
    contract = (((1,), (1,)), ((), ()))
    pre_gate = jnp.dot(rows_x, gate_cols, preferred_element_type=jnp.float32)
    pre_up = jnp.dot(rows_x, up_cols, preferred_element_type=jnp.float32)
    act_grad = lax.dot_general(rows_g, down_rows, contract, preferred_element_type=jnp.float32)
    sigmoid_gate = jax.nn.sigmoid(pre_gate)
    gate_grad = (act_grad * pre_up * sigmoid_gate * (1.0 + pre_gate * (1.0 - sigmoid_gate))).astype(
        jnp.bfloat16
    )
    up_grad = (act_grad * pre_gate * sigmoid_gate).astype(jnp.bfloat16)
    back_rows = lax.dot_general(gate_grad, gate_cols, contract, preferred_element_type=jnp.float32)
    back_rows = back_rows + lax.dot_general(
        up_grad, up_cols, contract, preferred_element_type=jnp.float32
    )
    return back_rows.astype(jnp.bfloat16).reshape(in_shape)


def body(
    x_fwd,
    routes_fwd,
    gates_fwd,
    x_bwd,
    grad_bwd,
    routes_bwd,
    gates_bwd,
    gate_proj,
    up_proj,
    down_proj,
):
    tokens_a = x_fwd[0]
    tokens_b = x_bwd[0]
    grads_b = grad_bwd[0]
    gate_cols = gate_proj[0]
    up_cols = up_proj[0]
    down_rows = down_proj[0]
    experts = lax.axis_size("expert") // HSPLIT
    tok_rows = tokens_a.shape[0]
    capacity = min(tok_rows, tok_rows * TOPK * 3 // (2 * experts))
    slots_a = slot_table(routes_fwd[0], experts, capacity)
    slots_b = slot_table(routes_bwd[0], experts, capacity)
    send_a = dispatch_rows(tokens_a, slots_a, experts, capacity)
    send_x = dispatch_rows(tokens_b, slots_b, experts, capacity)
    send_g = dispatch_rows(grads_b, slots_b, experts, capacity)
    back_a = lax.all_to_all(
        forward_rows(
            lax.all_to_all(send_a, "expert", split_axis=0, concat_axis=0, tiled=True),
            gate_cols,
            up_cols,
            down_rows,
        ),
        "expert",
        split_axis=0,
        concat_axis=0,
        tiled=True,
    )
    back_b = lax.all_to_all(
        backward_rows(
            lax.all_to_all(send_x, "expert", split_axis=0, concat_axis=0, tiled=True),
            lax.all_to_all(send_g, "expert", split_axis=0, concat_axis=0, tiled=True),
            gate_cols,
            up_cols,
            down_rows,
        ),
        "expert",
        split_axis=0,
        concat_axis=0,
        tiled=True,
    )
    out_fwd = combine_rows(tokens_a, back_a, slots_a, gates_fwd[0], experts, capacity)
    out_bwd = combine_rows(grads_b, back_b, slots_b, gates_bwd[0], experts, capacity)
    fwd_next = shifted(out_fwd, "pipe", 1)
    bwd_next = shifted(out_bwd, "pipe", -1)
    return (fwd_next[None], bwd_next[None])


def solution(mesh):
    in_specs = (
        P("pipe", "expert", None),
        P("pipe", "expert", None),
        P("pipe", "expert", None),
        P("pipe", "expert", None),
        P("pipe", "expert", None),
        P("pipe", "expert", None),
        P("pipe", "expert", None),
        P("pipe", None, "expert"),
        P("pipe", None, "expert"),
        P("pipe", "expert", None),
    )
    out_specs = (P("pipe", "expert", None), P("pipe", "expert", None))
    two_experts = mesh.shape["expert"] == 2 * HSPLIT
    chosen = crossing_body if two_experts else body
    return jax.shard_map(chosen, mesh=mesh, in_specs=in_specs, out_specs=out_specs, check_vma=False)
```

```python
import functools
import jax
import jax.numpy as jnp
from jax import lax
from jax.sharding import PartitionSpec as P
from jax.experimental import pallas as pl
from jax.experimental.pallas import tpu as pltpu

HSPLIT = 4
TOPK = 1
MESH = pl.DeviceIdType.MESH
F32, BF16 = jnp.float32, jnp.bfloat16
COLS = 896


def to_column(row):
    count = row.shape[1]
    first = lax.broadcasted_iota(jnp.int32, (count, count), 0)
    second = lax.broadcasted_iota(jnp.int32, (count, count), 1)
    wide = jnp.broadcast_to(row, (count, count))
    return jnp.sum(jnp.where(first == second, wide, 0.0), axis=1, keepdims=True)


def places_rows(ids_row):
    count = ids_row.shape[1]
    first = lax.broadcasted_iota(jnp.int32, (count, count), 0)
    second = lax.broadcasted_iota(jnp.int32, (count, count), 1)
    ids = to_column(ids_row)
    same = ids == ids_row
    row = jnp.sum(jnp.where(same & (first < second), 1.0, 0.0), axis=0, keepdims=True)
    col = jnp.sum(jnp.where(same & (second < first), 1.0, 0.0), axis=1, keepdims=True)
    return ids_row, row, ids, col


def crossing_kernel(
    capacity,
    xf_ref, rf_ref, gf_ref, xb_ref, gb_ref, rb_ref, gtb_ref, wg_hbm, wu_hbm, wd_hbm,
    of_ref, ob_ref,
    wg, wu, wd, ids_out, ids_in, raw, tok, far, mine, theirs, pbuf, csum, peer_own, peer_tail, peer_in, comb, ret, dense, dense_in, outb,
    w_sem, tail_sem, ids_sem, raw_send, raw_recv, s1_sem, s2_sem, fwd_sem, relay_sem, tok_sem,
    pb_send, pb_recv, own_send, own_recv, cs_send, cs_recv, ret_send, ret_recv, de_send, de_recv, out_send, out_recv,
):
    rows_here, width = xf_ref.shape[1:]
    me = lax.axis_index("expert")
    pipe = lax.axis_index("pipe")
    n_pipe = lax.axis_size("pipe")
    z, core = lax.div(me, 2), lax.rem(me, 2)
    expert = lax.div(z, 2)
    outer = lax.rem(lax.div(z + 1, 2) + 1, 2)
    peer = me + 2 - 4 * lax.rem(z, 2)
    partner = me + 1 - 2 * core
    across = 2 * (2 - expert) + core
    is_inner, is_outer = outer == 0, outer == 1
    has_next, has_prev = pipe < n_pipe - 1, pipe > 0

    weight_copies = [
        pltpu.make_async_copy(src.at[0], dst, w_sem.at[i])
        for i, (src, dst) in enumerate(((wg_hbm, wg), (wu_hbm, wu), (wd_hbm, wd)))
    ]
    for copy in weight_copies:
        copy.start()

    barrier = pltpu.get_barrier_semaphore()
    for other in (partner, peer):
        pl.semaphore_signal(barrier, inc=1, device_id={"expert": other}, device_id_type=MESH)

    def greet(other_pipe, other):
        pl.semaphore_signal(
            barrier, inc=1, device_id={"pipe": other_pipe, "expert": other}, device_id_type=MESH
        )

    @pl.when(is_inner)
    def _():
        greet(pipe, across)

    @pl.when(has_next)
    def _():
        greet(pipe + 1, me)

    @pl.when(has_next & is_outer)
    def _():
        greet(pipe + 1, peer)

    @pl.when(has_prev)
    def _():
        greet(pipe - 1, (1 - outer) * me + outer * peer)

    def remote(src, dst, send, recv, axis, index):
        return pltpu.make_async_remote_copy(
            src_ref=src, dst_ref=dst, send_sem=send, recv_sem=recv,
            device_id={axis: index}, device_id_type=MESH,
        )

    def columns(body):
        def step(i, carry):
            body(pl.ds(pl.multiple_of(i * COLS, COLS), COLS))
            return carry

        lax.fori_loop(0, width // COLS, step, 0)

    mine_id = expert.astype(F32)
    other_id = 1.0 - mine_id
    inputs = (xf_ref, xb_ref, gb_ref)

    def pickers(routes):
        ids_row, row, _, _ = places_rows(routes)
        slot = lax.broadcasted_iota(jnp.int32, (capacity, routes.shape[1]), 0).astype(F32)
        hit = slot == row
        return (
            jnp.where(hit & (ids_row == mine_id), 1.0, 0.0).astype(BF16),
            jnp.where(hit & (ids_row == other_id), 1.0, 0.0).astype(BF16),
        )

    def placers(routes):
        _, _, ids, col = places_rows(routes)
        slot = lax.broadcasted_iota(jnp.int32, (routes.shape[1], capacity), 1).astype(F32)
        hit = slot == col
        return (
            jnp.where(hit & (ids == mine_id), 1.0, 0.0).astype(BF16),
            jnp.where(hit & (ids == other_id), 1.0, 0.0).astype(BF16),
        )

    def near_ids(m):
        return ids_in[m:m + 1, :rows_here]

    def near_gates(m):
        return ids_in[m + 2:m + 3, :rows_here]

    def pick(a, k, source, picks):
        def body(at):
            block = source(at)
            tok[a, k, 0, :, at] = jnp.dot(picks[0], block, preferred_element_type=F32).astype(BF16)

            @pl.when(is_inner)
            def _():
                far[a, k, :, at] = jnp.dot(picks[1], block, preferred_element_type=F32).astype(BF16)

        columns(body)

    def dispatch(a, picks):
        pick(a, 0, lambda at: inputs[a][0, :, at], picks)

    def to_near():
        return remote(ids_out, ids_in, ids_sem.at[0], ids_sem.at[1], "expert", peer)

    def to_raw(a):
        return remote(inputs[a].at[0], raw.at[a], raw_send.at[a], raw_recv.at[a], "expert", peer)

    def to_peer(a):
        return remote(tok.at[a, 0, 0], tok.at[a, 1, 0], s1_sem.at[a], tok_sem.at[a, 1, 0], "expert", peer)

    def to_across(a, k):
        return remote(
            far.at[a, k], tok.at[a, k + 2, 0], s2_sem.at[a, k], tok_sem.at[a, k + 2, 0], "expert", across
        )

    def to_partner(a, k):
        return remote(
            tok.at[a, k, 0], tok.at[a, k, 1], fwd_sem.at[a, k], tok_sem.at[a, k, 1], "expert", partner
        )

    def relay(a, k):
        return remote(
            tok.at[a, k, 0], tok.at[a, k, 0], relay_sem.at[a, k - 2], tok_sem.at[a, k, 0], "expert", peer
        )

    def half(m, k):
        return remote(theirs.at[m, k], pbuf.at[m, k], pb_send.at[m, k], pb_recv.at[m, k], "expert", partner)

    parts = range(width // COLS)

    def part(h):
        return pl.ds(h * COLS, COLS)

    def to_combiner(m, k, h):
        return remote(
            csum.at[m, k, :, part(h)], peer_in.at[m, k - 1, :, part(h)],
            cs_send.at[m, k - 1, h], cs_recv.at[m, k - 1, h], "expert", peer,
        )

    def to_finisher(h):
        return remote(
            csum.at[0, 0, :, part(h)], peer_own.at[:, part(h)], own_send.at[h], own_recv.at[h], "expert", peer
        )

    def to_finisher_tail():
        return remote(
            csum.at[1, 0, :, part(parts[-1])], peer_tail, tail_sem.at[0], tail_sem.at[1], "expert", peer
        )

    def to_outer_section_tail():
        return pltpu.make_async_remote_copy(
            src_ref=dense.at[1, :, part(parts[-1])], dst_ref=ob_ref.at[0, :, part(parts[-1])],
            send_sem=de_send.at[1, parts[-1]], recv_sem=out_recv.at[1, parts[-1]],
            device_id={"pipe": pipe - 1, "expert": peer}, device_id_type=MESH,
        )

    def to_home(m, k, h):
        return remote(
            comb.at[m, k - 2, :, part(h)], ret.at[m, k - 2, :, part(h)],
            ret_send.at[m, k - 2, h], ret_recv.at[m, k - 2, h], "expert", across,
        )

    def to_outer(h):
        return remote(
            dense.at[1, :, part(h)], dense_in.at[:, part(h)], de_send.at[1, h], de_recv.at[h], "expert", peer
        )

    def to_outer_section(h):
        return pltpu.make_async_remote_copy(
            src_ref=dense.at[0, :, part(h)], dst_ref=of_ref.at[0, :, part(h)],
            send_sem=de_send.at[0, h], recv_sem=out_recv.at[0, h],
            device_id={"pipe": pipe + 1, "expert": peer}, device_id_type=MESH,
        )

    def to_section(m, h):
        dst = of_ref if m == 0 else ob_ref
        other = pipe + 1 if m == 0 else pipe - 1
        return remote(
            outb.at[m, :, part(h)], dst.at[0, :, part(h)],
            out_send.at[m, h], out_recv.at[m, h], "pipe", other,
        )

    def near(a):
        if a == 0:
            to_near().wait_recv()
        to_raw(a).wait_recv()
        pick(a, 1, lambda at: raw[a, :, at], pickers(near_ids(min(a, 1))))
        to_across(a, 1).start()
        to_partner(a, 1).start()

    def pass_on(a, k):
        relay(a, k).wait_recv()
        relay(a, k).start()
        to_partner(a, k).start()

    def take(a, k):
        (to_peer(a) if k == 1 else relay(a, k)).wait_recv()
        to_partner(a, k).start()

    def rows_of(a, k):
        to_partner(a, k).wait_recv()
        return tok[a, k].reshape(2 * capacity, width)

    def keep(m, k, at, value):
        value = value.astype(BF16)
        mine[m, k, :, at] = value[:capacity]
        theirs[m, k, :, at] = value[capacity:]

    contract = (((1,), (1,)), ((), ()))

    def compute_fwd(k):
        rows = rows_of(0, k)
        pre_gate = jnp.dot(rows, wg[...], preferred_element_type=F32)
        pre_up = jnp.dot(rows, wu[...], preferred_element_type=F32)
        hidden = (pre_gate * jax.nn.sigmoid(pre_gate) * pre_up).astype(BF16)
        columns(lambda at: keep(0, k, at, jnp.dot(hidden, wd[:, at], preferred_element_type=F32)))
        half(0, k).start()

    def compute_bwd(k):
        rows_x, rows_g = rows_of(1, k), rows_of(2, k)
        pre_gate = jnp.dot(rows_x, wg[...], preferred_element_type=F32)
        pre_up = jnp.dot(rows_x, wu[...], preferred_element_type=F32)
        act_grad = lax.dot_general(rows_g, wd[...], contract, preferred_element_type=F32)
        sig = jax.nn.sigmoid(pre_gate)
        gate_grad = (act_grad * pre_up * sig * (1.0 + pre_gate * (1.0 - sig))).astype(BF16)
        up_grad = (act_grad * pre_gate * sig).astype(BF16)

        def body(at):
            total = lax.dot_general(gate_grad, wg[at, :], contract, preferred_element_type=F32)
            total = total + lax.dot_general(up_grad, wu[at, :], contract, preferred_element_type=F32)
            keep(1, k, at, total)

        columns(body)
        half(1, k).start()

    def chip_sum(m, k, at):
        csum[m, k, :, at] = (mine[m, k, :, at].astype(F32) + pbuf[m, k, :, at].astype(F32)).astype(BF16)

    def hold(m, k):
        half(m, k).wait_recv()
        for h in parts:
            chip_sum(m, k, part(h))

    def give(m, k):
        half(m, k).wait_recv()
        for h in parts:
            chip_sum(m, k, part(h))
            if k >= 1:
                to_combiner(m, k, h).start()
            elif m == 0:
                to_finisher(h).start()
            elif h == parts[-1]:
                to_finisher_tail().start()

    def combine(m, k):
        for h in parts:
            at = part(h)
            to_combiner(m, k, h).wait_recv()
            comb[m, k - 2, :, at] = (
                csum[m, k, :, at].astype(F32) + peer_in[m, k - 1, :, at].astype(F32)
            ).astype(BF16)
            to_home(m, k, h).start()

    def serve(m):
        pick_mine, pick_other = placers(near_ids(m))
        gates = to_column(near_gates(m))
        for h in parts:
            at = part(h)
            to_home(m, 3, h).wait_recv()
            total = jnp.dot(pick_mine, csum[m, 1, :, at], preferred_element_type=F32)
            total = total + jnp.dot(pick_other, ret[m, 1, :, at], preferred_element_type=F32)
            if m == 1 and h == parts[-1]:
                to_finisher_tail().wait_recv()
                total = total + jnp.dot(pick_mine, peer_tail[...], preferred_element_type=F32)
                dense[m, :, at] = (raw[2, :, at].astype(F32) + gates * total).astype(BF16)

                @pl.when(has_prev)
                def _():
                    to_outer_section_tail().start()
            elif m == 1:
                dense[m, :, at] = total.astype(BF16)
                to_outer(h).start()
            else:
                to_finisher(h).wait_recv()
                total = total + jnp.dot(pick_mine, peer_own[:, at], preferred_element_type=F32)
                dense[m, :, at] = (raw[0, :, at].astype(F32) + gates * total).astype(BF16)

                @pl.when(has_next)
                def _():
                    to_outer_section(h).start()

    def tables(m):
        return (
            *placers((rf_ref if m == 0 else rb_ref)[...].astype(F32)),
            to_column((gf_ref if m == 0 else gtb_ref)[...]),
        )

    def close(m, h, gates, total):
        at = part(h)
        base = xf_ref if m == 0 else gb_ref
        outb[m, :, at] = (base[0, :, at].astype(F32) + gates * total).astype(BF16)

        @pl.when(has_next if m == 0 else has_prev)
        def _():
            to_section(m, h).start()

    def finish(m):
        pick_mine, pick_other, gates = tables(m)
        for h in parts:
            at = part(h)
            to_combiner(m, 1, h).wait_recv()
            to_home(m, 2, h).wait_recv()
            total = jnp.dot(pick_mine, csum[m, 0, :, at], preferred_element_type=F32)
            total = total + jnp.dot(pick_mine, peer_in[m, 0, :, at], preferred_element_type=F32)
            close(m, h, gates, total + jnp.dot(pick_other, ret[m, 0, :, at], preferred_element_type=F32))

    def finish_outer():
        pick_mine, _, gates = tables(1)
        for h in parts[:-1]:
            at = part(h)
            total = jnp.dot(pick_mine, csum[1, 0, :, at], preferred_element_type=F32)
            to_outer(h).wait_recv()
            close(1, h, gates, total + dense_in[:, at].astype(F32))

    ids_out[...] = jnp.zeros_like(ids_out)
    ids_out[0:1, :rows_here] = rf_ref[...].astype(F32)
    ids_out[1:2, :rows_here] = rb_ref[...].astype(F32)
    ids_out[2:3, :rows_here] = gf_ref[...]
    ids_out[3:4, :rows_here] = gtb_ref[...]
    picks_f = pickers(rf_ref[...].astype(F32))
    picks_b = pickers(rb_ref[...].astype(F32))
    dispatch(0, picks_f)
    nexts = lax.div(n_pipe - 1 - pipe + n_pipe - 2, n_pipe - 1)
    prevs = lax.div(pipe + n_pipe - 2, n_pipe - 1)
    pl.semaphore_wait(barrier, 3 - outer + prevs + (1 - outer) * (2 * nexts + prevs))

    @pl.when(is_outer)
    def _():
        to_near().start()
        for a in range(3):
            to_raw(a).start()

    @pl.when(is_inner)
    def _():
        to_peer(0).start()
        to_across(0, 0).start()

    to_partner(0, 0).start()
    dispatch(1, picks_b)

    @pl.when(is_inner)
    def _():
        to_peer(1).start()

    to_partner(1, 0).start()
    dispatch(2, picks_b)

    to_partner(2, 0).start()

    @pl.when(pipe == 0)
    def _():
        of_ref[...] = jnp.zeros_like(of_ref)

    @pl.when(pipe == n_pipe - 1)
    def _():
        ob_ref[...] = jnp.zeros_like(ob_ref)

    for copy in weight_copies:
        copy.wait()

    @pl.when(is_inner)
    def _():
        to_across(1, 0).start()

    compute_bwd(0)

    @pl.when(is_inner)
    def _():
        pass_on(0, 2)
        near(0)
        to_across(2, 0).start()

    @pl.when(is_outer)
    def _():
        take(0, 2)
        take(0, 1)

    compute_fwd(0)

    @pl.when(is_inner)
    def _():
        pass_on(1, 2)

    compute_fwd(2)
    compute_fwd(1)

    @pl.when(is_inner)
    def _():
        pass_on(0, 3)
        hold(0, 1)
        near(2)
        near(1)

    @pl.when(is_outer)
    def _():
        take(1, 1)
        give(0, 0)
        take(1, 2)
        give(0, 2)
        take(0, 3)

    compute_fwd(3)

    @pl.when(is_inner)
    def _():
        pass_on(2, 2)
        hold(1, 0)
        hold(0, 0)

    @pl.when(is_outer)
    def _():
        give(0, 3)
        take(2, 2)
        give(0, 1)
        take(2, 3)

    compute_bwd(2)

    @pl.when(is_inner)
    def _():
        hold(0, 2)
        pass_on(2, 3)
        hold(0, 3)
        hold(1, 2)
        pass_on(1, 3)
        combine(0, 3)
        combine(0, 2)
        to_peer(2).start()

    @pl.when(is_outer)
    def _():
        give(1, 2)
        take(1, 3)

    compute_bwd(3)

    @pl.when(is_inner)
    def _():
        serve(0)
        hold(1, 3)

    @pl.when(is_outer)
    def _():
        give(1, 3)
        give(1, 0)
        take(2, 1)

    compute_bwd(1)

    @pl.when(is_inner)
    def _():
        combine(1, 2)
        finish(0)
        hold(1, 1)
        combine(1, 3)
        serve(1)
        finish(1)

    @pl.when(is_outer)
    def _():
        give(1, 1)
        finish_outer()

    for a in range(3):
        for k in range(4):
            to_partner(a, k).wait_send()

    for m in range(2):
        for k in range(4):
            half(m, k).wait_send()

    @pl.when(is_inner)
    def _():
        for a in range(3):
            to_peer(a).wait_send()
            for k in range(2):
                to_across(a, k).wait_send()
                relay(a, k + 2).wait_send()
        for h in parts:
            if h != parts[-1]:
                to_outer(h).wait_send()
            for m in range(2):
                for k in (2, 3):
                    to_home(m, k, h).wait_send()

    @pl.when(is_outer)
    def _():
        to_near().wait_send()
        to_finisher_tail().wait_send()
        for a in range(3):
            to_raw(a).wait_send()
        for h in parts:
            to_finisher(h).wait_send()
            for m in range(2):
                for k in (1, 2, 3):
                    to_combiner(m, k, h).wait_send()

    @pl.when(has_next)
    def _():
        for h in parts:
            to_section(1, h).wait_recv()

    @pl.when(has_prev)
    def _():
        for h in parts:
            to_section(0, h).wait_recv()
            if h != parts[-1]:
                to_section(1, h).wait_send()

    @pl.when(has_prev & is_inner)
    def _():
        to_section(1, parts[-1]).wait_send()
        to_outer_section_tail().wait_send()

    @pl.when(has_next & is_inner)
    def _():
        for h in parts:
            to_section(0, h).wait_send()
            to_outer_section(h).wait_send()


def hand_on_kernel(a_ref, b_ref, c_ref, d_ref, sem):
    copies = [
        pltpu.make_async_copy(src, dst, sem.at[i])
        for i, (src, dst) in enumerate(((a_ref, c_ref), (b_ref, d_ref)))
    ]
    for copy in copies:
        copy.start()
    for copy in copies:
        copy.wait()


def handed_on(a, b):
    vmem = pl.BlockSpec(memory_space=pltpu.VMEM)
    hbm = pl.BlockSpec(memory_space=pl.ANY)
    return pl.pallas_call(
        hand_on_kernel,
        out_shape=(jax.ShapeDtypeStruct(a.shape, a.dtype), jax.ShapeDtypeStruct(b.shape, b.dtype)),
        in_specs=[vmem, vmem],
        out_specs=(hbm, hbm),
        scratch_shapes=[pltpu.SemaphoreType.DMA((2,))],
    )(*(pltpu.with_memory_space_constraint(x, pltpu.VMEM) for x in (a, b)))


def crossing_body(xf, rf, gf, xb, gb, rb, gtb, wg, wu, wd):
    _, rows, width = xf.shape
    capacity = min(rows, rows * TOPK * 3 // 4)
    hid = wg.shape[2]
    parts = width // COLS
    vmem = pl.BlockSpec(memory_space=pltpu.VMEM)
    hbm = pl.BlockSpec(memory_space=pl.ANY)
    block = (capacity, width)
    dma = pltpu.SemaphoreType.DMA
    out = pltpu.VMEM(xf.shape, BF16)
    arrived = pl.pallas_call(
        functools.partial(crossing_kernel, capacity),
        out_shape=(out, out),
        in_specs=[vmem] * 7 + [hbm] * 3,
        out_specs=(vmem, vmem),
        scratch_shapes=[
            pltpu.VMEM((width, hid), BF16),
            pltpu.VMEM((width, hid), BF16),
            pltpu.VMEM((hid, width), BF16),
            pltpu.VMEM((8, max(rows, 128)), F32),
            pltpu.VMEM((8, max(rows, 128)), F32),
            pltpu.VMEM((3, rows, width), BF16),
            pltpu.VMEM((3, 4, 2) + block, BF16),
            pltpu.VMEM((3, 2) + block, BF16),
            pltpu.VMEM((2, 4) + block, BF16),
            pltpu.VMEM((2, 4) + block, BF16),
            pltpu.VMEM((2, 4) + block, BF16),
            pltpu.VMEM((2, 4) + block, BF16),
            pltpu.VMEM(block, BF16),
            pltpu.VMEM((capacity, COLS), BF16),
            pltpu.VMEM((2, 3) + block, BF16),
            pltpu.VMEM((2, 2) + block, BF16),
            pltpu.VMEM((2, 2) + block, BF16),
            pltpu.VMEM((2, rows, width), BF16),
            pltpu.VMEM((rows, width), BF16),
            pltpu.VMEM((2, rows, width), BF16),
            dma((3,)), dma((2,)), dma((2,)), dma((3,)), dma((3,)), dma((3,)), dma((3, 2)), dma((3, 4)), dma((3, 2)), dma((3, 4, 2)),
            dma((2, 4)), dma((2, 4)), dma((parts,)), dma((parts,)), dma((2, 3, parts)), dma((2, 3, parts)), dma((2, 2, parts)), dma((2, 2, parts)),
            dma((2, parts)), dma((parts,)), dma((2, parts)), dma((2, parts)),
        ],
        compiler_params=pltpu.CompilerParams(
            collective_id=0, has_side_effects=True, vmem_limit_bytes=56 * 1024 * 1024
        ),
    )(xf, rf.reshape(1, rows), gf.reshape(1, rows), xb, gb, rb.reshape(1, rows), gtb.reshape(1, rows), wg, wu, wd)
    return handed_on(*arrived)


def shifted(block, axis, distance):
    devices = range(lax.axis_size(axis))
    route = [(i - distance, i) for i in devices if i - distance in devices]
    return lax.ppermute(block, axis, route)


def slot_table(routes, experts, capacity):
    flat_ids = routes.reshape(-1)
    number = jnp.arange(flat_ids.shape[0], dtype=jnp.int32)
    same = flat_ids[:, None] == flat_ids[None, :]
    before = number[None, :] < number[:, None]
    places = jnp.sum((same & before).astype(jnp.int32), axis=1)
    return (flat_ids * capacity + places).reshape(routes.shape)


def dispatch_rows(tokens, slot_ids, experts, capacity):
    numbered = jnp.arange(experts * capacity, dtype=jnp.int32)
    picker = jnp.any(slot_ids[None, :, :] == numbered[:, None, None], axis=2).astype(jnp.bfloat16)
    filled = jnp.dot(picker, tokens, preferred_element_type=jnp.float32).astype(jnp.bfloat16)
    return jnp.repeat(filled.reshape(experts, capacity, tokens.shape[1]), HSPLIT, axis=0)


def combine_rows(base, returned, slot_ids, weights, experts, capacity):
    width = base.shape[1]
    summed = jnp.sum(returned.astype(jnp.float32).reshape(experts, HSPLIT, capacity, width), axis=1)
    summed = summed.reshape(experts * capacity, width)
    numbered = jnp.arange(experts * capacity, dtype=jnp.int32)
    mixing = jnp.sum(
        weights[:, :, None] * (slot_ids[:, :, None] == numbered[None, None, :]).astype(jnp.float32),
        axis=1,
    )
    total = base.astype(jnp.float32) + jnp.dot(mixing, summed, precision=lax.Precision.HIGHEST)
    return total.astype(jnp.bfloat16)


def forward_rows(received, gate_cols, up_cols, down_rows):
    in_shape = received.shape
    row_block = received.reshape(-1, in_shape[-1])
    pre_gate = jnp.dot(row_block, gate_cols, preferred_element_type=jnp.float32)
    pre_up = jnp.dot(row_block, up_cols, preferred_element_type=jnp.float32)
    hidden = (jax.nn.silu(pre_gate) * pre_up).astype(jnp.bfloat16)
    result = jnp.dot(hidden, down_rows, preferred_element_type=jnp.float32).astype(jnp.bfloat16)
    return result.reshape(in_shape)


def backward_rows(received_x, received_g, gate_cols, up_cols, down_rows):
    in_shape = received_x.shape
    rows_x = received_x.reshape(-1, in_shape[-1])
    rows_g = received_g.reshape(-1, in_shape[-1])
    contract = (((1,), (1,)), ((), ()))
    pre_gate = jnp.dot(rows_x, gate_cols, preferred_element_type=jnp.float32)
    pre_up = jnp.dot(rows_x, up_cols, preferred_element_type=jnp.float32)
    act_grad = lax.dot_general(rows_g, down_rows, contract, preferred_element_type=jnp.float32)
    sigmoid_gate = jax.nn.sigmoid(pre_gate)
    gate_grad = (act_grad * pre_up * sigmoid_gate * (1.0 + pre_gate * (1.0 - sigmoid_gate))).astype(
        jnp.bfloat16
    )
    up_grad = (act_grad * pre_gate * sigmoid_gate).astype(jnp.bfloat16)
    back_rows = lax.dot_general(gate_grad, gate_cols, contract, preferred_element_type=jnp.float32)
    back_rows = back_rows + lax.dot_general(
        up_grad, up_cols, contract, preferred_element_type=jnp.float32
    )
    return back_rows.astype(jnp.bfloat16).reshape(in_shape)


def body(
    x_fwd,
    routes_fwd,
    gates_fwd,
    x_bwd,
    grad_bwd,
    routes_bwd,
    gates_bwd,
    gate_proj,
    up_proj,
    down_proj,
):
    tokens_a = x_fwd[0]
    tokens_b = x_bwd[0]
    grads_b = grad_bwd[0]
    gate_cols = gate_proj[0]
    up_cols = up_proj[0]
    down_rows = down_proj[0]
    experts = lax.axis_size("expert") // HSPLIT
    tok_rows = tokens_a.shape[0]
    capacity = min(tok_rows, tok_rows * TOPK * 3 // (2 * experts))
    slots_a = slot_table(routes_fwd[0], experts, capacity)
    slots_b = slot_table(routes_bwd[0], experts, capacity)
    send_a = dispatch_rows(tokens_a, slots_a, experts, capacity)
    send_x = dispatch_rows(tokens_b, slots_b, experts, capacity)
    send_g = dispatch_rows(grads_b, slots_b, experts, capacity)
    back_a = lax.all_to_all(
        forward_rows(
            lax.all_to_all(send_a, "expert", split_axis=0, concat_axis=0, tiled=True),
            gate_cols,
            up_cols,
            down_rows,
        ),
        "expert",
        split_axis=0,
        concat_axis=0,
        tiled=True,
    )
    back_b = lax.all_to_all(
        backward_rows(
            lax.all_to_all(send_x, "expert", split_axis=0, concat_axis=0, tiled=True),
            lax.all_to_all(send_g, "expert", split_axis=0, concat_axis=0, tiled=True),
            gate_cols,
            up_cols,
            down_rows,
        ),
        "expert",
        split_axis=0,
        concat_axis=0,
        tiled=True,
    )
    out_fwd = combine_rows(tokens_a, back_a, slots_a, gates_fwd[0], experts, capacity)
    out_bwd = combine_rows(grads_b, back_b, slots_b, gates_bwd[0], experts, capacity)
    fwd_next = shifted(out_fwd, "pipe", 1)
    bwd_next = shifted(out_bwd, "pipe", -1)
    return (fwd_next[None], bwd_next[None])


def solution(mesh):
    in_specs = (
        P("pipe", "expert", None),
        P("pipe", "expert", None),
        P("pipe", "expert", None),
        P("pipe", "expert", None),
        P("pipe", "expert", None),
        P("pipe", "expert", None),
        P("pipe", "expert", None),
        P("pipe", None, "expert"),
        P("pipe", None, "expert"),
        P("pipe", "expert", None),
    )
    out_specs = (P("pipe", "expert", None), P("pipe", "expert", None))
    two_experts = mesh.shape["expert"] == 2 * HSPLIT
    chosen = crossing_body if two_experts else body
    return jax.shard_map(chosen, mesh=mesh, in_specs=in_specs, out_specs=out_specs, check_vma=False)
```

```python
import functools
import jax
import jax.numpy as jnp
from jax import lax
from jax.sharding import PartitionSpec as P
from jax.experimental import pallas as pl
from jax.experimental.pallas import tpu as pltpu

HSPLIT = 4
TOPK = 1
MESH = pl.DeviceIdType.MESH
F32, BF16 = jnp.float32, jnp.bfloat16
COLS = 896


def to_column(row):
    count = row.shape[1]
    first = lax.broadcasted_iota(jnp.int32, (count, count), 0)
    second = lax.broadcasted_iota(jnp.int32, (count, count), 1)
    wide = jnp.broadcast_to(row, (count, count))
    return jnp.sum(jnp.where(first == second, wide, 0.0), axis=1, keepdims=True)


def places_rows(ids_row):
    count = ids_row.shape[1]
    first = lax.broadcasted_iota(jnp.int32, (count, count), 0)
    second = lax.broadcasted_iota(jnp.int32, (count, count), 1)
    ids = to_column(ids_row)
    same = ids == ids_row
    row = jnp.sum(jnp.where(same & (first < second), 1.0, 0.0), axis=0, keepdims=True)
    col = jnp.sum(jnp.where(same & (second < first), 1.0, 0.0), axis=1, keepdims=True)
    return ids_row, row, ids, col


def crossing_kernel(
    capacity,
    xf_ref, rf_ref, gf_ref, xb_ref, gb_ref, rb_ref, gtb_ref, wg_hbm, wu_hbm, wd_hbm,
    of_ref, ob_ref,
    wg, wu, wd, ids_out, ids_in, raw, tok, far, mine, theirs, pbuf, csum, peer_own, peer_tail, peer_in, comb, ret, dense, dense_in, outb,
    w_sem, tail_sem, ids_sem, raw_send, raw_recv, s1_sem, s2_sem, fwd_sem, relay_sem, tok_sem,
    pb_send, pb_recv, own_send, own_recv, cs_send, cs_recv, ret_send, ret_recv, de_send, de_recv, out_send, out_recv,
):
    rows_here, width = xf_ref.shape[1:]
    me = lax.axis_index("expert")
    pipe = lax.axis_index("pipe")
    n_pipe = lax.axis_size("pipe")
    z, core = lax.div(me, 2), lax.rem(me, 2)
    expert = lax.div(z, 2)
    outer = lax.rem(lax.div(z + 1, 2) + 1, 2)
    peer = me + 2 - 4 * lax.rem(z, 2)
    partner = me + 1 - 2 * core
    across = 2 * (2 - expert) + core
    is_inner, is_outer = outer == 0, outer == 1
    has_next, has_prev = pipe < n_pipe - 1, pipe > 0

    weight_copies = [
        pltpu.make_async_copy(src.at[0], dst, w_sem.at[i])
        for i, (src, dst) in enumerate(((wg_hbm, wg), (wu_hbm, wu), (wd_hbm, wd)))
    ]
    barrier = pltpu.get_barrier_semaphore()
    for other in (partner, peer):
        pl.semaphore_signal(barrier, inc=1, device_id={"expert": other}, device_id_type=MESH)

    def greet(other_pipe, other):
        pl.semaphore_signal(
            barrier, inc=1, device_id={"pipe": other_pipe, "expert": other}, device_id_type=MESH
        )

    @pl.when(is_inner)
    def _():
        greet(pipe, across)

    @pl.when(has_next)
    def _():
        greet(pipe + 1, me)

    @pl.when(has_next & is_outer)
    def _():
        greet(pipe + 1, peer)

    @pl.when(has_prev)
    def _():
        greet(pipe - 1, (1 - outer) * me + outer * peer)

    for copy in weight_copies:
        copy.start()

    def remote(src, dst, send, recv, axis, index):
        return pltpu.make_async_remote_copy(
            src_ref=src, dst_ref=dst, send_sem=send, recv_sem=recv,
            device_id={axis: index}, device_id_type=MESH,
        )

    def columns(body):
        def step(i, carry):
            body(pl.ds(pl.multiple_of(i * COLS, COLS), COLS))
            return carry

        lax.fori_loop(0, width // COLS, step, 0)

    mine_id = expert.astype(F32)
    other_id = 1.0 - mine_id
    inputs = (xf_ref, xb_ref, gb_ref)

    def pickers(routes):
        ids_row, row, _, _ = places_rows(routes)
        slot = lax.broadcasted_iota(jnp.int32, (capacity, routes.shape[1]), 0).astype(F32)
        hit = slot == row
        return (
            jnp.where(hit & (ids_row == mine_id), 1.0, 0.0).astype(BF16),
            jnp.where(hit & (ids_row == other_id), 1.0, 0.0).astype(BF16),
        )

    def placers(routes):
        _, _, ids, col = places_rows(routes)
        slot = lax.broadcasted_iota(jnp.int32, (routes.shape[1], capacity), 1).astype(F32)
        hit = slot == col
        return (
            jnp.where(hit & (ids == mine_id), 1.0, 0.0).astype(BF16),
            jnp.where(hit & (ids == other_id), 1.0, 0.0).astype(BF16),
        )

    def near_ids(m):
        return ids_in[m:m + 1, :rows_here]

    def near_gates(m):
        return ids_in[m + 2:m + 3, :rows_here]

    def pick(a, k, source, picks):
        def body(at):
            block = source(at)
            tok[a, k, 0, :, at] = jnp.dot(picks[0], block, preferred_element_type=F32).astype(BF16)

            @pl.when(is_inner)
            def _():
                far[a, k, :, at] = jnp.dot(picks[1], block, preferred_element_type=F32).astype(BF16)

        columns(body)

    def dispatch(a, picks):
        pick(a, 0, lambda at: inputs[a][0, :, at], picks)

    def to_near():
        return remote(ids_out, ids_in, ids_sem.at[0], ids_sem.at[1], "expert", peer)

    def to_raw(a):
        return remote(inputs[a].at[0], raw.at[a], raw_send.at[a], raw_recv.at[a], "expert", peer)

    def to_peer(a):
        return remote(tok.at[a, 0, 0], tok.at[a, 1, 0], s1_sem.at[a], tok_sem.at[a, 1, 0], "expert", peer)

    def to_across(a, k):
        return remote(
            far.at[a, k], tok.at[a, k + 2, 0], s2_sem.at[a, k], tok_sem.at[a, k + 2, 0], "expert", across
        )

    def to_partner(a, k):
        return remote(
            tok.at[a, k, 0], tok.at[a, k, 1], fwd_sem.at[a, k], tok_sem.at[a, k, 1], "expert", partner
        )

    def relay(a, k):
        return remote(
            tok.at[a, k, 0], tok.at[a, k, 0], relay_sem.at[a, k - 2], tok_sem.at[a, k, 0], "expert", peer
        )

    def half(m, k):
        return remote(theirs.at[m, k], pbuf.at[m, k], pb_send.at[m, k], pb_recv.at[m, k], "expert", partner)

    parts = range(width // COLS)

    def part(h):
        return pl.ds(h * COLS, COLS)

    def to_combiner(m, k, h):
        return remote(
            csum.at[m, k, :, part(h)], peer_in.at[m, k - 1, :, part(h)],
            cs_send.at[m, k - 1, h], cs_recv.at[m, k - 1, h], "expert", peer,
        )

    def to_finisher(h):
        return remote(
            csum.at[0, 0, :, part(h)], peer_own.at[:, part(h)], own_send.at[h], own_recv.at[h], "expert", peer
        )

    def to_finisher_tail():
        return remote(
            csum.at[1, 0, :, part(parts[-1])], peer_tail, tail_sem.at[0], tail_sem.at[1], "expert", peer
        )

    def to_outer_section_tail():
        return pltpu.make_async_remote_copy(
            src_ref=dense.at[1, :, part(parts[-1])], dst_ref=ob_ref.at[0, :, part(parts[-1])],
            send_sem=de_send.at[1, parts[-1]], recv_sem=out_recv.at[1, parts[-1]],
            device_id={"pipe": pipe - 1, "expert": peer}, device_id_type=MESH,
        )

    def to_home(m, k, h):
        return remote(
            comb.at[m, k - 2, :, part(h)], ret.at[m, k - 2, :, part(h)],
            ret_send.at[m, k - 2, h], ret_recv.at[m, k - 2, h], "expert", across,
        )

    def to_outer(h):
        return remote(
            dense.at[1, :, part(h)], dense_in.at[:, part(h)], de_send.at[1, h], de_recv.at[h], "expert", peer
        )

    def to_outer_section(h):
        return pltpu.make_async_remote_copy(
            src_ref=dense.at[0, :, part(h)], dst_ref=of_ref.at[0, :, part(h)],
            send_sem=de_send.at[0, h], recv_sem=out_recv.at[0, h],
            device_id={"pipe": pipe + 1, "expert": peer}, device_id_type=MESH,
        )

    def to_section(m, h):
        dst = of_ref if m == 0 else ob_ref
        other = pipe + 1 if m == 0 else pipe - 1
        return remote(
            outb.at[m, :, part(h)], dst.at[0, :, part(h)],
            out_send.at[m, h], out_recv.at[m, h], "pipe", other,
        )

    def near(a):
        if a == 0:
            to_near().wait_recv()
        to_raw(a).wait_recv()
        pick(a, 1, lambda at: raw[a, :, at], pickers(near_ids(min(a, 1))))
        to_across(a, 1).start()
        to_partner(a, 1).start()

    def pass_on(a, k):
        relay(a, k).wait_recv()
        relay(a, k).start()
        to_partner(a, k).start()

    def take(a, k):
        (to_peer(a) if k == 1 else relay(a, k)).wait_recv()
        to_partner(a, k).start()

    def rows_of(a, k):
        to_partner(a, k).wait_recv()
        return tok[a, k].reshape(2 * capacity, width)

    def keep(m, k, at, value):
        value = value.astype(BF16)
        mine[m, k, :, at] = value[:capacity]
        theirs[m, k, :, at] = value[capacity:]

    contract = (((1,), (1,)), ((), ()))

    def compute_fwd(k):
        rows = rows_of(0, k)
        pre_gate = jnp.dot(rows, wg[...], preferred_element_type=F32)
        pre_up = jnp.dot(rows, wu[...], preferred_element_type=F32)
        hidden = (pre_gate * jax.nn.sigmoid(pre_gate) * pre_up).astype(BF16)
        columns(lambda at: keep(0, k, at, jnp.dot(hidden, wd[:, at], preferred_element_type=F32)))
        half(0, k).start()

    def compute_bwd(k):
        rows_x, rows_g = rows_of(1, k), rows_of(2, k)
        pre_gate = jnp.dot(rows_x, wg[...], preferred_element_type=F32)
        pre_up = jnp.dot(rows_x, wu[...], preferred_element_type=F32)
        act_grad = lax.dot_general(rows_g, wd[...], contract, preferred_element_type=F32)
        sig = jax.nn.sigmoid(pre_gate)
        gate_grad = (act_grad * pre_up * sig * (1.0 + pre_gate * (1.0 - sig))).astype(BF16)
        up_grad = (act_grad * pre_gate * sig).astype(BF16)

        def body(at):
            total = lax.dot_general(gate_grad, wg[at, :], contract, preferred_element_type=F32)
            total = total + lax.dot_general(up_grad, wu[at, :], contract, preferred_element_type=F32)
            keep(1, k, at, total)

        columns(body)
        half(1, k).start()

    def chip_sum(m, k, at):
        csum[m, k, :, at] = (mine[m, k, :, at].astype(F32) + pbuf[m, k, :, at].astype(F32)).astype(BF16)

    def hold(m, k):
        half(m, k).wait_recv()
        for h in parts:
            chip_sum(m, k, part(h))

    def give(m, k):
        half(m, k).wait_recv()
        for h in parts:
            chip_sum(m, k, part(h))
            if k >= 1:
                to_combiner(m, k, h).start()
            elif m == 0:
                to_finisher(h).start()
            elif h == parts[-1]:
                to_finisher_tail().start()

    def combine(m, k):
        for h in parts:
            at = part(h)
            to_combiner(m, k, h).wait_recv()
            comb[m, k - 2, :, at] = (
                csum[m, k, :, at].astype(F32) + peer_in[m, k - 1, :, at].astype(F32)
            ).astype(BF16)
            to_home(m, k, h).start()

    def serve(m):
        pick_mine, pick_other = placers(near_ids(m))
        gates = to_column(near_gates(m))
        for h in parts:
            at = part(h)
            to_home(m, 3, h).wait_recv()
            total = jnp.dot(pick_mine, csum[m, 1, :, at], preferred_element_type=F32)
            total = total + jnp.dot(pick_other, ret[m, 1, :, at], preferred_element_type=F32)
            if m == 1 and h == parts[-1]:
                to_finisher_tail().wait_recv()
                total = total + jnp.dot(pick_mine, peer_tail[...], preferred_element_type=F32)
                dense[m, :, at] = (raw[2, :, at].astype(F32) + gates * total).astype(BF16)

                @pl.when(has_prev)
                def _():
                    to_outer_section_tail().start()
            elif m == 1:
                dense[m, :, at] = total.astype(BF16)
                to_outer(h).start()
            else:
                to_finisher(h).wait_recv()
                total = total + jnp.dot(pick_mine, peer_own[:, at], preferred_element_type=F32)
                dense[m, :, at] = (raw[0, :, at].astype(F32) + gates * total).astype(BF16)

                @pl.when(has_next)
                def _():
                    to_outer_section(h).start()

    def tables(m):
        return (
            *placers((rf_ref if m == 0 else rb_ref)[...].astype(F32)),
            to_column((gf_ref if m == 0 else gtb_ref)[...]),
        )

    def close(m, h, gates, total):
        at = part(h)
        base = xf_ref if m == 0 else gb_ref
        outb[m, :, at] = (base[0, :, at].astype(F32) + gates * total).astype(BF16)

        @pl.when(has_next if m == 0 else has_prev)
        def _():
            to_section(m, h).start()

    def finish(m):
        pick_mine, pick_other, gates = tables(m)
        for h in parts:
            at = part(h)
            to_combiner(m, 1, h).wait_recv()
            to_home(m, 2, h).wait_recv()
            total = jnp.dot(pick_mine, csum[m, 0, :, at], preferred_element_type=F32)
            total = total + jnp.dot(pick_mine, peer_in[m, 0, :, at], preferred_element_type=F32)
            close(m, h, gates, total + jnp.dot(pick_other, ret[m, 0, :, at], preferred_element_type=F32))

    def finish_outer():
        pick_mine, _, gates = tables(1)
        for h in parts[:-1]:
            at = part(h)
            total = jnp.dot(pick_mine, csum[1, 0, :, at], preferred_element_type=F32)
            to_outer(h).wait_recv()
            close(1, h, gates, total + dense_in[:, at].astype(F32))

    ids_out[...] = jnp.zeros_like(ids_out)
    ids_out[0:1, :rows_here] = rf_ref[...].astype(F32)
    ids_out[1:2, :rows_here] = rb_ref[...].astype(F32)
    ids_out[2:3, :rows_here] = gf_ref[...]
    ids_out[3:4, :rows_here] = gtb_ref[...]
    picks_f = pickers(rf_ref[...].astype(F32))
    picks_b = pickers(rb_ref[...].astype(F32))
    dispatch(0, picks_f)
    nexts = lax.div(n_pipe - 1 - pipe + n_pipe - 2, n_pipe - 1)
    prevs = lax.div(pipe + n_pipe - 2, n_pipe - 1)
    pl.semaphore_wait(barrier, 3 - outer + prevs + (1 - outer) * (2 * nexts + prevs))

    @pl.when(is_outer)
    def _():
        to_near().start()
        for a in range(3):
            to_raw(a).start()

    @pl.when(is_inner)
    def _():
        to_peer(0).start()
        to_across(0, 0).start()

    to_partner(0, 0).start()
    dispatch(1, picks_b)

    @pl.when(is_inner)
    def _():
        to_peer(1).start()

    to_partner(1, 0).start()
    dispatch(2, picks_b)

    to_partner(2, 0).start()

    @pl.when(pipe == 0)
    def _():
        of_ref[...] = jnp.zeros_like(of_ref)

    @pl.when(pipe == n_pipe - 1)
    def _():
        ob_ref[...] = jnp.zeros_like(ob_ref)

    for copy in weight_copies:
        copy.wait()

    @pl.when(is_inner)
    def _():
        to_across(1, 0).start()

    compute_bwd(0)

    @pl.when(is_inner)
    def _():
        pass_on(0, 2)
        near(0)
        to_across(2, 0).start()

    @pl.when(is_outer)
    def _():
        take(0, 2)
        take(0, 1)

    compute_fwd(0)

    @pl.when(is_inner)
    def _():
        pass_on(1, 2)

    compute_fwd(2)
    compute_fwd(1)

    @pl.when(is_inner)
    def _():
        pass_on(0, 3)
        hold(0, 1)
        near(2)
        near(1)

    @pl.when(is_outer)
    def _():
        take(1, 1)
        give(0, 0)
        take(1, 2)
        give(0, 2)
        take(0, 3)

    compute_fwd(3)

    @pl.when(is_inner)
    def _():
        pass_on(2, 2)
        hold(1, 0)
        hold(0, 0)

    @pl.when(is_outer)
    def _():
        give(0, 3)
        take(2, 2)
        give(0, 1)
        take(2, 3)

    compute_bwd(2)

    @pl.when(is_inner)
    def _():
        hold(0, 2)
        pass_on(2, 3)
        hold(0, 3)
        hold(1, 2)
        pass_on(1, 3)
        combine(0, 3)
        combine(0, 2)
        to_peer(2).start()

    @pl.when(is_outer)
    def _():
        give(1, 2)
        take(1, 3)

    compute_bwd(3)

    @pl.when(is_inner)
    def _():
        serve(0)
        hold(1, 3)

    @pl.when(is_outer)
    def _():
        give(1, 3)
        give(1, 0)
        take(2, 1)

    compute_bwd(1)

    @pl.when(is_inner)
    def _():
        combine(1, 2)
        finish(0)
        hold(1, 1)
        combine(1, 3)
        serve(1)
        finish(1)

    @pl.when(is_outer)
    def _():
        give(1, 1)
        finish_outer()

    for a in range(3):
        for k in range(4):
            to_partner(a, k).wait_send()

    for m in range(2):
        for k in range(4):
            half(m, k).wait_send()

    @pl.when(is_inner)
    def _():
        for a in range(3):
            to_peer(a).wait_send()
            for k in range(2):
                to_across(a, k).wait_send()
                relay(a, k + 2).wait_send()
        for h in parts:
            if h != parts[-1]:
                to_outer(h).wait_send()
            for m in range(2):
                for k in (2, 3):
                    to_home(m, k, h).wait_send()

    @pl.when(is_outer)
    def _():
        to_near().wait_send()
        to_finisher_tail().wait_send()
        for a in range(3):
            to_raw(a).wait_send()
        for h in parts:
            to_finisher(h).wait_send()
            for m in range(2):
                for k in (1, 2, 3):
                    to_combiner(m, k, h).wait_send()

    @pl.when(has_next)
    def _():
        for h in parts:
            to_section(1, h).wait_recv()

    @pl.when(has_prev)
    def _():
        for h in parts:
            to_section(0, h).wait_recv()
            if h != parts[-1]:
                to_section(1, h).wait_send()

    @pl.when(has_prev & is_inner)
    def _():
        to_section(1, parts[-1]).wait_send()
        to_outer_section_tail().wait_send()

    @pl.when(has_next & is_inner)
    def _():
        for h in parts:
            to_section(0, h).wait_send()
            to_outer_section(h).wait_send()


def hand_on_kernel(a_ref, b_ref, c_ref, d_ref, sem):
    copies = [
        pltpu.make_async_copy(src, dst, sem.at[i])
        for i, (src, dst) in enumerate(((a_ref, c_ref), (b_ref, d_ref)))
    ]
    for copy in copies:
        copy.start()
    for copy in copies:
        copy.wait()


def handed_on(a, b):
    vmem = pl.BlockSpec(memory_space=pltpu.VMEM)
    hbm = pl.BlockSpec(memory_space=pl.ANY)
    return pl.pallas_call(
        hand_on_kernel,
        out_shape=(jax.ShapeDtypeStruct(a.shape, a.dtype), jax.ShapeDtypeStruct(b.shape, b.dtype)),
        in_specs=[vmem, vmem],
        out_specs=(hbm, hbm),
        scratch_shapes=[pltpu.SemaphoreType.DMA((2,))],
    )(*(pltpu.with_memory_space_constraint(x, pltpu.VMEM) for x in (a, b)))


def crossing_body(xf, rf, gf, xb, gb, rb, gtb, wg, wu, wd):
    _, rows, width = xf.shape
    capacity = min(rows, rows * TOPK * 3 // 4)
    hid = wg.shape[2]
    parts = width // COLS
    vmem = pl.BlockSpec(memory_space=pltpu.VMEM)
    hbm = pl.BlockSpec(memory_space=pl.ANY)
    block = (capacity, width)
    dma = pltpu.SemaphoreType.DMA
    out = pltpu.VMEM(xf.shape, BF16)
    arrived = pl.pallas_call(
        functools.partial(crossing_kernel, capacity),
        out_shape=(out, out),
        in_specs=[vmem] * 7 + [hbm] * 3,
        out_specs=(vmem, vmem),
        scratch_shapes=[
            pltpu.VMEM((width, hid), BF16),
            pltpu.VMEM((width, hid), BF16),
            pltpu.VMEM((hid, width), BF16),
            pltpu.VMEM((8, max(rows, 128)), F32),
            pltpu.VMEM((8, max(rows, 128)), F32),
            pltpu.VMEM((3, rows, width), BF16),
            pltpu.VMEM((3, 4, 2) + block, BF16),
            pltpu.VMEM((3, 2) + block, BF16),
            pltpu.VMEM((2, 4) + block, BF16),
            pltpu.VMEM((2, 4) + block, BF16),
            pltpu.VMEM((2, 4) + block, BF16),
            pltpu.VMEM((2, 4) + block, BF16),
            pltpu.VMEM(block, BF16),
            pltpu.VMEM((capacity, COLS), BF16),
            pltpu.VMEM((2, 3) + block, BF16),
            pltpu.VMEM((2, 2) + block, BF16),
            pltpu.VMEM((2, 2) + block, BF16),
            pltpu.VMEM((2, rows, width), BF16),
            pltpu.VMEM((rows, width), BF16),
            pltpu.VMEM((2, rows, width), BF16),
            dma((3,)), dma((2,)), dma((2,)), dma((3,)), dma((3,)), dma((3,)), dma((3, 2)), dma((3, 4)), dma((3, 2)), dma((3, 4, 2)),
            dma((2, 4)), dma((2, 4)), dma((parts,)), dma((parts,)), dma((2, 3, parts)), dma((2, 3, parts)), dma((2, 2, parts)), dma((2, 2, parts)),
            dma((2, parts)), dma((parts,)), dma((2, parts)), dma((2, parts)),
        ],
        compiler_params=pltpu.CompilerParams(
            collective_id=0, has_side_effects=True, vmem_limit_bytes=56 * 1024 * 1024
        ),
    )(xf, rf.reshape(1, rows), gf.reshape(1, rows), xb, gb, rb.reshape(1, rows), gtb.reshape(1, rows), wg, wu, wd)
    return handed_on(*arrived)


def shifted(block, axis, distance):
    devices = range(lax.axis_size(axis))
    route = [(i - distance, i) for i in devices if i - distance in devices]
    return lax.ppermute(block, axis, route)


def slot_table(routes, experts, capacity):
    flat_ids = routes.reshape(-1)
    number = jnp.arange(flat_ids.shape[0], dtype=jnp.int32)
    same = flat_ids[:, None] == flat_ids[None, :]
    before = number[None, :] < number[:, None]
    places = jnp.sum((same & before).astype(jnp.int32), axis=1)
    return (flat_ids * capacity + places).reshape(routes.shape)


def dispatch_rows(tokens, slot_ids, experts, capacity):
    numbered = jnp.arange(experts * capacity, dtype=jnp.int32)
    picker = jnp.any(slot_ids[None, :, :] == numbered[:, None, None], axis=2).astype(jnp.bfloat16)
    filled = jnp.dot(picker, tokens, preferred_element_type=jnp.float32).astype(jnp.bfloat16)
    return jnp.repeat(filled.reshape(experts, capacity, tokens.shape[1]), HSPLIT, axis=0)


def combine_rows(base, returned, slot_ids, weights, experts, capacity):
    width = base.shape[1]
    summed = jnp.sum(returned.astype(jnp.float32).reshape(experts, HSPLIT, capacity, width), axis=1)
    summed = summed.reshape(experts * capacity, width)
    numbered = jnp.arange(experts * capacity, dtype=jnp.int32)
    mixing = jnp.sum(
        weights[:, :, None] * (slot_ids[:, :, None] == numbered[None, None, :]).astype(jnp.float32),
        axis=1,
    )
    total = base.astype(jnp.float32) + jnp.dot(mixing, summed, precision=lax.Precision.HIGHEST)
    return total.astype(jnp.bfloat16)


def forward_rows(received, gate_cols, up_cols, down_rows):
    in_shape = received.shape
    row_block = received.reshape(-1, in_shape[-1])
    pre_gate = jnp.dot(row_block, gate_cols, preferred_element_type=jnp.float32)
    pre_up = jnp.dot(row_block, up_cols, preferred_element_type=jnp.float32)
    hidden = (jax.nn.silu(pre_gate) * pre_up).astype(jnp.bfloat16)
    result = jnp.dot(hidden, down_rows, preferred_element_type=jnp.float32).astype(jnp.bfloat16)
    return result.reshape(in_shape)


def backward_rows(received_x, received_g, gate_cols, up_cols, down_rows):
    in_shape = received_x.shape
    rows_x = received_x.reshape(-1, in_shape[-1])
    rows_g = received_g.reshape(-1, in_shape[-1])
    contract = (((1,), (1,)), ((), ()))
    pre_gate = jnp.dot(rows_x, gate_cols, preferred_element_type=jnp.float32)
    pre_up = jnp.dot(rows_x, up_cols, preferred_element_type=jnp.float32)
    act_grad = lax.dot_general(rows_g, down_rows, contract, preferred_element_type=jnp.float32)
    sigmoid_gate = jax.nn.sigmoid(pre_gate)
    gate_grad = (act_grad * pre_up * sigmoid_gate * (1.0 + pre_gate * (1.0 - sigmoid_gate))).astype(
        jnp.bfloat16
    )
    up_grad = (act_grad * pre_gate * sigmoid_gate).astype(jnp.bfloat16)
    back_rows = lax.dot_general(gate_grad, gate_cols, contract, preferred_element_type=jnp.float32)
    back_rows = back_rows + lax.dot_general(
        up_grad, up_cols, contract, preferred_element_type=jnp.float32
    )
    return back_rows.astype(jnp.bfloat16).reshape(in_shape)


def body(
    x_fwd,
    routes_fwd,
    gates_fwd,
    x_bwd,
    grad_bwd,
    routes_bwd,
    gates_bwd,
    gate_proj,
    up_proj,
    down_proj,
):
    tokens_a = x_fwd[0]
    tokens_b = x_bwd[0]
    grads_b = grad_bwd[0]
    gate_cols = gate_proj[0]
    up_cols = up_proj[0]
    down_rows = down_proj[0]
    experts = lax.axis_size("expert") // HSPLIT
    tok_rows = tokens_a.shape[0]
    capacity = min(tok_rows, tok_rows * TOPK * 3 // (2 * experts))
    slots_a = slot_table(routes_fwd[0], experts, capacity)
    slots_b = slot_table(routes_bwd[0], experts, capacity)
    send_a = dispatch_rows(tokens_a, slots_a, experts, capacity)
    send_x = dispatch_rows(tokens_b, slots_b, experts, capacity)
    send_g = dispatch_rows(grads_b, slots_b, experts, capacity)
    back_a = lax.all_to_all(
        forward_rows(
            lax.all_to_all(send_a, "expert", split_axis=0, concat_axis=0, tiled=True),
            gate_cols,
            up_cols,
            down_rows,
        ),
        "expert",
        split_axis=0,
        concat_axis=0,
        tiled=True,
    )
    back_b = lax.all_to_all(
        backward_rows(
            lax.all_to_all(send_x, "expert", split_axis=0, concat_axis=0, tiled=True),
            lax.all_to_all(send_g, "expert", split_axis=0, concat_axis=0, tiled=True),
            gate_cols,
            up_cols,
            down_rows,
        ),
        "expert",
        split_axis=0,
        concat_axis=0,
        tiled=True,
    )
    out_fwd = combine_rows(tokens_a, back_a, slots_a, gates_fwd[0], experts, capacity)
    out_bwd = combine_rows(grads_b, back_b, slots_b, gates_bwd[0], experts, capacity)
    fwd_next = shifted(out_fwd, "pipe", 1)
    bwd_next = shifted(out_bwd, "pipe", -1)
    return (fwd_next[None], bwd_next[None])


def solution(mesh):
    in_specs = (
        P("pipe", "expert", None),
        P("pipe", "expert", None),
        P("pipe", "expert", None),
        P("pipe", "expert", None),
        P("pipe", "expert", None),
        P("pipe", "expert", None),
        P("pipe", "expert", None),
        P("pipe", None, "expert"),
        P("pipe", None, "expert"),
        P("pipe", "expert", None),
    )
    out_specs = (P("pipe", "expert", None), P("pipe", "expert", None))
    two_experts = mesh.shape["expert"] == 2 * HSPLIT
    chosen = crossing_body if two_experts else body
    return jax.shard_map(chosen, mesh=mesh, in_specs=in_specs, out_specs=out_specs, check_vma=False)
```
